128 devices in a mesh: pipe: 2 (over x_lo), ctx: 16 (over x_hi, z, core), tp: 4 (over y).
Axes of the slice: x: 4 (x_hi: 2, x_lo: 2; x = x_hi * 2 + x_lo), y: 4, z: 4, core: 2. Of those that a mesh axis runs over, the one named last changes fastest.
Arguments:
- value_input: bfloat16 [2, 2048, 16384], P('pipe', 'ctx', 'tp'), may hold values from -6 to 6
- state_input: bfloat16 [2, 2048, 4096], P('pipe', 'ctx', 'tp'), may hold values from -6 to 6
- step_raw: bfloat16 [2, 2048, 256], P('pipe', 'ctx', 'tp'), may hold values from -4 to 11
- upstream: bfloat16 [2, 2048, 16384], P('pipe', 'ctx', 'tp'), may hold values from -6 to 6
- step_bias: float32 [256], P('tp'), may hold values from -6.9 to -2.3
- decay_log: float32 [256], P('tp'), may hold values from 0 to 2.77
- skip_gain: float32 [256], P('tp'), may hold values from 0.5 to 2
- value_kernel: float32 [4, 16384], P(None, 'tp'), may hold values from -0.5 to 0.5
- value_offset: float32 [16384], P('tp'), may hold values from -0.5 to 0.5
- state_kernel: float32 [4, 4096], P(None, 'tp'), may hold values from -0.5 to 0.5
- state_offset: float32 [4096], P('tp'), may hold values from -0.5 to 0.5
Outputs:
- value_grad: bfloat16 [2, 2048, 16384], P('pipe', 'ctx', 'tp')
- state_grad: bfloat16 [2, 2048, 4096], P('pipe', 'ctx', 'tp')
- step_grad: bfloat16 [2, 2048, 256], P('pipe', 'ctx', 'tp')
The draws below stay inside these ranges and needn't reach their ends.
All inputs are finite; a program needn't handle non-finite values.
Results may differ from the reference program's by a relative error of at most 0.011.
Values may be sent and summed in bfloat16 or wider, within the bound.
No kernel may reach another device: no remote copies, remote signals or barrier semaphores. Data moves between devices by JAX's collectives and lax.ppermute only.
A program may use at most 128 MiB of HBM per device.

```python
import jax
import jax.numpy as jnp
from jax import lax

HEAD_DIM = 64
STATE = 256
CONV = 4
STRETCH = 128
TOK_DEV = 128
BATCH_COUNT = 2
SEQUENCE_LENGTH = 2048
HEADS = 256
GROUPS = 8
WIDTH_X = 16384
WIDTH_BC = 4096


def draw_step_raw(key, part):
    jitter_random_key, offset_random_key, spike_random_key = jax.random.split(key, 3)
    jitter_values = jnp.clip(0.6 * jax.random.normal(jitter_random_key, (BATCH_COUNT, SEQUENCE_LENGTH, HEADS), jnp.float32), -3.0, 3.0)
    shifts = jax.random.uniform(offset_random_key, (BATCH_COUNT, SEQUENCE_LENGTH // TOK_DEV, HEADS), jnp.float32, -0.7, 0.7)
    displaced_values = jnp.repeat(shifts, TOK_DEV, axis=1)
    chosen_positions = jax.random.randint(spike_random_key, (BATCH_COUNT, 1, 6), 0, SEQUENCE_LENGTH)
    target_positions = jnp.arange(SEQUENCE_LENGTH, dtype=jnp.int32)[None, :, None]
    spike_values = jnp.any(target_positions == chosen_positions, axis=2, keepdims=True).astype(jnp.float32)
    return (jitter_values + displaced_values + 7.0 * spike_values).astype(jnp.bfloat16)


def shard_levels(key, shape, pieces, smallest, largest):
    factor_of = 1.0
    for axis_at, shards_of in pieces:
        steps = jax.random.uniform(jax.random.fold_in(jax.random.fold_in(key, 6), axis_at), (shards_of,), jnp.float32, smallest / len(pieces), largest / len(pieces))
        factor_of = factor_of * jnp.repeat(jnp.exp(steps), shape[axis_at] // shards_of).reshape((-1,) + (1,) * (len(shape) - 1 - axis_at))
    return factor_of


def gaussian(key, extent, deviation, limit, pieces=(), kind=jnp.bfloat16):
    level = shard_levels(key, extent, pieces, -0.22, 0.18) if pieces else 1.0
    result = jax.random.normal(key, extent, jnp.float32) * deviation * level
    return jnp.minimum(jnp.maximum(result, -limit), limit).astype(kind)


def setup_inputs(seed: int = 0) -> dict:
    splits = jax.random.split(jax.random.key(seed), 12)
    return {
        "value_input": gaussian(splits[0], (BATCH_COUNT, SEQUENCE_LENGTH, WIDTH_X), 1.0, 6.0, ((0, 2), (1, 16), (2, 4))),
        "state_input": gaussian(splits[1], (BATCH_COUNT, SEQUENCE_LENGTH, WIDTH_BC), 1.0, 6.0, ((0, 2), (1, 16), (2, 4))),
        "step_raw": draw_step_raw(jax.random.fold_in(splits[11], 71), 0),
        "upstream": gaussian(splits[3], (BATCH_COUNT, SEQUENCE_LENGTH, WIDTH_X), 1.0, 6.0, ((0, 2), (1, 16), (2, 4))),
        "step_bias": jnp.clip(-6.9 + 4.6000001430511475 * jax.random.uniform(splits[4], (HEADS,), jnp.float32) ** shard_levels(splits[4], (HEADS,), ((0, 4),), -0.2, 0.2), -6.9, -2.3),
        "decay_log": jnp.clip(2.77 * jax.random.uniform(splits[5], (HEADS,), jnp.float32) ** shard_levels(splits[5], (HEADS,), ((0, 4),), -0.2, 0.2), 0.0, 2.77),
        "skip_gain": jnp.clip(0.5 + 1.5 * jax.random.uniform(splits[6], (HEADS,), jnp.float32) ** shard_levels(splits[6], (HEADS,), ((0, 4),), -0.2, 0.2), 0.5, 2.0),
        "value_kernel": jnp.clip(jax.random.uniform(splits[7], (CONV, WIDTH_X), jnp.float32, -0.5, 0.5) * shard_levels(splits[7], (CONV, WIDTH_X), ((1, 4),), -0.4, 0.0), -0.5, 0.5),
        "value_offset": jnp.clip(jax.random.uniform(splits[8], (WIDTH_X,), jnp.float32, -0.5, 0.5) * shard_levels(splits[8], (WIDTH_X,), ((0, 4),), -0.4, 0.0), -0.5, 0.5),
        "state_kernel": jnp.clip(jax.random.uniform(splits[9], (CONV, WIDTH_BC), jnp.float32, -0.5, 0.5) * shard_levels(splits[9], (CONV, WIDTH_BC), ((1, 4),), -0.4, 0.0), -0.5, 0.5),
        "state_offset": jnp.clip(jax.random.uniform(splits[10], (WIDTH_BC,), jnp.float32, -0.5, 0.5) * shard_levels(splits[10], (WIDTH_BC,), ((0, 4),), -0.4, 0.0), -0.5, 0.5),
    }


precise = lax.Precision.HIGHEST

def causal_conv(values, weight, offset):
    length = values.shape[0]
    padded = jnp.pad(values, ((CONV - 1, 0), (0, 0)))
    summed = jnp.zeros_like(values) + offset[None, :]
    for tap_index in range(CONV):
        summed = summed + weight[tap_index][None, :] * padded[tap_index:tap_index + length]
    return summed

def conv_back(gradient, weight):
    length = gradient.shape[0]
    padded = jnp.pad(gradient, ((0, CONV - 1), (0, 0)))
    summed = jnp.zeros_like(gradient)
    for tap_index in range(CONV):
        shift_by = CONV - 1 - tap_index
        summed = summed + weight[tap_index][None, :] * padded[shift_by:shift_by + length]
    return summed

def silu_slope(before):
    sigmoid_part = jax.nn.sigmoid(before)
    return sigmoid_part * (1.0 + before * (1.0 - sigmoid_part))

def ssd_core(inputs, deltas, write_rows, read_rows, decay_rate, skip_weight):
    nheads, length, channels = inputs.shape
    blocks = length // STRETCH
    rate_block = (deltas * decay_rate[:, None]).reshape(nheads, blocks, STRETCH)
    within = jnp.cumsum(rate_block, axis=2)
    scaled = (inputs * deltas[:, :, None]).reshape(nheads, blocks, STRETCH, channels)
    write_block = write_rows.reshape(blocks, STRETCH, -1)
    read_block = read_rows.reshape(blocks, STRETCH, -1)
    scores = jnp.einsum('kqn,ksn->kqs', read_block, write_block, precision=precise)
    target_positions = jnp.arange(STRETCH)
    causal = target_positions[:, None] >= target_positions[None, :]
    decays = jnp.exp(jnp.where(causal[None, None], within[:, :, :, None] - within[:, :, None, :], -jnp.inf))
    inner_out = jnp.einsum('hkqs,hksp->hkqp', decays * scores[None], scaled, precision=precise)
    totals = within[:, :, -1]
    tail_decay = jnp.exp(totals[:, :, None] - within)
    states = jnp.einsum('ksn,hksp->hknp', write_block, tail_decay[:, :, :, None] * scaled, precision=precise)
    block_ends = jnp.cumsum(totals, axis=1)
    starts = block_ends - totals
    block_order = jnp.arange(blocks)
    earlier = block_order[:, None] > block_order[None, :]
    crossing = jnp.exp(jnp.where(earlier[None], starts[:, :, None] - block_ends[:, None, :], -jnp.inf))
    carried = jnp.einsum('hkj,hjnp->hknp', crossing, states, precision=precise)
    outer_out = jnp.einsum('kqn,hknp->hkqp', read_block, carried, precision=precise) * jnp.exp(within)[:, :, :, None]
    return (inner_out + outer_out).reshape(nheads, length, channels) + skip_weight[:, None, None] * inputs

def ssd_grads(inputs, deltas, write_rows, read_rows, decay_rate, skip_weight, gradient):

    def forward(values, steps_in, write_part, read_part):
        return ssd_core(values, steps_in, write_part, read_part, decay_rate, skip_weight)
    outputs, pullback = jax.vjp(forward, inputs, deltas, write_rows, read_rows)
    return pullback(gradient)

def reference(value_input, state_input, step_raw, upstream, step_bias, decay_log, skip_gain, value_kernel, value_offset, state_kernel, state_offset):
    per_group = HEADS // GROUPS
    head_span = per_group * HEAD_DIM
    decay_rates = -jnp.exp(decay_log)
    value_list = []
    state_list = []
    step_list = []
    for micro_index in range(BATCH_COUNT):
        arriving = upstream[BATCH_COUNT - 1 - micro_index].astype(jnp.float32)
        value_pre = causal_conv(value_input[micro_index].astype(jnp.float32), value_kernel, value_offset)
        value_post = jax.nn.silu(value_pre).astype(jnp.bfloat16)
        state_pre = causal_conv(state_input[micro_index].astype(jnp.float32), state_kernel, state_offset)
        state_post = jax.nn.silu(state_pre).astype(jnp.bfloat16)
        step_pre = step_raw[micro_index].astype(jnp.float32) + step_bias[None, :]
        deltas = jax.nn.softplus(step_pre)

        def one_group(group_index):
            column_start = group_index * head_span
            values = lax.dynamic_slice_in_dim(value_post, column_start, head_span, 1).astype(jnp.float32)
            values = values.reshape(SEQUENCE_LENGTH, per_group, HEAD_DIM).transpose(1, 0, 2)
            gradient = lax.dynamic_slice_in_dim(arriving, column_start, head_span, 1)
            gradient = gradient.reshape(SEQUENCE_LENGTH, per_group, HEAD_DIM).transpose(1, 0, 2)
            group_deltas = lax.dynamic_slice_in_dim(deltas, group_index * per_group, per_group, 1).T
            group_state = lax.dynamic_slice_in_dim(state_post, group_index * 2 * STATE, 2 * STATE, 1).astype(jnp.float32)
            group_rates = lax.dynamic_slice_in_dim(decay_rates, group_index * per_group, per_group, 0)
            group_skip = lax.dynamic_slice_in_dim(skip_gain, group_index * per_group, per_group, 0)
            grad_values, grad_deltas, grad_write, grad_read = ssd_grads(values, group_deltas, group_state[:, :STATE], group_state[:, STATE:], group_rates, group_skip, gradient)
            return (grad_values.transpose(1, 0, 2).reshape(SEQUENCE_LENGTH, head_span), grad_deltas.T, jnp.concatenate([grad_write, grad_read], axis=1))
        value_parts, delta_parts, state_parts = lax.map(one_group, jnp.arange(GROUPS, dtype=jnp.int32))
        d_value_post = jnp.moveaxis(value_parts, 0, 1).reshape(SEQUENCE_LENGTH, WIDTH_X)
        d_delta = jnp.moveaxis(delta_parts, 0, 1).reshape(SEQUENCE_LENGTH, HEADS)
        d_state_post = jnp.moveaxis(state_parts, 0, 1).reshape(SEQUENCE_LENGTH, WIDTH_BC)
        value_list.append(conv_back(d_value_post * silu_slope(value_pre), value_kernel).astype(jnp.bfloat16))
        state_list.append(conv_back(d_state_post * silu_slope(state_pre), state_kernel).astype(jnp.bfloat16))
        step_list.append((d_delta * jax.nn.sigmoid(step_pre)).astype(jnp.bfloat16))
    return (jnp.stack(value_list), jnp.stack(state_list), jnp.stack(step_list))
```

```python
import functools

import jax
import jax.numpy as jnp
from jax import lax
from jax.experimental import pallas as pl
from jax.experimental.pallas import tpu as pltpu
from jax.sharding import PartitionSpec as P

HEAD_DIM = 64
STATE = 256
CONV = 4
CORES = 2
RING = 4
HALVES = 2
f32 = jnp.float32
bf16 = jnp.bfloat16
HIGH = lax.Precision.HIGHEST

TOK = 128
ROWS = TOK * CORES
HEADS = 32
WIDE = HEADS * HEAD_DIM
PART = WIDE // RING
TAIL = 16


def nn(a, b, precision=None):
    return lax.dot_general(
        a, b, (((1,), (0,)), ((), ())), precision=precision, preferred_element_type=f32
    )


def nt(a, b):
    return lax.dot_general(a, b, (((1,), (1,)), ((), ())), preferred_element_type=f32)


def iota(shape, axis):
    return lax.broadcasted_iota(jnp.int32, shape, axis)


def split3(x):
    high = x.astype(bf16).astype(f32)
    rest = x - high
    mid = rest.astype(bf16).astype(f32)
    low = rest - mid
    part = iota(x.shape, 1) // HEADS
    picked = jnp.where(part == 0, high, jnp.where(part == 1, mid, jnp.where(part == 2, low, 0.0)))
    return picked.astype(bf16)


def spread(width, start=0):
    rows = iota((128, width), 0) % HEADS
    cols = (iota((128, width), 1) + start) // HEAD_DIM
    return jnp.where(rows == cols, 1.0, 0.0).astype(bf16)


def head_sum(x, ones):
    high = x.astype(bf16)
    low = (x - high.astype(f32)).astype(bf16)
    return nt(high, ones) + nt(low, ones)


def softplus(x):
    u = jnp.exp(-jnp.abs(x))
    small = u * (1.0 - u * (0.5 - u * (1.0 / 3.0 - u * 0.25)))
    return jnp.maximum(x, 0.0) + jnp.where(u < 0.01, small, jnp.log(1.0 + u))


def sigmoid(x):
    return 1.0 / (1.0 + jnp.exp(-x))


def first_kernel(
    ids, v_own, v_in, s_own, s_in, r_own, r_in, halo_a, halo_b, bias, rate_log,
    v_tap, v_off, s_tap, s_off,
    m0, m1, m2, m3, x_out, xs_out, sx_out, bc_out, sbc_out, delta_out, within_out, sig_out,
    buf, sbuf, raw, wide,
):
    core, ring = ids[0], ids[1]
    mine = pl.multiple_of(core * TOK, TOK)
    other = pl.multiple_of((1 - core) * TOK, TOK)
    raw[pl.ds(mine, TOK), :] = r_own[...].astype(f32)
    raw[pl.ds(other, TOK), :] = r_in[...].astype(f32)
    pre = raw[...] + bias[...]
    delta = softplus(pre)
    rate = -jnp.exp(rate_log[...])
    lower = jnp.where(iota((ROWS, ROWS), 0) >= iota((ROWS, ROWS), 1), 1.0, 0.0).astype(f32)
    within = nn(lower, delta * rate, HIGH)
    delta_out[...] = delta
    within_out[...] = within
    sig_out[...] = sigmoid(pre)
    total = within[ROWS - 1 : ROWS, :]
    scale = split3(delta * jnp.exp(total - within))
    wide[...] = nn(scale, spread(WIDE))

    buf[pl.ds(pl.multiple_of(8 + mine, 8), TOK), :] = v_own[...].astype(f32)
    buf[pl.ds(pl.multiple_of(8 + other, 8), TOK), :] = v_in[...].astype(f32)
    sbuf[pl.ds(pl.multiple_of(8 + mine, 8), TOK), :] = s_own[...].astype(f32)
    sbuf[pl.ds(pl.multiple_of(8 + other, 8), TOK), :] = s_in[...].astype(f32)
    halo = halo_a[...].astype(f32) + halo_b[...].astype(f32)
    buf[0:8, :] = halo[8:16, :WIDE]
    sbuf[0:8, :] = halo[8:16, WIDE:]

    def conv(source, tap, off, cols):
        acc = off[:, cols] + tap[0:1, cols] * source[5 : 5 + ROWS, cols]
        for j in range(1, CONV):
            acc = acc + tap[j : j + 1, cols] * source[5 + j : 5 + j + ROWS, cols]
        sig = sigmoid(acc)
        return acc * sig, sig * (1.0 + acc * (1.0 - sig))

    def state_block(b, carry):
        cols = pl.ds(pl.multiple_of(b * 128, 128), 128)
        post, slope = conv(sbuf, s_tap, s_off, cols)
        bc_out[:, cols] = post.astype(bf16)
        sbc_out[:, cols] = slope.astype(bf16)
        return carry

    lax.fori_loop(0, 4, state_block, 0)

    def value_block(b, carry):
        cols = pl.ds(pl.multiple_of(b * 128, 128), 128)
        post, slope = conv(buf, v_tap, v_off, cols)
        post = post.astype(bf16)
        x_out[:, cols] = post
        sx_out[:, cols] = slope.astype(bf16)
        xs_out[:, cols] = (post.astype(f32) * wide[:, cols]).astype(bf16)
        return carry

    lax.fori_loop(0, 16, value_block, 0)

    write_t = bc_out[:, :STATE].astype(f32).T.astype(bf16)
    total_parts = split3(jnp.broadcast_to(total, (8, 128)))
    for slot, out in enumerate((m0, m1, m2, m3)):
        start = pl.multiple_of(((ring + slot) % RING) * PART, PART)
        out[0:STATE, :] = nn(write_t, xs_out[:, pl.ds(start, PART)]).astype(bf16)
        full = nn(total_parts, spread(PART, start))[0:1, :]
        high = full.astype(bf16).astype(f32)
        mid = (full - high).astype(bf16).astype(f32)
        low = full - high - mid
        row = iota((TAIL, PART), 0)
        out[STATE : STATE + TAIL, :] = jnp.where(
            row == 0, high, jnp.where(row == 1, mid, jnp.where(row == 2, low, 0.0))
        ).astype(bf16)


def ring_totals(parts):
    out = []
    for part in parts:
        rows = part[STATE : STATE + TAIL, :].astype(f32)
        out.append(rows[0:1] + rows[1:2] + rows[2:3])
    return out


def between(totals, places, low, high):
    out = jnp.zeros_like(totals[0])
    for total, place in zip(totals, places):
        inside = jnp.logical_and(place > low, place < high)
        out = out + total * jnp.where(inside, 1.0, 0.0)
    return out


def edge_kernel(back, ids, m0, m1, m2, m3, d0, d1, d2, d3, out):
    ring = ids[1]
    places = [(ring + RING - s) % RING for s in range(RING)]
    totals = ring_totals((m0, m1, m2, m3))
    acc = jnp.zeros((STATE, PART), f32)
    for src, place in zip((d0, d1, d2, d3), places):
        if back:
            weight = jnp.exp(between(totals, places, -1, place))
        else:
            weight = jnp.exp(between(totals, places, place, RING))
        acc = acc + weight * src[0:STATE, :].astype(f32)
    out[...] = acc.astype(bf16)


def scan_kernel(back, ids, m0, m1, m2, m3, d0, d1, d2, d3, edge, o0, o1, o2, o3):
    ring = ids[1]
    places = [(ring + RING - s) % RING for s in range(RING)]
    totals = ring_totals((m0, m1, m2, m3))
    for out, here in zip((o0, o1, o2, o3), places):
        if back:
            weight = jnp.exp(between(totals, places, here, RING))
        else:
            weight = jnp.exp(between(totals, places, -1, here))
        acc = weight * edge[...].astype(f32)
        for src, place in zip((d0, d1, d2, d3), places):
            if back:
                gap = between(totals, places, here, place)
                live = place > here
            else:
                gap = between(totals, places, place, here)
                live = place < here
            weight = jnp.exp(gap) * jnp.where(live, 1.0, 0.0)
            acc = acc + weight * src[0:STATE, :].astype(f32)
        out[...] = acc.astype(bf16)


def second_kernel(ids, g_own, g_in, bc, within, d0, d1, d2, d3, dy_out, dye_out, wide):
    core, ring = ids[0], ids[1]
    mine = pl.multiple_of(core * TOK, TOK)
    other = pl.multiple_of((1 - core) * TOK, TOK)
    dy_out[pl.ds(mine, TOK), :] = g_own[...]
    dy_out[pl.ds(other, TOK), :] = g_in[...]
    wide[...] = nn(split3(jnp.exp(within[...])), spread(WIDE))
    read_t = bc[:, STATE:].astype(f32).T.astype(bf16)

    def block(b, carry):
        cols = pl.ds(pl.multiple_of(b * 128, 128), 128)
        dye_out[:, cols] = (dy_out[:, cols].astype(f32) * wide[:, cols]).astype(bf16)
        return carry

    lax.fori_loop(0, 16, block, 0)
    for slot, out in enumerate((d0, d1, d2, d3)):
        start = pl.multiple_of(((ring + slot) % RING) * PART, PART)
        out[...] = nn(read_t, dye_out[:, pl.ds(start, PART)]).astype(bf16)


def inner_kernel(
    x, dy, bc, delta, within, u_out, dbc_out, diff_out, wide, within_t, row_sum, bcs, dbcs
):
    half = ROWS // 2
    wide[...] = nn(split3(delta[...]), spread(WIDE))
    within_t[...] = within[...].T
    write, read = bc[:, :STATE], bc[:, STATE:]
    bcs[...] = nt(write, read)
    dbcs[...] = jnp.zeros_like(dbcs)
    diff_out[...] = jnp.zeros_like(diff_out)
    keep = iota((half, half), 1) >= iota((half, half), 0)
    lanes = iota((ROWS, 128), 1)
    first = lanes < HEAD_DIM

    def pair(b, carry):
        cols = pl.ds(pl.multiple_of(b * 128, 128), 128)
        xd = (x[:, cols].astype(f32) * wide[:, cols]).astype(bf16)
        grad = dy[:, cols]
        zero = jnp.zeros_like(grad)
        top = jnp.zeros((half, 128), f32)
        bot = jnp.zeros((half, 128), f32)
        col_total = jnp.zeros((ROWS, 128), f32)
        for e in range(2):
            h = 2 * b + e
            g = jnp.where(first, grad, zero) if e == 0 else jnp.where(first, zero, grad)
            wq = within_t[pl.ds(h, 1), :]
            ws = jnp.sum(jnp.where(lanes == h, within[...], 0.0), axis=1, keepdims=True)
            diff00 = jnp.where(keep, wq[:, :half] - ws[:half], -jnp.inf)
            diff01 = wq[:, half:] - ws[:half]
            diff11 = jnp.where(keep, wq[:, half:] - ws[half:], -jnp.inf)
            dm0 = nt(xd[:half], g)
            dm11 = nt(xd[half:], g[half:])
            sums = []
            rows0 = jnp.zeros((1, half), f32)
            rows1 = jnp.zeros((1, half), f32)
            products = []
            for dif, dm, r, c in (
                (diff00, dm0[:, :half], 0, 0),
                (diff01, dm0[:, half:], 0, 1),
                (diff11, dm11, 1, 1),
            ):
                rs, cs = pl.ds(r * half, half), pl.ds(c * half, half)
                decay = jnp.exp(dif)
                m = decay * bcs[rs, cs]
                p = dm * m
                dbcs[rs, cs] = dbcs[rs, cs] + dm * decay
                total = jnp.sum(p, axis=0, keepdims=True)
                if c == 0:
                    rows0 = rows0 + total
                else:
                    rows1 = rows1 + total
                sums.append(jnp.sum(p, axis=1, keepdims=True))
                products.append(m.astype(bf16))
            row_sum[pl.ds(h, 1), :] = jnp.concatenate([rows0, rows1], axis=1)
            top = top + nn(products[0], g[:half]) + nn(products[1], g[half:])
            bot = bot + nn(products[2], g[half:])
            col = jnp.concatenate([sums[0] + sums[1], sums[2]], axis=0)
            col_total = col_total + jnp.where(lanes % HEADS == h, col, 0.0)
        u_out[:half, cols] = top
        u_out[half:, cols] = bot
        diff_out[...] = diff_out[...] - col_total
        return carry

    for t in range(1, 4):
        row_sum[t * HEADS : (t + 1) * HEADS, :] = jnp.zeros((HEADS, ROWS), f32)
    lax.fori_loop(0, 16, pair, 0)
    for t in range(1, 4):
        row_sum[t * HEADS : (t + 1) * HEADS, :] = row_sum[0:HEADS, :]
    diff_out[...] = diff_out[...] + row_sum[...].T
    grad = dbcs[...]
    dbc_out[:, :STATE] = nn(grad.astype(bf16), read)
    dbc_out[:, STATE:] = nn(grad.T.astype(bf16), write)


def carry_kernel(ids, c0, c1, c2, c3, bc, dye, dbc, outer_out, dread_out, carried_out):
    ring = ids[1]
    for slot, src in enumerate((c0, c1, c2, c3)):
        start = pl.multiple_of(((ring + slot) % RING) * PART, PART)
        carried_out[:, pl.ds(start, PART)] = src[...]
    read = bc[:, STATE:]
    dread_out[...] = dbc[:, STATE:] + nt(dye[...], carried_out[...])
    outer = jnp.zeros((ROWS, 128), f32)
    for b in range(4):
        cols = slice(b * PART, (b + 1) * PART)
        part = nn(read, carried_out[:, cols]) * dye[:, cols].astype(f32)
        outer = outer + head_sum(part, spread(PART, b * PART))
    outer_out[...] = outer


def last_kernel(
    ids, g0, g1, g2, g3, carried, bc, x, xs, dy, u_in, sx, sbc, delta, within, sig, diff, outer,
    dread, dbc, rate_log, skip, v_tap, s_tap,
    vg_own, vg_out, sg_own, sg_out, st_own, st_out, head_out,
    gbuf, ebuf, sbuf, dbuf, back, sback,
):
    core, ring = ids[0], ids[1]
    mine = pl.multiple_of(core * TOK, TOK)
    other = pl.multiple_of((1 - core) * TOK, TOK)
    for slot, src in enumerate((g0, g1, g2, g3)):
        start = pl.multiple_of(((ring + slot) % RING) * PART, PART)
        gbuf[:, pl.ds(start, PART)] = src[...]
    write = bc[:, :STATE]
    w = within[...]
    dlt = delta[...]
    total = w[ROWS - 1 : ROWS, :]
    tail_parts = split3(jnp.exp(total - w))
    delta_parts = split3(dlt)
    rsum = jnp.zeros((ROWS, 128), f32)
    vsum = jnp.zeros((ROWS, 128), f32)
    tsum = jnp.zeros((8, 128), f32)
    ebuf[ROWS : ROWS + 8, :] = jnp.zeros((8, WIDE), f32)
    sbuf[ROWS : ROWS + 8, :] = jnp.zeros((8, 2 * STATE), f32)
    for b in range(4):
        cols = slice(b * PART, (b + 1) * PART)
        ones = spread(PART, b * PART)
        grad = gbuf[:, cols]
        through = nn(write, grad)
        rsum = rsum + head_sum(xs[:, cols].astype(f32) * through, ones)
        u = u_in[:, cols] + nn(tail_parts, ones) * through
        vsum = vsum + head_sum(x[:, cols].astype(f32) * u, ones)
        dx = nn(delta_parts, ones) * u + skip[:, cols] * dy[:, cols].astype(f32)
        ebuf[0:ROWS, cols] = dx * sx[:, cols].astype(f32)
        both = jnp.sum(
            grad.astype(f32) * carried[:, cols].astype(f32), axis=0, keepdims=True
        )
        tsum = tsum + head_sum(jnp.broadcast_to(both, (8, PART)), ones)
    dtotal = tsum[0:1, :] * jnp.exp(total)
    ra, rb = iota((ROWS, ROWS), 0), iota((ROWS, ROWS), 1)
    later = jnp.where(rb >= ra, 1.0, 0.0).astype(f32)
    earlier = jnp.where(rb < ra, 1.0, 0.0).astype(f32)
    da = nn(later, diff[...] + outer[...], HIGH) + nn(earlier, rsum, HIGH) + dtotal
    dbuf[...] = ((vsum - jnp.exp(rate_log[...]) * da) * sig[...])
    st_own[...] = dbuf[pl.ds(mine, TOK), :].astype(bf16)
    st_out[...] = dbuf[pl.ds(other, TOK), :].astype(bf16)

    dwrite = dbc[:, :STATE] + nt(xs[...], gbuf[...])
    sbuf[0:ROWS, :STATE] = dwrite * sbc[:, :STATE].astype(f32)
    sbuf[0:ROWS, STATE:] = dread[...] * sbc[:, STATE:].astype(f32)
    head_out[:, :WIDE] = ebuf[0:8, :]
    head_out[:, WIDE:] = sbuf[0:8, :]

    def conv(source, tap, cols):
        acc = tap[CONV - 1 : CONV, cols] * source[0:ROWS, cols]
        for shift in range(1, CONV):
            j = CONV - 1 - shift
            acc = acc + tap[j : j + 1, cols] * source[shift : shift + ROWS, cols]
        return acc

    def value_block(b, carry):
        cols = pl.ds(pl.multiple_of(b * 128, 128), 128)
        back[:, cols] = conv(ebuf, v_tap, cols).astype(bf16)
        return carry

    lax.fori_loop(0, 16, value_block, 0)

    def state_block(b, carry):
        cols = pl.ds(pl.multiple_of(b * 128, 128), 128)
        sback[:, cols] = conv(sbuf, s_tap, cols).astype(bf16)
        return carry

    lax.fori_loop(0, 4, state_block, 0)
    vg_own[...] = back[pl.ds(mine, TOK), :]
    vg_out[...] = back[pl.ds(other, TOK), :]
    sg_own[...] = sback[pl.ds(mine, TOK), :]
    sg_out[...] = sback[pl.ds(other, TOK), :]


def join_kernel(
    ids, v_own, v_in, s_own, s_in, t_own, t_in, e0, e1, v_tap, s_tap, v_out, s_out, t_out
):
    core = ids[0]

    def place(out, own, arrived, width, where):
        here = pl.multiple_of(core * width, width)
        there = pl.multiple_of((1 - core) * width, width)
        out[:, pl.ds(here, width)] = own[...]
        out[:, pl.ds(there, width)] = arrived[...]

    def patch(out, tap, edge, width, group, start):
        cols = slice(group * width, (group + 1) * width)
        rows = edge[:, start : start + width]
        row = iota((TAIL, width), 0)
        acc = out[TOK - TAIL :, cols].astype(f32)
        for shift in range(1, CONV):
            j = CONV - 1 - shift
            for k in range(shift):
                acc = acc + jnp.where(
                    row == TAIL - shift + k, tap[j : j + 1, cols] * rows[k : k + 1], 0.0
                )
        out[TOK - TAIL :, cols] = acc.astype(bf16)

    place(v_out, v_own, v_in, WIDE, core)
    place(s_out, s_own, s_in, 2 * STATE, core)
    for group, edge in enumerate((e0, e1)):
        patch(v_out, v_tap, edge, WIDE, group, 0)
        patch(s_out, s_tap, edge, 2 * STATE, group, WIDE)
    lanes = iota((TOK, HEADS), 1)
    own, arrived = t_own[:, :HEADS].astype(f32), t_in[:, :HEADS].astype(f32)
    low = jnp.where(core == 0, own, arrived)
    high = jnp.where(core == 0, arrived, own)
    t_out[...] = jnp.concatenate([low, high], axis=1).astype(bf16)


def call(kernel, ids, specs, args, outs, scratch=(), name=None):
    def full(shape):
        return pl.BlockSpec(shape, lambda i, s, n=len(shape): (0,) * n)

    in_specs = [full(a.shape) if spec is None else spec for spec, a in zip(specs, args)]
    result = pl.pallas_call(
        kernel,
        grid_spec=pltpu.PrefetchScalarGridSpec(
            num_scalar_prefetch=1,
            grid=(1,),
            in_specs=in_specs,
            out_specs=[full(o[0]) for o in outs],
            scratch_shapes=[pltpu.VMEM(*s) for s in scratch],
        ),
        out_shape=[jax.ShapeDtypeStruct(*o) for o in outs],
        compiler_params=pltpu.CompilerParams(vmem_limit_bytes=56 * 1024 * 1024),
        name=name,
    )(ids, *args)
    return result


def local(
    value_input, state_input, step_raw, upstream, step_bias, decay_log, skip_gain,
    value_kernel, value_offset, state_kernel, state_offset,
):
    count = lax.axis_size("ctx")
    index = lax.axis_index("ctx")
    core = index % CORES
    ring = (index // CORES) % RING
    ids = jnp.stack([core, ring]).astype(jnp.int32)
    chips = count // CORES

    def send(x, pairs):
        return lax.ppermute(x, "ctx", pairs)

    swap_pairs = [(i, i ^ 1) for i in range(count)]

    def around(i, shift):
        half, place, c = i // (RING * CORES), (i // CORES) % RING, i % CORES
        return (half * RING + (place + shift) % RING) * CORES + c

    def ring_send(x, shift):
        return send(x, [(i, around(i, shift)) for i in range(count)])

    def pick(x, group, width):
        return lax.dynamic_slice_in_dim(x, group * width, width, 1)

    g = upstream[0]
    g_own = lax.ppermute(pick(g, core, WIDE), "pipe", [(0, 1), (1, 0)])
    g_in = lax.ppermute(
        pick(g, 1 - core, WIDE),
        ("pipe", "ctx"),
        [(p * count + i, (1 - p) * count + (i ^ 1)) for p in range(2) for i in range(count)],
    )
    v, s, r = value_input[0], state_input[0], step_raw[0]
    v_in = send(pick(v, 1 - core, WIDE), swap_pairs)
    s_in = send(pick(s, 1 - core, 2 * STATE), swap_pairs)
    r_own = jnp.tile(pick(r, core, HEADS), (1, 4))
    r_in = send(jnp.tile(pick(r, 1 - core, HEADS), (1, 4)), swap_pairs)

    def tail(group):
        return jnp.concatenate(
            [
                v[TOK - TAIL :, group * WIDE : (group + 1) * WIDE],
                s[TOK - TAIL :, group * 2 * STATE : (group + 1) * 2 * STATE],
            ],
            axis=1,
        )

    halo_a = send(tail(1), [(k * 2 + 1, k * 2 + 3) for k in range(chips - 1)])
    halo_b = send(tail(0), [(k * 2 + 1, k * 2 + 2) for k in range(chips - 1)])

    row = lambda x: x.reshape(1, -1)
    bias = jnp.tile(row(lax.dynamic_slice_in_dim(step_bias, core * HEADS, HEADS)), (1, 4))
    rate_log = jnp.tile(row(lax.dynamic_slice_in_dim(decay_log, core * HEADS, HEADS)), (1, 4))
    skip = row(
        jnp.repeat(lax.dynamic_slice_in_dim(skip_gain, core * HEADS, HEADS), HEAD_DIM)
    )

    def group_block(rows, width):
        return pl.BlockSpec((rows, width), lambda i, ids: (0, ids[0]))

    tall = (ROWS, WIDE)
    narrow = (ROWS, 128)
    message = ((STATE + TAIL, PART), bf16)
    state_part = ((STATE, PART), bf16)
    v_spec, s_spec = group_block(CONV, WIDE), group_block(CONV, 2 * STATE)
    (m0, m1, m2, m3, x, xs, sx, bc, sbc, delta, within, sig) = call(
        first_kernel,
        ids,
        [group_block(TOK, WIDE), None, group_block(TOK, 2 * STATE)] + [None] * 7
        + [v_spec, group_block(1, WIDE), s_spec, group_block(1, 2 * STATE)],
        [v, v_in, s, s_in, r_own, r_in, halo_a, halo_b, bias, rate_log,
         value_kernel, row(value_offset), state_kernel, row(state_offset)],
        [message] * 4
        + [(tall, bf16)] * 3
        + [((ROWS, 2 * STATE), bf16)] * 2
        + [(narrow, f32)] * 3,
        [((ROWS + 8, WIDE), f32), ((ROWS + 8, 2 * STATE), f32), (narrow, f32), (tall, f32)],
        name="first",
    )

    def exchange(parts):
        return [parts[0]] + [ring_send(parts[k], k) for k in range(1, RING)]

    def exchange_back(parts):
        return [parts[0]] + [ring_send(parts[k], -k) for k in range(1, RING)]

    per_half = count // HALVES
    marks = exchange((m0, m1, m2, m3))
    edge = call(
        functools.partial(edge_kernel, False), ids, [None] * 8, marks + marks, [state_part],
        name="edge_forward",
    )[0]
    edge = send(edge, [(i, i + per_half) for i in range(per_half)])
    carried = exchange_back(
        call(
            functools.partial(scan_kernel, False), ids, [None] * 9, marks + marks + [edge],
            [state_part] * 4, name="scan_forward",
        )
    )

    d0, d1, d2, d3, dy, dye = call(
        second_kernel, ids, [None] * 4, [g_own, g_in, bc, within],
        [state_part] * 4 + [(tall, bf16)] * 2, [(tall, f32)], name="second",
    )
    grads = exchange((d0, d1, d2, d3))
    edge_back = call(
        functools.partial(edge_kernel, True), ids, [None] * 8, marks + grads, [state_part],
        name="edge_back",
    )[0]
    edge_back = send(edge_back, [(i + per_half, i) for i in range(per_half)])
    back = exchange_back(
        call(
            functools.partial(scan_kernel, True), ids, [None] * 9, marks + grads + [edge_back],
            [state_part] * 4, name="scan_back",
        )
    )

    u, dbc, diff = call(
        lambda ids, *refs: inner_kernel(*refs), ids, [None] * 5, [x, dy, bc, delta, within],
        [(tall, f32), ((ROWS, 2 * STATE), f32), (narrow, f32)],
        [(tall, f32), ((128, ROWS), f32), ((128, ROWS), f32), ((ROWS, ROWS), f32),
         ((ROWS, ROWS), f32)],
        name="inner",
    )
    outer, dread, held = call(
        carry_kernel, ids, [None] * 7, list(carried) + [bc, dye, dbc],
        [(narrow, f32), ((ROWS, STATE), f32), ((STATE, WIDE), bf16)], name="carry",
    )
    edge_shape = ((8, WIDE + 2 * STATE), f32)
    vg_own, vg_out, sg_own, sg_out, st_own, st_out, head = call(
        last_kernel,
        ids,
        [None] * 21 + [v_spec, s_spec],
        list(back)
        + [held, bc, x, xs, dy, u, sx, sbc, delta, within, sig, diff, outer, dread, dbc,
           rate_log, skip, value_kernel, state_kernel],
        [((TOK, WIDE), bf16)] * 2 + [((TOK, 2 * STATE), bf16)] * 2 + [((TOK, 128), bf16)] * 2
        + [edge_shape],
        [((STATE, WIDE), bf16), ((ROWS + 8, WIDE), f32), ((ROWS + 8, 2 * STATE), f32),
         (narrow, f32), (tall, bf16), ((ROWS, 2 * STATE), bf16)],
        name="last",
    )
    vg_in, sg_in, st_in = send(vg_out, swap_pairs), send(sg_out, swap_pairs), send(st_out, swap_pairs)
    e0 = send(head, [(k * 2, k * 2 - 1) for k in range(1, chips)])
    e1 = send(head, [(k * 2 + 1, k * 2 - 1) for k in range(1, chips)])
    value_out, state_out, step_out = call(
        join_kernel,
        ids,
        [None] * 10,
        [vg_own, vg_in, sg_own, sg_in, st_own, st_in, e0, e1, value_kernel, state_kernel],
        [((TOK, 2 * WIDE), bf16), ((TOK, 4 * STATE), bf16), ((TOK, 2 * HEADS), bf16)],
        name="join",
    )
    return value_out[None], state_out[None], step_out[None]


def solution(mesh):
    wide = P("pipe", "ctx", "tp")
    placed = (wide, wide, wide, wide, P("tp"), P("tp"), P("tp"), P(None, "tp"), P("tp"), P(None, "tp"), P("tp"))
    return jax.shard_map(
        local, mesh=mesh, in_specs=placed, out_specs=(wide, wide, wide), check_vma=False
    )
```

```python
import functools

import jax
import jax.numpy as jnp
from jax import lax
from jax.experimental import pallas as pl
from jax.experimental.pallas import tpu as pltpu
from jax.sharding import PartitionSpec as P

HEAD_DIM = 64
STATE = 256
CONV = 4
CORES = 2
RING = 4
HALVES = 2
f32 = jnp.float32
bf16 = jnp.bfloat16
HIGH = lax.Precision.HIGHEST

TOK = 128
ROWS = TOK * CORES
HEADS = 32
WIDE = HEADS * HEAD_DIM
PART = WIDE // RING
TAIL = 16
LOG2E = 1.4426950408889634


def place():
    index = lax.axis_index("ctx")
    return lax.rem(index, CORES), lax.rem(lax.div(index, CORES), RING)


def rows_of(core):
    return (
        pl.ds(pl.multiple_of(core * TOK, TOK), TOK),
        pl.ds(pl.multiple_of((1 - core) * TOK, TOK), TOK),
    )


def block128(b, start=0):
    return pl.ds(pl.multiple_of(start + b * 128, 128), 128)


def head_columns(ring, slot):
    return pl.ds(pl.multiple_of(lax.rem(ring + slot, RING) * PART, PART), PART)


def nn(a, b, precision=None):
    return lax.dot_general(
        a, b, (((1,), (0,)), ((), ())), precision=precision, preferred_element_type=f32
    )


def nt(a, b):
    return lax.dot_general(a, b, (((1,), (1,)), ((), ())), preferred_element_type=f32)


def iota(shape, axis):
    return lax.broadcasted_iota(jnp.int32, shape, axis)


def split3(x):
    high = x.astype(bf16).astype(f32)
    rest = x - high
    mid = rest.astype(bf16).astype(f32)
    low = rest - mid
    part = iota(x.shape, 1) // HEADS
    picked = jnp.where(part == 0, high, jnp.where(part == 1, mid, jnp.where(part == 2, low, 0.0)))
    return picked.astype(bf16)


def head_sum(x, ones):
    high = x.astype(bf16)
    low = (x - high.astype(f32)).astype(bf16)
    return nt(high, ones) + nt(low, ones)


def tiled_heads(x, group):
    x = x.astype(f32)
    mine = jnp.where(group == 0, x[:, :HEADS], x[:, HEADS:])
    return jnp.concatenate([mine] * 4, axis=1)


def softplus(x):
    u = jnp.exp(-jnp.abs(x))
    small = u * (1.0 - u * (0.5 - u * (1.0 / 3.0 - u * 0.25)))
    return jnp.maximum(x, 0.0) + jnp.where(u < 0.01, small, jnp.log(1.0 + u))


def sigmoid(x):
    return 1.0 / (1.0 + jnp.exp(-x))


def sigmoid_by_tanh(x):
    return 0.5 + 0.5 * jnp.tanh(0.5 * x)


def pack_kernel(v, s, r, message, halo_a, halo_b, sems):
    core, ring = place()
    there = 1 - core
    copies = [
        (v.at[:, pl.ds(pl.multiple_of(there * WIDE, 128), WIDE)], message.at[:, pl.ds(0, WIDE)]),
        (
            s.at[:, pl.ds(pl.multiple_of(there * 2 * STATE, 128), 2 * STATE)],
            message.at[:, pl.ds(WIDE, 2 * STATE)],
        ),
    ]
    for group, halo in ((1, halo_a), (0, halo_b)):
        rows = pl.ds(TOK - TAIL, TAIL)
        copies.append((v.at[rows, pl.ds(group * WIDE, WIDE)], halo.at[:, pl.ds(0, WIDE)]))
        copies.append(
            (s.at[rows, pl.ds(group * 2 * STATE, 2 * STATE)], halo.at[:, pl.ds(WIDE, 2 * STATE)])
        )
    copies = [pltpu.make_async_copy(a, b, sems.at[k]) for k, (a, b) in enumerate(copies)]
    for copy in copies:
        copy.start()
    message[:, WIDE + 2 * STATE :] = tiled_heads(r[...], there).astype(bf16)
    for copy in copies:
        copy.wait()


def pack_grad_kernel(g, own, across, sems):
    core, ring = place()
    copies = [
        pltpu.make_async_copy(
            g.at[:, pl.ds(pl.multiple_of(group * WIDE, 128), WIDE)], out, sems.at[k]
        )
        for k, (group, out) in enumerate(((core, own), (1 - core, across)))
    ]
    for copy in copies:
        copy.start()
    for copy in copies:
        copy.wait()


def ones_kernel(out):
    rows = iota((128, WIDE), 0) % HEADS
    cols = iota((128, WIDE), 1) // HEAD_DIM
    out[...] = jnp.where(rows == cols, 1.0, 0.0).astype(bf16)


def first_kernel(
    v, s, r, message, halo_a, halo_b, step_bias, decay_log, v_tap, v_off, s_tap, s_off, ones,
    m0, m1, m2, m3, x_out, xs_out, sx_out, k_out, bc_out, sbc_out, delta_out, within_out, sig_out,
    buf, sbuf, raw, wide,
):
    core, ring = place()
    mine, other = rows_of(core)
    raw[mine, :] = tiled_heads(r[...], core)
    raw[other, :] = message[:, WIDE + 2 * STATE :].astype(f32)
    pre = raw[...] + tiled_heads(step_bias[...], core)
    delta = softplus(pre)
    rate = -jnp.exp(tiled_heads(decay_log[...], core))
    lower = jnp.where(iota((ROWS, ROWS), 0) >= iota((ROWS, ROWS), 1), 1.0, 0.0).astype(f32)
    within = nn(lower, delta * rate, HIGH)
    delta_out[...] = delta
    within_out[...] = within
    sig_out[...] = sigmoid(pre)
    total = within[ROWS - 1 : ROWS, :]
    wide[...] = nn(split3(delta * jnp.exp(total - within)), ones[...])

    below = pl.ds(pl.multiple_of(8 + core * TOK, 8), TOK)
    above = pl.ds(pl.multiple_of(8 + (1 - core) * TOK, 8), TOK)
    v_mine = pl.ds(pl.multiple_of(core * WIDE, 128), WIDE)
    s_mine = pl.ds(pl.multiple_of(core * 2 * STATE, 128), 2 * STATE)
    buf[below, :] = v[:, v_mine].astype(f32)
    buf[above, :] = message[:, :WIDE].astype(f32)
    sbuf[below, :] = s[:, s_mine].astype(f32)
    sbuf[above, :] = message[:, WIDE : WIDE + 2 * STATE].astype(f32)
    halo = halo_a[...].astype(f32) + halo_b[...].astype(f32)
    buf[0:8, :] = halo[8:16, :WIDE]
    sbuf[0:8, :] = halo[8:16, WIDE:]

    def conv(source, tap, off, b, width):
        cols, par = block128(b), block128(b, core * width)
        acc = off[:, par] + tap[0:1, par] * source[5 : 5 + ROWS, cols]
        for j in range(1, CONV):
            acc = acc + tap[j : j + 1, par] * source[5 + j : 5 + j + ROWS, cols]
        sig = sigmoid_by_tanh(acc)
        return acc * sig, sig * (1.0 + acc * (1.0 - sig))

    def state_block(b, carry):
        cols = block128(b)
        post, slope = conv(sbuf, s_tap, s_off, b, 2 * STATE)
        bc_out[:, cols] = post.astype(bf16)
        sbc_out[:, cols] = slope.astype(bf16)
        return carry

    lax.fori_loop(0, 4, state_block, 0)

    def value_block(b, carry):
        cols = block128(b)
        post, slope = conv(buf, v_tap, v_off, b, WIDE)
        post = post.astype(bf16)
        scale = wide[:, cols]
        x_out[:, cols] = post
        sx_out[:, cols] = slope.astype(bf16)
        k_out[:, cols] = (slope * scale).astype(bf16)
        xs_out[:, cols] = (post.astype(f32) * scale).astype(bf16)
        return carry

    lax.fori_loop(0, 16, value_block, 0)

    write_t = bc_out[:, :STATE].astype(f32).T.astype(bf16)
    total_parts = split3(jnp.broadcast_to(total, (8, 128)))
    for slot, out in enumerate((m0, m1, m2, m3)):
        cols = head_columns(ring, slot)
        out[0:STATE, :] = nn(write_t, xs_out[:, cols]).astype(bf16)
        full = nn(total_parts, ones[:, cols])[0:1, :]
        high = full.astype(bf16).astype(f32)
        mid = (full - high).astype(bf16).astype(f32)
        low = full - high - mid
        row = iota((TAIL, PART), 0)
        out[STATE : STATE + TAIL, :] = jnp.where(
            row == 0, high, jnp.where(row == 1, mid, jnp.where(row == 2, low, 0.0))
        ).astype(bf16)


def ring_totals(parts):
    out = []
    for part in parts:
        rows = part[STATE : STATE + TAIL, :].astype(f32)
        out.append(rows[0:1] + rows[1:2] + rows[2:3])
    return out


def between(totals, places, low, high):
    out = jnp.zeros_like(totals[0])
    for total, p in zip(totals, places):
        inside = jnp.logical_and(p > low, p < high)
        out = out + total * jnp.where(inside, 1.0, 0.0)
    return out


def edge_kernel(back, m0, m1, m2, m3, d0, d1, d2, d3, out):
    core, ring = place()
    places = [lax.rem(ring + RING - s, RING) for s in range(RING)]
    totals = ring_totals((m0, m1, m2, m3))
    weights = []
    for p in places:
        low, high = (-1, p) if back else (p, RING)
        weights.append(jnp.exp(between(totals, places, low, high)))
    for c in range(0, PART, 128):
        cols = slice(c, c + 128)
        acc = None
        for src, weight in zip((d0, d1, d2, d3), weights):
            term = weight[:, cols] * src[0:STATE, cols].astype(f32)
            acc = term if acc is None else acc + term
        out[:, cols] = acc.astype(bf16)


def scan_kernel(back, m0, m1, m2, m3, d0, d1, d2, d3, edge, o0, o1, o2, o3):
    core, ring = place()
    places = [lax.rem(ring + RING - s, RING) for s in range(RING)]
    totals = ring_totals((m0, m1, m2, m3))
    weights = []
    for here in places:
        low, high = (here, RING) if back else (-1, here)
        row = [jnp.exp(between(totals, places, low, high))]
        for p in places:
            low, high, live = (here, p, p > here) if back else (p, here, p < here)
            row.append(jnp.exp(between(totals, places, low, high)) * jnp.where(live, 1.0, 0.0))
        weights.append(row)
    for c in range(0, PART, 128):
        cols = slice(c, c + 128)
        for r in range(0, STATE, 64):
            rows = slice(r, r + 64)
            parts = [edge[rows, cols].astype(f32)]
            parts += [src[rows, cols].astype(f32) for src in (d0, d1, d2, d3)]
            for out, row in zip((o0, o1, o2, o3), weights):
                acc = row[0][:, cols] * parts[0]
                for weight, part in zip(row[1:], parts[1:]):
                    acc = acc + weight[:, cols] * part
                out[rows, cols] = acc.astype(bf16)


def second_kernel(g_own, g_in, bc, within, ones, d0, d1, d2, d3, dy_out, dye_out, wide):
    core, ring = place()
    mine, other = rows_of(core)
    dy_out[mine, :] = g_own[...]
    dy_out[other, :] = g_in[...]
    wide[...] = nn(split3(jnp.exp(within[...])), ones[...])
    read_t = bc[:, STATE:].astype(f32).T.astype(bf16)

    def block(b, carry):
        cols = block128(b)
        dye_out[:, cols] = (dy_out[:, cols].astype(f32) * wide[:, cols]).astype(bf16)
        return carry

    lax.fori_loop(0, 16, block, 0)
    for slot, out in enumerate((d0, d1, d2, d3)):
        out[...] = nn(read_t, dye_out[:, head_columns(ring, slot)]).astype(bf16)


def inner_kernel(
    x, dy, bc, delta, within, sx, skip_gain, ones,
    base_out, dbc_out, diff_out, vsum_out,
    wide, skips, within_3, row_sum, bcs, dbcs,
):
    core, ring = place()
    half = ROWS // 2
    wide[...] = nn(split3(delta[...]), ones[...])
    skip = jnp.broadcast_to(tiled_heads(skip_gain[...], core), (8, 128))
    skips[...] = nn(split3(skip), ones[...])
    scaled = within[...] * LOG2E
    lane_part = iota((ROWS, 128), 1) // HEADS
    left = jnp.where(lane_part == 3, 1.0, -split3(scaled).astype(f32)).astype(bf16)
    parts_t = split3(scaled).astype(f32).T
    for h in range(HEADS):
        within_3[h, 0:1, :] = parts_t[h : h + 1, :]
        within_3[h, 1:2, :] = parts_t[HEADS + h : HEADS + h + 1, :]
        within_3[h, 2:3, :] = parts_t[2 * HEADS + h : 2 * HEADS + h + 1, :]
        within_3[h, 3:8, :] = jnp.zeros((5, ROWS), f32)
    write, read = bc[:, :STATE], bc[:, STATE:]
    bcs[...] = nt(write, read)
    dbcs[...] = jnp.zeros_like(dbcs)
    diff_out[...] = jnp.zeros_like(diff_out)
    vsum_out[...] = jnp.zeros_like(vsum_out)
    keep = iota((half, half), 1) >= iota((half, half), 0)
    lanes = iota((ROWS, 128), 1)
    first = lanes < HEAD_DIM
    row_head = iota((96, ROWS), 0) % HEADS
    pad = jnp.zeros((24, ROWS), f32)

    def pair(b, carry):
        cols = block128(b)
        xb = x[:, cols].astype(f32)
        xd = (xb * wide[:, cols]).astype(bf16)
        grad = dy[:, cols]
        zero = jnp.zeros_like(grad)
        top = jnp.zeros((half, 128), f32)
        bot = jnp.zeros((half, 128), f32)
        col_total = jnp.zeros((ROWS, 128), f32)
        grads_of = [0.0, 0.0, 0.0]
        for e in range(2):
            h = 2 * b + e
            g = jnp.where(first, grad, zero) if e == 0 else jnp.where(first, zero, grad)
            right = jnp.concatenate(
                [jnp.where(row_head == h, 1.0, 0.0), within_3[h], pad], axis=0
            ).astype(bf16)
            gap0 = nn(left[:half], right)
            gap1 = nn(left[half:], right[:, half:])
            dm0 = nt(xd[:half], g)
            dm1 = nt(xd[half:], g[half:])
            blocks = (
                (jnp.where(keep, gap0[:, :half], -jnp.inf), dm0[:, :half], 0, 0),
                (gap0[:, half:], dm0[:, half:], 0, 1),
                (jnp.where(keep, gap1, -jnp.inf), dm1, 1, 1),
            )
            ps, ms = [], []
            for k, (gap, dm, r, c) in enumerate(blocks):
                decay = jnp.exp2(gap)
                m = decay * bcs[r * half : (r + 1) * half, c * half : (c + 1) * half]
                grads_of[k] = grads_of[k] + dm * decay
                ps.append(dm * m)
                ms.append(m.astype(bf16))
            sum_rows = jnp.concatenate(
                [
                    jnp.sum(ps[0], axis=0, keepdims=True),
                    jnp.sum(ps[1] + ps[2], axis=0, keepdims=True),
                ],
                axis=1,
            )
            row_sum[pl.ds(h, 1), :] = sum_rows
            top = top + nn(ms[0], g[:half]) + nn(ms[1], g[half:])
            bot = bot + nn(ms[2], g[half:])
            col = jnp.concatenate(
                [
                    jnp.sum(ps[0] + ps[1], axis=1, keepdims=True),
                    jnp.sum(ps[2], axis=1, keepdims=True),
                ],
                axis=0,
            )
            col_total = col_total + jnp.where(lanes % HEADS == h, col, 0.0)
        for k, (r, c) in enumerate(((0, 0), (0, 1), (1, 1))):
            rs, cs = slice(r * half, (r + 1) * half), slice(c * half, (c + 1) * half)
            dbcs[rs, cs] = dbcs[rs, cs] + grads_of[k]
        u = jnp.concatenate([top, bot], axis=0)
        diff_out[...] = diff_out[...] - col_total
        vsum_out[...] = vsum_out[...] + head_sum(xb * u, ones[:, cols])
        base_out[:, cols] = (
            wide[:, cols] * u + skips[0:1, cols] * grad.astype(f32)
        ) * sx[:, cols].astype(f32)
        return carry

    lax.fori_loop(0, 16, pair, 0)
    for t in range(1, 4):
        row_sum[t * HEADS : (t + 1) * HEADS, :] = row_sum[0:HEADS, :]
    diff_out[...] = diff_out[...] + row_sum[...].T
    grad = dbcs[...]
    dbc_out[:, :STATE] = nn(grad.astype(bf16), read)
    dbc_out[:, STATE:] = nn(grad.T.astype(bf16), write)


def carry_kernel(c0, c1, c2, c3, bc, dye, dbc, diff, ones, diff_out, dread_out, carried_out):
    core, ring = place()
    for slot, src in enumerate((c0, c1, c2, c3)):
        carried_out[:, head_columns(ring, slot)] = src[...]
    read = bc[:, STATE:]
    dread_out[...] = dbc[:, STATE:] + nt(dye[...], carried_out[...])
    outer = diff[...]
    for b in range(4):
        cols = slice(b * PART, (b + 1) * PART)
        part = nn(read, carried_out[:, cols]) * dye[:, cols].astype(f32)
        outer = outer + head_sum(part, ones[:, cols])
    diff_out[...] = outer


def last_kernel(
    g0, g1, g2, g3, carried, bc, xs, k, base, sbc, delta, within, sig, diff, vsum,
    dread, dbc, decay_log, v_tap, s_tap, ones,
    vg_own, sg_own, st_own, message, head_out,
    gbuf, ebuf, sbuf, dbuf, back, sback,
):
    core, ring = place()
    mine, other = rows_of(core)
    for slot, src in enumerate((g0, g1, g2, g3)):
        gbuf[:, head_columns(ring, slot)] = src[...]
    write = bc[:, :STATE]
    rsum = jnp.zeros((ROWS, 128), f32)
    tsum = jnp.zeros((8, 128), f32)
    ebuf[ROWS : ROWS + 8, :] = jnp.zeros((8, WIDE), f32)
    sbuf[ROWS : ROWS + 8, :] = jnp.zeros((8, 2 * STATE), f32)
    for b in range(4):
        cols = slice(b * PART, (b + 1) * PART)
        grad = gbuf[:, cols]
        through = nn(write, grad)
        rsum = rsum + head_sum(xs[:, cols].astype(f32) * through, ones[:, cols])
        ebuf[0:ROWS, cols] = base[:, cols] + k[:, cols].astype(f32) * through
        both = jnp.sum(
            grad.astype(f32) * carried[:, cols].astype(f32), axis=0, keepdims=True
        )
        tsum = tsum + head_sum(jnp.broadcast_to(both, (8, PART)), ones[:, cols])
    total = within[ROWS - 1 : ROWS, :]
    dtotal = tsum[0:1, :] * jnp.exp(total)
    ra, rb = iota((ROWS, ROWS), 0), iota((ROWS, ROWS), 1)
    later = jnp.where(rb >= ra, 1.0, 0.0).astype(f32)
    earlier = jnp.where(rb < ra, 1.0, 0.0).astype(f32)
    da = nn(later, diff[...], HIGH) + nn(earlier, rsum, HIGH) + dtotal
    rate = -jnp.exp(tiled_heads(decay_log[...], core))
    dbuf[...] = (vsum[...] + rsum / delta[...] + rate * da) * sig[...]
    st_own[...] = dbuf[mine, :].astype(bf16)
    message[:, WIDE + 2 * STATE :] = dbuf[other, :].astype(bf16)

    dwrite = dbc[:, :STATE] + nt(xs[...], gbuf[...])
    sbuf[0:ROWS, :STATE] = dwrite * sbc[:, :STATE].astype(f32)
    sbuf[0:ROWS, STATE:] = dread[...] * sbc[:, STATE:].astype(f32)
    head_out[:, :WIDE] = ebuf[0:8, :]
    head_out[:, WIDE:] = sbuf[0:8, :]

    def conv(source, tap, b, width):
        cols, par = block128(b), block128(b, core * width)
        acc = tap[CONV - 1 : CONV, par] * source[0:ROWS, cols]
        for shift in range(1, CONV):
            j = CONV - 1 - shift
            acc = acc + tap[j : j + 1, par] * source[shift : shift + ROWS, cols]
        return acc.astype(bf16)

    def value_block(b, carry):
        back[:, block128(b)] = conv(ebuf, v_tap, b, WIDE)
        return carry

    lax.fori_loop(0, 16, value_block, 0)

    def state_block(b, carry):
        sback[:, block128(b)] = conv(sbuf, s_tap, b, 2 * STATE)
        return carry

    lax.fori_loop(0, 4, state_block, 0)
    vg_own[...] = back[mine, :]
    message[:, :WIDE] = back[other, :]
    sg_own[...] = sback[mine, :]
    message[:, WIDE : WIDE + 2 * STATE] = sback[other, :]


def join_kernel(v_own, s_own, t_own, message, e0, e1, v_tap, s_tap, v_out, s_out, t_out):
    core, ring = place()

    def place_in(out, own, arrived, width):
        out[:, pl.ds(pl.multiple_of(core * width, 128), width)] = own
        out[:, pl.ds(pl.multiple_of((1 - core) * width, 128), width)] = arrived

    def patch(out, tap, edge, width, group, start):
        cols = slice(group * width, (group + 1) * width)
        rows = edge[:, start : start + width]
        row = iota((TAIL, width), 0)
        acc = out[TOK - TAIL :, cols].astype(f32)
        for shift in range(1, CONV):
            j = CONV - 1 - shift
            for k in range(shift):
                acc = acc + jnp.where(
                    row == TAIL - shift + k, tap[j : j + 1, cols] * rows[k : k + 1], 0.0
                )
        out[TOK - TAIL :, cols] = acc.astype(bf16)

    place_in(v_out, v_own[...], message[:, :WIDE], WIDE)
    place_in(s_out, s_own[...], message[:, WIDE : WIDE + 2 * STATE], 2 * STATE)

    @pl.when(core == CORES - 1)
    def _():
        for group, edge in enumerate((e0, e1)):
            patch(v_out, v_tap, edge, WIDE, group, 0)
            patch(s_out, s_tap, edge, 2 * STATE, group, WIDE)

    own = t_own[:, :HEADS].astype(f32)
    arrived = message[:, WIDE + 2 * STATE : WIDE + 2 * STATE + HEADS].astype(f32)
    low = jnp.where(core == 0, own, arrived)
    high = jnp.where(core == 0, arrived, own)
    t_out[...] = jnp.concatenate([low, high], axis=1).astype(bf16)


def call(kernel, args, outs, scratch=(), name=None, anywhere=(), cost=None):
    vmem = pl.BlockSpec(memory_space=pltpu.VMEM)
    return pl.pallas_call(
        kernel,
        in_specs=[
            pl.BlockSpec(memory_space=pl.ANY) if k in anywhere else vmem for k in range(len(args))
        ],
        out_specs=[vmem for _ in outs],
        out_shape=[jax.ShapeDtypeStruct(*o) for o in outs],
        scratch_shapes=[s if not isinstance(s, tuple) else pltpu.VMEM(*s) for s in scratch],
        compiler_params=pltpu.CompilerParams(vmem_limit_bytes=24 * 1024 * 1024),
        cost_estimate=None
        if cost is None
        else pl.CostEstimate(flops=0, transcendentals=0, bytes_accessed=int(cost * 3.0e6)),
        name=name,
    )(*args)


def local(
    value_input, state_input, step_raw, upstream, step_bias, decay_log, skip_gain,
    value_kernel, value_offset, state_kernel, state_offset,
):
    count = lax.axis_size("ctx")
    chips = count // CORES
    per_half = count // HALVES

    def send(x, pairs):
        return lax.ppermute(x, "ctx", pairs)

    swap_pairs = [(i, i ^ 1) for i in range(count)]

    def around(i, shift):
        half, at, c = i // (RING * CORES), (i // CORES) % RING, i % CORES
        return (half * RING + (at + shift) % RING) * CORES + c

    def exchange(parts, sign):
        out = [parts[0]]
        for k in range(1, RING):
            out.append(send(parts[k], [(i, around(i, sign * k)) for i in range(count)]))
        return out

    row = lambda x: x.reshape(1, -1)
    v, s, r, g = value_input[0], state_input[0], step_raw[0], upstream[0]
    bias, rate_log, skip = row(step_bias), row(decay_log), row(skip_gain)
    joint = WIDE + 2 * STATE + 128
    tall = (ROWS, WIDE)
    narrow = (ROWS, 128)
    marked = ((STATE + TAIL, PART), bf16)
    state_part = ((STATE, PART), bf16)
    sems = pltpu.SemaphoreType.DMA

    message, halo_a, halo_b = call(
        pack_kernel, [v, s, r],
        [((TOK, joint), bf16), ((TAIL, WIDE + 2 * STATE), bf16), ((TAIL, WIDE + 2 * STATE), bf16)],
        [sems((6,))], "pack", (0, 1),
    )
    message = send(message, swap_pairs)
    halo_a = send(halo_a, [(k * 2 + 1, k * 2 + 3) for k in range(chips - 1)])
    halo_b = send(halo_b, [(k * 2 + 1, k * 2 + 2) for k in range(chips - 1)])
    g_own, g_in = call(
        pack_grad_kernel, [g], [((TOK, WIDE), bf16)] * 2, [sems((2,))], "pack_grad", (0,)
    )
    g_own = lax.ppermute(g_own, "pipe", [(0, 1), (1, 0)])
    g_in = lax.ppermute(
        g_in,
        ("pipe", "ctx"),
        [(p * count + i, (1 - p) * count + (i ^ 1)) for p in range(2) for i in range(count)],
    )
    ones = call(ones_kernel, [], [((128, WIDE), bf16)], name="ones")[0]
    (m0, m1, m2, m3, x, xs, sx, k, bc, sbc, delta, within, sig) = call(
        first_kernel,
        [v, s, r, message, halo_a, halo_b, bias, rate_log,
         value_kernel, row(value_offset), state_kernel, row(state_offset), ones],
        [marked] * 4 + [(tall, bf16)] * 4 + [((ROWS, 2 * STATE), bf16)] * 2 + [(narrow, f32)] * 3,
        [((ROWS + 8, WIDE), f32), ((ROWS + 8, 2 * STATE), f32), (narrow, f32), (tall, f32)],
        "first", cost=8,
    )
    marks = exchange((m0, m1, m2, m3), 1)
    d0, d1, d2, d3, dy, dye = call(
        second_kernel, [g_own, g_in, bc, within, ones],
        [state_part] * 4 + [(tall, bf16)] * 2, [(tall, f32)], "second", cost=4,
    )
    grads = exchange((d0, d1, d2, d3), 1)
    edge = call(
        functools.partial(edge_kernel, False), marks + marks, [state_part], (), "edge_forward",
        cost=2,
    )[0]
    edge_in = send(edge, [(i, i + per_half) for i in range(per_half)])
    dy_now, _ = lax.optimization_barrier((dy, edge))
    base, dbc, diff, vsum = call(
        inner_kernel, [x, dy_now, bc, delta, within, sx, skip, ones],
        [(tall, f32), ((ROWS, 2 * STATE), f32), (narrow, f32), (narrow, f32)],
        [(tall, f32), ((8, WIDE), f32), ((HEADS, 8, ROWS), f32), ((128, ROWS), f32),
         ((ROWS, ROWS), f32), ((ROWS, ROWS), f32)],
        "inner", cost=12,
    )
    edge_in, diff = lax.optimization_barrier((edge_in, diff))
    carried = exchange(
        call(
            functools.partial(scan_kernel, False), marks + marks + [edge_in],
            [state_part] * 4, (), "scan_forward", cost=3,
        ),
        -1,
    )
    edge_back = call(
        functools.partial(edge_kernel, True), marks + grads, [state_part], (), "edge_back", cost=2,
    )[0]
    edge_back = send(edge_back, [(i + per_half, i) for i in range(per_half)])
    back = exchange(
        call(
            functools.partial(scan_kernel, True), marks + grads + [edge_back],
            [state_part] * 4, (), "scan_back", cost=3,
        ),
        -1,
    )
    diff, dread, held = call(
        carry_kernel, list(carried) + [bc, dye, dbc, diff, ones],
        [(narrow, f32), ((ROWS, STATE), f32), ((STATE, WIDE), bf16)], (), "carry", cost=4,
    )
    vg_own, sg_own, st_own, message, head = call(
        last_kernel,
        list(back)
        + [held, bc, xs, k, base, sbc, delta, within, sig, diff, vsum, dread, dbc,
           rate_log, value_kernel, state_kernel, ones],
        [((TOK, WIDE), bf16), ((TOK, 2 * STATE), bf16), ((TOK, 128), bf16),
         ((TOK, joint), bf16), ((8, WIDE + 2 * STATE), f32)],
        [((STATE, WIDE), bf16), ((ROWS + 8, WIDE), f32), ((ROWS + 8, 2 * STATE), f32),
         (narrow, f32), (tall, bf16), ((ROWS, 2 * STATE), bf16)],
        "last", cost=8,
    )
    e0 = send(head, [(j * 2, j * 2 - 1) for j in range(1, chips)])
    e1 = send(head, [(j * 2 + 1, j * 2 - 1) for j in range(1, chips)])
    message = send(message, swap_pairs)
    value_out, state_out, step_out = call(
        join_kernel,
        [vg_own, sg_own, st_own, message, e0, e1, value_kernel, state_kernel],
        [((TOK, 2 * WIDE), bf16), ((TOK, 4 * STATE), bf16), ((TOK, 2 * HEADS), bf16)],
        (), "join",
    )
    return value_out[None], state_out[None], step_out[None]


def solution(mesh):
    wide = P("pipe", "ctx", "tp")
    placed = (wide, wide, wide, wide, P("tp"), P("tp"), P("tp"), P(None, "tp"), P("tp"), P(None, "tp"), P("tp"))
    return jax.shard_map(
        local, mesh=mesh, in_specs=placed, out_specs=(wide, wide, wide), check_vma=False
    )
```

```python
import functools

import jax
import jax.numpy as jnp
from jax import lax
from jax.experimental import pallas as pl
from jax.experimental.pallas import tpu as pltpu
from jax.sharding import PartitionSpec as P

HEAD_DIM = 64
STATE = 256
CONV = 4
CORES = 2
RING = 4
HALVES = 2
f32 = jnp.float32
bf16 = jnp.bfloat16
HIGH = lax.Precision.HIGHEST

TOK = 128
ROWS = TOK * CORES
HEADS = 32
WIDE = HEADS * HEAD_DIM
PART = WIDE // RING
TAIL = 16
LOG2E = 1.4426950408889634


def place():
    index = lax.axis_index("ctx")
    return lax.rem(index, CORES), lax.rem(lax.div(index, CORES), RING)


def rows_of(core):
    return (
        pl.ds(pl.multiple_of(core * TOK, TOK), TOK),
        pl.ds(pl.multiple_of((1 - core) * TOK, TOK), TOK),
    )


def block128(b, start=0):
    return pl.ds(pl.multiple_of(start + b * 128, 128), 128)


def head_columns(ring, slot):
    return pl.ds(pl.multiple_of(lax.rem(ring + slot, RING) * PART, PART), PART)


def nn(a, b, precision=None):
    return lax.dot_general(
        a, b, (((1,), (0,)), ((), ())), precision=precision, preferred_element_type=f32
    )


def nt(a, b):
    return lax.dot_general(a, b, (((1,), (1,)), ((), ())), preferred_element_type=f32)


def iota(shape, axis):
    return lax.broadcasted_iota(jnp.int32, shape, axis)


def split3(x):
    high = x.astype(bf16).astype(f32)
    rest = x - high
    mid = rest.astype(bf16).astype(f32)
    low = rest - mid
    part = iota(x.shape, 1) // HEADS
    picked = jnp.where(part == 0, high, jnp.where(part == 1, mid, jnp.where(part == 2, low, 0.0)))
    return picked.astype(bf16)


def head_sum(x, ones):
    high = x.astype(bf16)
    low = (x - high.astype(f32)).astype(bf16)
    return nt(high, ones) + nt(low, ones)


def tiled_heads(x, group):
    x = x.astype(f32)
    mine = jnp.where(group == 0, x[:, :HEADS], x[:, HEADS:])
    return jnp.concatenate([mine] * 4, axis=1)


def tiled_steps(x, group):
    x = x.astype(f32)
    mine = jnp.where(group == 0, x[:HEADS], x[HEADS:])
    return jnp.concatenate([mine] * 4, axis=0).T


def softplus(x):
    u = jnp.exp(-jnp.abs(x))
    small = u * (1.0 - u * (0.5 - u * (1.0 / 3.0 - u * 0.25)))
    return jnp.maximum(x, 0.0) + jnp.where(u < 0.01, small, jnp.log(1.0 + u))


def sigmoid(x):
    return 1.0 / (1.0 + jnp.exp(-x))


def sigmoid_by_tanh(x):
    return 0.5 + 0.5 * jnp.tanh(0.5 * x)


def pack_kernel(v, s, r, message, halo_a, halo_b, sems):
    core, ring = place()
    there = 1 - core
    copies = [
        (v.at[:, pl.ds(pl.multiple_of(there * WIDE, 128), WIDE)], message.at[:, pl.ds(0, WIDE)]),
        (
            s.at[:, pl.ds(pl.multiple_of(there * 2 * STATE, 128), 2 * STATE)],
            message.at[:, pl.ds(WIDE, 2 * STATE)],
        ),
    ]
    for group, halo in ((1, halo_a), (0, halo_b)):
        rows = pl.ds(TOK - TAIL, TAIL)
        copies.append((v.at[rows, pl.ds(group * WIDE, WIDE)], halo.at[:, pl.ds(0, WIDE)]))
        copies.append(
            (s.at[rows, pl.ds(group * 2 * STATE, 2 * STATE)], halo.at[:, pl.ds(WIDE, 2 * STATE)])
        )
    copies = [pltpu.make_async_copy(a, b, sems.at[k]) for k, (a, b) in enumerate(copies)]
    for copy in copies:
        copy.start()
    message[:, WIDE + 2 * STATE :] = tiled_steps(r[...], there).astype(bf16)
    for copy in copies:
        copy.wait()


def pack_grad_kernel(g, own, across, sems):
    core, ring = place()
    copies = [
        pltpu.make_async_copy(
            g.at[:, pl.ds(pl.multiple_of(group * WIDE, 128), WIDE)], out, sems.at[k]
        )
        for k, (group, out) in enumerate(((core, own), (1 - core, across)))
    ]
    for copy in copies:
        copy.start()
    for copy in copies:
        copy.wait()


def ones_kernel(out):
    rows = iota((128, WIDE), 0) % HEADS
    cols = iota((128, WIDE), 1) // HEAD_DIM
    out[...] = jnp.where(rows == cols, 1.0, 0.0).astype(bf16)


def first_kernel(
    v, s, r, message, halo_a, halo_b, step_bias, decay_log, v_tap, v_off, s_tap, s_off, ones,
    m0, m1, m2, m3, x_out, xs_out, sx_out, k_out, bc_out, sbc_out, delta_out, within_out, sig_out,
    buf, sbuf, raw, wide,
):
    core, ring = place()
    mine, other = rows_of(core)
    raw[mine, :] = tiled_steps(r[...], core)
    raw[other, :] = message[:, WIDE + 2 * STATE :].astype(f32)
    pre = raw[...] + tiled_heads(step_bias[...], core)
    delta = softplus(pre)
    rate = -jnp.exp(tiled_heads(decay_log[...], core))
    lower = jnp.where(iota((ROWS, ROWS), 0) >= iota((ROWS, ROWS), 1), 1.0, 0.0).astype(f32)
    within = nn(lower, delta * rate, HIGH)
    delta_out[...] = delta
    within_out[...] = within
    sig_out[...] = sigmoid(pre)
    total = within[ROWS - 1 : ROWS, :]
    wide[...] = nn(split3(delta * jnp.exp(total - within)), ones[...])

    below = pl.ds(pl.multiple_of(8 + core * TOK, 8), TOK)
    above = pl.ds(pl.multiple_of(8 + (1 - core) * TOK, 8), TOK)
    v_mine = pl.ds(pl.multiple_of(core * WIDE, 128), WIDE)
    s_mine = pl.ds(pl.multiple_of(core * 2 * STATE, 128), 2 * STATE)
    buf[below, :] = v[:, v_mine].astype(f32)
    buf[above, :] = message[:, :WIDE].astype(f32)
    sbuf[below, :] = s[:, s_mine].astype(f32)
    sbuf[above, :] = message[:, WIDE : WIDE + 2 * STATE].astype(f32)
    halo = halo_a[...].astype(f32) + halo_b[...].astype(f32)
    buf[0:8, :] = halo[8:16, :WIDE]
    sbuf[0:8, :] = halo[8:16, WIDE:]

    def conv(source, tap, off, b, width):
        cols, par = block128(b), block128(b, core * width)
        acc = off[:, par] + tap[0:1, par] * source[5 : 5 + ROWS, cols]
        for j in range(1, CONV):
            acc = acc + tap[j : j + 1, par] * source[5 + j : 5 + j + ROWS, cols]
        sig = sigmoid_by_tanh(acc)
        return acc * sig, sig * (1.0 + acc * (1.0 - sig))

    def state_block(b, carry):
        cols = block128(b)
        post, slope = conv(sbuf, s_tap, s_off, b, 2 * STATE)
        bc_out[:, cols] = post.astype(bf16)
        sbc_out[:, cols] = slope.astype(bf16)
        return carry

    lax.fori_loop(0, 4, state_block, 0)

    def value_block(b, carry):
        cols = block128(b)
        post, slope = conv(buf, v_tap, v_off, b, WIDE)
        post = post.astype(bf16)
        scale = wide[:, cols]
        x_out[:, cols] = post
        sx_out[:, cols] = slope.astype(bf16)
        k_out[:, cols] = (slope * scale).astype(bf16)
        xs_out[:, cols] = (post.astype(f32) * scale).astype(bf16)
        return carry

    lax.fori_loop(0, 16, value_block, 0)

    write_t = bc_out[:, :STATE].astype(f32).T.astype(bf16)
    total_parts = split3(jnp.broadcast_to(total, (8, 128)))
    for slot, out in enumerate((m0, m1, m2, m3)):
        cols = head_columns(ring, slot)
        out[0:STATE, :] = nn(write_t, xs_out[:, cols]).astype(bf16)
        full = nn(total_parts, ones[:, cols])[0:1, :]
        high = full.astype(bf16).astype(f32)
        mid = (full - high).astype(bf16).astype(f32)
        low = full - high - mid
        row = iota((TAIL, PART), 0)
        out[STATE : STATE + TAIL, :] = jnp.where(
            row == 0, high, jnp.where(row == 1, mid, jnp.where(row == 2, low, 0.0))
        ).astype(bf16)


def ring_totals(parts):
    out = []
    for part in parts:
        rows = part[STATE : STATE + TAIL, :].astype(f32)
        out.append(rows[0:1] + rows[1:2] + rows[2:3])
    return out


def between(totals, places, low, high):
    out = jnp.zeros_like(totals[0])
    for total, p in zip(totals, places):
        inside = jnp.logical_and(p > low, p < high)
        out = out + total * jnp.where(inside, 1.0, 0.0)
    return out


def edge_kernel(back, m0, m1, m2, m3, d0, d1, d2, d3, out):
    core, ring = place()
    places = [lax.rem(ring + RING - s, RING) for s in range(RING)]
    totals = ring_totals((m0, m1, m2, m3))
    weights = []
    for p in places:
        low, high = (-1, p) if back else (p, RING)
        weights.append(jnp.exp(between(totals, places, low, high)))
    for c in range(0, PART, 128):
        cols = slice(c, c + 128)
        acc = None
        for src, weight in zip((d0, d1, d2, d3), weights):
            term = weight[:, cols] * src[0:STATE, cols].astype(f32)
            acc = term if acc is None else acc + term
        out[:, cols] = acc.astype(bf16)


def scan_kernel(back, m0, m1, m2, m3, d0, d1, d2, d3, edge, o0, o1, o2, o3):
    core, ring = place()
    places = [lax.rem(ring + RING - s, RING) for s in range(RING)]
    totals = ring_totals((m0, m1, m2, m3))
    weights = []
    for here in places:
        low, high = (here, RING) if back else (-1, here)
        row = [jnp.exp(between(totals, places, low, high))]
        for p in places:
            low, high, live = (here, p, p > here) if back else (p, here, p < here)
            row.append(jnp.exp(between(totals, places, low, high)) * jnp.where(live, 1.0, 0.0))
        weights.append(row)
    for c in range(0, PART, 128):
        cols = slice(c, c + 128)
        for r in range(0, STATE, 64):
            rows = slice(r, r + 64)
            parts = [edge[rows, cols].astype(f32)]
            parts += [src[rows, cols].astype(f32) for src in (d0, d1, d2, d3)]
            for out, row in zip((o0, o1, o2, o3), weights):
                acc = row[0][:, cols] * parts[0]
                for weight, part in zip(row[1:], parts[1:]):
                    acc = acc + weight[:, cols] * part
                out[rows, cols] = acc.astype(bf16)


def second_kernel(g_own, g_in, bc, within, ones, d0, d1, d2, d3, dy_out, dye_out, wide):
    core, ring = place()
    mine, other = rows_of(core)
    dy_out[mine, :] = g_own[...]
    dy_out[other, :] = g_in[...]
    wide[...] = nn(split3(jnp.exp(within[...])), ones[...])
    read_t = bc[:, STATE:].astype(f32).T.astype(bf16)

    def block(b, carry):
        cols = block128(b)
        dye_out[:, cols] = (dy_out[:, cols].astype(f32) * wide[:, cols]).astype(bf16)
        return carry

    lax.fori_loop(0, 16, block, 0)
    for slot, out in enumerate((d0, d1, d2, d3)):
        out[...] = nn(read_t, dye_out[:, head_columns(ring, slot)]).astype(bf16)


def inner_kernel(
    x, dy, bc, delta, within, sx, skip_gain, ones,
    base_out, dbc_out, diff_out, vsum_out,
    wide, skips, within_3, row_sum, bcs, dbcs,
):
    core, ring = place()
    half = ROWS // 2
    wide[...] = nn(split3(delta[...]), ones[...])
    skip = jnp.broadcast_to(tiled_heads(skip_gain[...], core), (8, 128))
    skips[...] = nn(split3(skip), ones[...])
    scaled = within[...] * LOG2E
    lane_part = iota((ROWS, 128), 1) // HEADS
    left = jnp.where(lane_part == 3, 1.0, -split3(scaled).astype(f32)).astype(bf16)
    parts_t = split3(scaled).astype(f32).T
    for h in range(HEADS):
        within_3[h, 0:1, :] = parts_t[h : h + 1, :]
        within_3[h, 1:2, :] = parts_t[HEADS + h : HEADS + h + 1, :]
        within_3[h, 2:3, :] = parts_t[2 * HEADS + h : 2 * HEADS + h + 1, :]
        within_3[h, 3:8, :] = jnp.zeros((5, ROWS), f32)
    write, read = bc[:, :STATE], bc[:, STATE:]
    bcs[...] = nt(write, read)
    dbcs[...] = jnp.zeros_like(dbcs)
    diff_out[...] = jnp.zeros_like(diff_out)
    vsum_out[...] = jnp.zeros_like(vsum_out)
    keep = iota((half, half), 1) >= iota((half, half), 0)
    lanes = iota((ROWS, 128), 1)
    first = lanes < HEAD_DIM
    row_head = iota((96, ROWS), 0) % HEADS
    pad = jnp.zeros((24, ROWS), f32)

    def pair(b, carry):
        cols = block128(b)
        xb = x[:, cols].astype(f32)
        xd = (xb * wide[:, cols]).astype(bf16)
        grad = dy[:, cols]
        zero = jnp.zeros_like(grad)
        top = jnp.zeros((half, 128), f32)
        bot = jnp.zeros((half, 128), f32)
        col_total = jnp.zeros((ROWS, 128), f32)
        grads_of = [0.0, 0.0, 0.0]
        for e in range(2):
            h = 2 * b + e
            g = jnp.where(first, grad, zero) if e == 0 else jnp.where(first, zero, grad)
            right = jnp.concatenate(
                [jnp.where(row_head == h, 1.0, 0.0), within_3[h], pad], axis=0
            ).astype(bf16)
            gap0 = nn(left[:half], right)
            gap1 = nn(left[half:], right[:, half:])
            dm0 = nt(xd[:half], g)
            dm1 = nt(xd[half:], g[half:])
            blocks = (
                (jnp.where(keep, gap0[:, :half], -jnp.inf), dm0[:, :half], 0, 0),
                (gap0[:, half:], dm0[:, half:], 0, 1),
                (jnp.where(keep, gap1, -jnp.inf), dm1, 1, 1),
            )
            ps, ms = [], []
            for k, (gap, dm, r, c) in enumerate(blocks):
                decay = jnp.exp2(gap)
                m = decay * bcs[r * half : (r + 1) * half, c * half : (c + 1) * half]
                grads_of[k] = grads_of[k] + dm * decay
                ps.append(dm * m)
                ms.append(m.astype(bf16))
            sum_rows = jnp.concatenate(
                [
                    jnp.sum(ps[0], axis=0, keepdims=True),
                    jnp.sum(ps[1] + ps[2], axis=0, keepdims=True),
                ],
                axis=1,
            )
            row_sum[pl.ds(h, 1), :] = sum_rows
            top = top + nn(ms[0], g[:half]) + nn(ms[1], g[half:])
            bot = bot + nn(ms[2], g[half:])
            col = jnp.concatenate(
                [
                    jnp.sum(ps[0] + ps[1], axis=1, keepdims=True),
                    jnp.sum(ps[2], axis=1, keepdims=True),
                ],
                axis=0,
            )
            col_total = col_total + jnp.where(lanes % HEADS == h, col, 0.0)
        for k, (r, c) in enumerate(((0, 0), (0, 1), (1, 1))):
            rs, cs = slice(r * half, (r + 1) * half), slice(c * half, (c + 1) * half)
            dbcs[rs, cs] = dbcs[rs, cs] + grads_of[k]
        u = jnp.concatenate([top, bot], axis=0)
        diff_out[...] = diff_out[...] - col_total
        vsum_out[...] = vsum_out[...] + head_sum(xb * u, ones[:, cols])
        base_out[:, cols] = (
            wide[:, cols] * u + skips[0:1, cols] * grad.astype(f32)
        ) * sx[:, cols].astype(f32)
        return carry

    lax.fori_loop(0, 16, pair, 0)
    for t in range(1, 4):
        row_sum[t * HEADS : (t + 1) * HEADS, :] = row_sum[0:HEADS, :]
    diff_out[...] = diff_out[...] + row_sum[...].T
    grad = dbcs[...]
    dbc_out[:, :STATE] = nn(grad.astype(bf16), read)
    dbc_out[:, STATE:] = nn(grad.T.astype(bf16), write)


def carry_kernel(c0, c1, c2, c3, bc, dye, dbc, diff, ones, diff_out, dread_out, carried_out):
    core, ring = place()
    for slot, src in enumerate((c0, c1, c2, c3)):
        carried_out[:, head_columns(ring, slot)] = src[...]
    read = bc[:, STATE:]
    dread_out[...] = dbc[:, STATE:] + nt(dye[...], carried_out[...])
    outer = diff[...]
    for b in range(4):
        cols = slice(b * PART, (b + 1) * PART)
        part = nn(read, carried_out[:, cols]) * dye[:, cols].astype(f32)
        outer = outer + head_sum(part, ones[:, cols])
    diff_out[...] = outer


def last_kernel(
    g0, g1, g2, g3, carried, bc, xs, k, base, sbc, delta, within, sig, diff, vsum,
    dread, dbc, decay_log, v_tap, s_tap, ones,
    vg_own, sg_own, st_own, message, head_out,
    gbuf, ebuf, sbuf, dbuf, back, sback,
):
    core, ring = place()
    mine, other = rows_of(core)
    for slot, src in enumerate((g0, g1, g2, g3)):
        gbuf[:, head_columns(ring, slot)] = src[...]
    write = bc[:, :STATE]
    rsum = jnp.zeros((ROWS, 128), f32)
    tsum = jnp.zeros((8, 128), f32)
    ebuf[ROWS : ROWS + 8, :] = jnp.zeros((8, WIDE), f32)
    sbuf[ROWS : ROWS + 8, :] = jnp.zeros((8, 2 * STATE), f32)
    for b in range(4):
        cols = slice(b * PART, (b + 1) * PART)
        grad = gbuf[:, cols]
        through = nn(write, grad)
        rsum = rsum + head_sum(xs[:, cols].astype(f32) * through, ones[:, cols])
        ebuf[0:ROWS, cols] = base[:, cols] + k[:, cols].astype(f32) * through
        both = jnp.sum(
            grad.astype(f32) * carried[:, cols].astype(f32), axis=0, keepdims=True
        )
        tsum = tsum + head_sum(jnp.broadcast_to(both, (8, PART)), ones[:, cols])
    total = within[ROWS - 1 : ROWS, :]
    dtotal = tsum[0:1, :] * jnp.exp(total)
    ra, rb = iota((ROWS, ROWS), 0), iota((ROWS, ROWS), 1)
    later = jnp.where(rb >= ra, 1.0, 0.0).astype(f32)
    earlier = jnp.where(rb < ra, 1.0, 0.0).astype(f32)
    da = nn(later, diff[...], HIGH) + nn(earlier, rsum, HIGH) + dtotal
    rate = -jnp.exp(tiled_heads(decay_log[...], core))
    dbuf[...] = (vsum[...] + rsum / delta[...] + rate * da) * sig[...]
    st_own[...] = dbuf[mine, :].astype(bf16)
    message[:, WIDE + 2 * STATE :] = dbuf[other, :].astype(bf16)

    dwrite = dbc[:, :STATE] + nt(xs[...], gbuf[...])
    sbuf[0:ROWS, :STATE] = dwrite * sbc[:, :STATE].astype(f32)
    sbuf[0:ROWS, STATE:] = dread[...] * sbc[:, STATE:].astype(f32)
    head_out[:, :WIDE] = ebuf[0:8, :]
    head_out[:, WIDE:] = sbuf[0:8, :]

    def conv(source, tap, b, width):
        cols, par = block128(b), block128(b, core * width)
        acc = tap[CONV - 1 : CONV, par] * source[0:ROWS, cols]
        for shift in range(1, CONV):
            j = CONV - 1 - shift
            acc = acc + tap[j : j + 1, par] * source[shift : shift + ROWS, cols]
        return acc.astype(bf16)

    def value_block(b, carry):
        back[:, block128(b)] = conv(ebuf, v_tap, b, WIDE)
        return carry

    lax.fori_loop(0, 16, value_block, 0)

    def state_block(b, carry):
        sback[:, block128(b)] = conv(sbuf, s_tap, b, 2 * STATE)
        return carry

    lax.fori_loop(0, 4, state_block, 0)
    vg_own[...] = back[mine, :]
    message[:, :WIDE] = back[other, :]
    sg_own[...] = sback[mine, :]
    message[:, WIDE : WIDE + 2 * STATE] = sback[other, :]


def join_kernel(v_own, s_own, t_own, message, e0, e1, v_tap, s_tap, v_out, s_out, t_out):
    core, ring = place()

    def place_in(out, own, arrived, width):
        out[:, pl.ds(pl.multiple_of(core * width, 128), width)] = own
        out[:, pl.ds(pl.multiple_of((1 - core) * width, 128), width)] = arrived

    def patch(out, tap, edge, width, group, start):
        cols = slice(group * width, (group + 1) * width)
        rows = edge[:, start : start + width]
        row = iota((TAIL, width), 0)
        acc = out[TOK - TAIL :, cols].astype(f32)
        for shift in range(1, CONV):
            j = CONV - 1 - shift
            for k in range(shift):
                acc = acc + jnp.where(
                    row == TAIL - shift + k, tap[j : j + 1, cols] * rows[k : k + 1], 0.0
                )
        out[TOK - TAIL :, cols] = acc.astype(bf16)

    place_in(v_out, v_own[...], message[:, :WIDE], WIDE)
    place_in(s_out, s_own[...], message[:, WIDE : WIDE + 2 * STATE], 2 * STATE)

    @pl.when(core == CORES - 1)
    def _():
        for group, edge in enumerate((e0, e1)):
            patch(v_out, v_tap, edge, WIDE, group, 0)
            patch(s_out, s_tap, edge, 2 * STATE, group, WIDE)

    own = t_own[...].astype(f32).T[:HEADS]
    arrived = message[:, WIDE + 2 * STATE :].astype(f32).T[:HEADS]
    low = jnp.where(core == 0, own, arrived)
    high = jnp.where(core == 0, arrived, own)
    t_out[...] = jnp.concatenate([low, high], axis=0).astype(bf16)


def call(kernel, args, outs, scratch=(), name=None, anywhere=(), cost=None):
    vmem = pl.BlockSpec(memory_space=pltpu.VMEM)
    return pl.pallas_call(
        kernel,
        in_specs=[
            pl.BlockSpec(memory_space=pltpu.HBM) if k in anywhere else vmem for k in range(len(args))
        ],
        out_specs=[vmem for _ in outs],
        out_shape=[jax.ShapeDtypeStruct(*o) for o in outs],
        scratch_shapes=[s if not isinstance(s, tuple) else pltpu.VMEM(*s) for s in scratch],
        compiler_params=pltpu.CompilerParams(vmem_limit_bytes=24 * 1024 * 1024),
        cost_estimate=None
        if cost is None
        else pl.CostEstimate(flops=0, transcendentals=0, bytes_accessed=int(cost * 3.0e6)),
        name=name,
    )(*args)


def local(
    value_input, state_input, step_raw, upstream, step_bias, decay_log, skip_gain,
    value_kernel, value_offset, state_kernel, state_offset,
):
    count = lax.axis_size("ctx")
    chips = count // CORES
    per_half = count // HALVES

    def send(x, pairs):
        return lax.ppermute(x, "ctx", pairs)

    swap_pairs = [(i, i ^ 1) for i in range(count)]

    def around(i, shift):
        half, at, c = i // (RING * CORES), (i // CORES) % RING, i % CORES
        return (half * RING + (at + shift) % RING) * CORES + c

    def exchange(parts, sign):
        out = [parts[0]]
        for k in range(1, RING):
            out.append(send(parts[k], [(i, around(i, sign * k)) for i in range(count)]))
        return out

    row = lambda x: x.reshape(1, -1)
    v, s, r, g = value_input[0], state_input[0], step_raw[0].T, upstream[0]
    bias, rate_log, skip = row(step_bias), row(decay_log), row(skip_gain)
    joint = WIDE + 2 * STATE + 128
    tall = (ROWS, WIDE)
    narrow = (ROWS, 128)
    marked = ((STATE + TAIL, PART), bf16)
    state_part = ((STATE, PART), bf16)
    sems = pltpu.SemaphoreType.DMA

    message, halo_a, halo_b = call(
        pack_kernel, [v, s, r],
        [((TOK, joint), bf16), ((TAIL, WIDE + 2 * STATE), bf16), ((TAIL, WIDE + 2 * STATE), bf16)],
        [sems((6,))], "pack", (0, 1),
    )
    message = send(message, swap_pairs)
    halo_a = send(halo_a, [(k * 2 + 1, k * 2 + 3) for k in range(chips - 1)])
    halo_b = send(halo_b, [(k * 2 + 1, k * 2 + 2) for k in range(chips - 1)])
    g, message, halo_a, halo_b = lax.optimization_barrier((g, message, halo_a, halo_b))
    g_own, g_in = call(
        pack_grad_kernel, [g], [((TOK, WIDE), bf16)] * 2, [sems((2,))], "pack_grad", (0,)
    )
    g_own = lax.ppermute(g_own, "pipe", [(0, 1), (1, 0)])
    g_in = lax.ppermute(
        g_in,
        ("pipe", "ctx"),
        [(p * count + i, (1 - p) * count + (i ^ 1)) for p in range(2) for i in range(count)],
    )
    ones = call(ones_kernel, [], [((128, WIDE), bf16)], name="ones")[0]
    (m0, m1, m2, m3, x, xs, sx, k, bc, sbc, delta, within, sig) = call(
        first_kernel,
        [v, s, r, message, halo_a, halo_b, bias, rate_log,
         value_kernel, row(value_offset), state_kernel, row(state_offset), ones],
        [marked] * 4 + [(tall, bf16)] * 4 + [((ROWS, 2 * STATE), bf16)] * 2 + [(narrow, f32)] * 3,
        [((ROWS + 8, WIDE), f32), ((ROWS + 8, 2 * STATE), f32), (narrow, f32), (tall, f32)],
        "first", cost=8,
    )
    marks = exchange((m0, m1, m2, m3), 1)
    d0, d1, d2, d3, dy, dye = call(
        second_kernel, [g_own, g_in, bc, within, ones],
        [state_part] * 4 + [(tall, bf16)] * 2, [(tall, f32)], "second", cost=4,
    )
    grads = exchange((d0, d1, d2, d3), 1)
    edge = call(
        functools.partial(edge_kernel, False), marks + marks, [state_part], (), "edge_forward",
        cost=2,
    )[0]
    edge_in = send(edge, [(i, i + per_half) for i in range(per_half)])
    dy_now, _ = lax.optimization_barrier((dy, edge))
    base, dbc, diff, vsum = call(
        inner_kernel, [x, dy_now, bc, delta, within, sx, skip, ones],
        [(tall, f32), ((ROWS, 2 * STATE), f32), (narrow, f32), (narrow, f32)],
        [(tall, f32), ((8, WIDE), f32), ((HEADS, 8, ROWS), f32), ((128, ROWS), f32),
         ((ROWS, ROWS), f32), ((ROWS, ROWS), f32)],
        "inner", cost=12,
    )
    edge_in, diff = lax.optimization_barrier((edge_in, diff))
    carried = exchange(
        call(
            functools.partial(scan_kernel, False), marks + marks + [edge_in],
            [state_part] * 4, (), "scan_forward", cost=3,
        ),
        -1,
    )
    edge_back = call(
        functools.partial(edge_kernel, True), marks + grads, [state_part], (), "edge_back", cost=2,
    )[0]
    edge_back = send(edge_back, [(i + per_half, i) for i in range(per_half)])
    back = exchange(
        call(
            functools.partial(scan_kernel, True), marks + grads + [edge_back],
            [state_part] * 4, (), "scan_back", cost=3,
        ),
        -1,
    )
    diff, dread, held = call(
        carry_kernel, list(carried) + [bc, dye, dbc, diff, ones],
        [(narrow, f32), ((ROWS, STATE), f32), ((STATE, WIDE), bf16)], (), "carry", cost=4,
    )
    vg_own, sg_own, st_own, message, head = call(
        last_kernel,
        list(back)
        + [held, bc, xs, k, base, sbc, delta, within, sig, diff, vsum, dread, dbc,
           rate_log, value_kernel, state_kernel, ones],
        [((TOK, WIDE), bf16), ((TOK, 2 * STATE), bf16), ((TOK, 128), bf16),
         ((TOK, joint), bf16), ((8, WIDE + 2 * STATE), f32)],
        [((STATE, WIDE), bf16), ((ROWS + 8, WIDE), f32), ((ROWS + 8, 2 * STATE), f32),
         (narrow, f32), (tall, bf16), ((ROWS, 2 * STATE), bf16)],
        "last", cost=8,
    )
    e0 = send(head, [(j * 2, j * 2 - 1) for j in range(1, chips)])
    e1 = send(head, [(j * 2 + 1, j * 2 - 1) for j in range(1, chips)])
    message = send(message, swap_pairs)
    value_out, state_out, step_out = call(
        join_kernel,
        [vg_own, sg_own, st_own, message, e0, e1, value_kernel, state_kernel],
        [((TOK, 2 * WIDE), bf16), ((TOK, 4 * STATE), bf16), ((2 * HEADS, TOK), bf16)],
        (), "join",
    )
    return value_out[None], state_out[None], step_out.T[None]


def solution(mesh):
    wide = P("pipe", "ctx", "tp")
    placed = (wide, wide, wide, wide, P("tp"), P("tp"), P("tp"), P(None, "tp"), P("tp"), P(None, "tp"), P("tp"))
    return jax.shard_map(
        local, mesh=mesh, in_specs=placed, out_specs=(wide, wide, wide), check_vma=False
    )
```

```python
import functools

import jax
import jax.numpy as jnp
from jax import lax
from jax.experimental import pallas as pl
from jax.experimental.pallas import tpu as pltpu
from jax.sharding import PartitionSpec as P

HEAD_DIM = 64
STATE = 256
CONV = 4
CORES = 2
RING = 4
HALVES = 2
f32 = jnp.float32
bf16 = jnp.bfloat16
HIGH = lax.Precision.HIGHEST

TOK = 128
ROWS = TOK * CORES
HEADS = 32
WIDE = HEADS * HEAD_DIM
PART = WIDE // RING
TAIL = 16
LOG2E = 1.4426950408889634


def place():
    index = lax.axis_index("ctx")
    return lax.rem(index, CORES), lax.rem(lax.div(index, CORES), RING)


def rows_of(core):
    return (
        pl.ds(pl.multiple_of(core * TOK, TOK), TOK),
        pl.ds(pl.multiple_of((1 - core) * TOK, TOK), TOK),
    )


def block128(b, start=0):
    return pl.ds(pl.multiple_of(start + b * 128, 128), 128)


def head_columns(ring, slot):
    return pl.ds(pl.multiple_of(lax.rem(ring + slot, RING) * PART, PART), PART)


def nn(a, b, precision=None):
    return lax.dot_general(
        a, b, (((1,), (0,)), ((), ())), precision=precision, preferred_element_type=f32
    )


def nt(a, b):
    return lax.dot_general(a, b, (((1,), (1,)), ((), ())), preferred_element_type=f32)


def iota(shape, axis):
    return lax.broadcasted_iota(jnp.int32, shape, axis)


def split3(x):
    high = x.astype(bf16).astype(f32)
    rest = x - high
    mid = rest.astype(bf16).astype(f32)
    low = rest - mid
    part = iota(x.shape, 1) // HEADS
    picked = jnp.where(part == 0, high, jnp.where(part == 1, mid, jnp.where(part == 2, low, 0.0)))
    return picked.astype(bf16)


def head_sum(x, ones):
    high = x.astype(bf16)
    low = (x - high.astype(f32)).astype(bf16)
    return nt(high, ones) + nt(low, ones)


def tiled_heads(x, group):
    x = x.astype(f32)
    mine = jnp.where(group == 0, x[:, :HEADS], x[:, HEADS:])
    return jnp.concatenate([mine] * 4, axis=1)


def tiled_steps(x, group):
    x = x.astype(f32)
    mine = jnp.where(group == 0, x[:HEADS], x[HEADS:])
    return jnp.concatenate([mine] * 4, axis=0).T


def softplus(x):
    u = jnp.exp(-jnp.abs(x))
    small = u * (1.0 - u * (0.5 - u * (1.0 / 3.0 - u * 0.25)))
    return jnp.maximum(x, 0.0) + jnp.where(u < 0.01, small, jnp.log(1.0 + u))


def sigmoid(x):
    return 1.0 / (1.0 + jnp.exp(-x))


def sigmoid_by_tanh(x):
    return 0.5 + 0.5 * jnp.tanh(0.5 * x)


def pack_kernel(v, s, r, message, halo_a, halo_b, sems):
    core, ring = place()
    there = 1 - core
    copies = [
        (v.at[:, pl.ds(pl.multiple_of(there * WIDE, 128), WIDE)], message.at[:, pl.ds(0, WIDE)]),
        (
            s.at[:, pl.ds(pl.multiple_of(there * 2 * STATE, 128), 2 * STATE)],
            message.at[:, pl.ds(WIDE, 2 * STATE)],
        ),
    ]
    for group, halo in ((1, halo_a), (0, halo_b)):
        rows = pl.ds(TOK - TAIL, TAIL)
        copies.append((v.at[rows, pl.ds(group * WIDE, WIDE)], halo.at[:, pl.ds(0, WIDE)]))
        copies.append(
            (s.at[rows, pl.ds(group * 2 * STATE, 2 * STATE)], halo.at[:, pl.ds(WIDE, 2 * STATE)])
        )
    copies = [pltpu.make_async_copy(a, b, sems.at[k]) for k, (a, b) in enumerate(copies)]
    for copy in copies:
        copy.start()
    message[:, WIDE + 2 * STATE :] = tiled_steps(r[...], there).astype(bf16)
    for copy in copies:
        copy.wait()


def pack_grad_kernel(g, own, across, sems):
    core, ring = place()
    copies = [
        pltpu.make_async_copy(
            g.at[:, pl.ds(pl.multiple_of(group * WIDE, 128), WIDE)], out, sems.at[k]
        )
        for k, (group, out) in enumerate(((core, own), (1 - core, across)))
    ]
    for copy in copies:
        copy.start()
    for copy in copies:
        copy.wait()


def ones_kernel(out):
    rows = iota((128, WIDE), 0) % HEADS
    cols = iota((128, WIDE), 1) // HEAD_DIM
    out[...] = jnp.where(rows == cols, 1.0, 0.0).astype(bf16)


def first_kernel(
    v, s, r, message, halo_a, halo_b, step_bias, decay_log, v_tap, v_off, s_tap, s_off, ones,
    m0, m1, m2, m3, x_out, xs_out, sx_out, k_out, bc_out, sbc_out, delta_out, within_out, sig_out,
    buf, sbuf, raw, wide,
):
    core, ring = place()
    mine, other = rows_of(core)
    raw[mine, :] = tiled_steps(r[...], core)
    raw[other, :] = message[:, WIDE + 2 * STATE :].astype(f32)
    pre = raw[...] + tiled_heads(step_bias[...], core)
    delta = softplus(pre)
    rate = -jnp.exp(tiled_heads(decay_log[...], core))
    lower = jnp.where(iota((ROWS, ROWS), 0) >= iota((ROWS, ROWS), 1), 1.0, 0.0).astype(f32)
    within = nn(lower, delta * rate, HIGH)
    delta_out[...] = delta
    within_out[...] = within
    sig_out[...] = sigmoid(pre)
    total = within[ROWS - 1 : ROWS, :]
    wide[...] = nn(split3(delta * jnp.exp(total - within)), ones[...])

    below = pl.ds(pl.multiple_of(8 + core * TOK, 8), TOK)
    above = pl.ds(pl.multiple_of(8 + (1 - core) * TOK, 8), TOK)
    v_mine = pl.ds(pl.multiple_of(core * WIDE, 128), WIDE)
    s_mine = pl.ds(pl.multiple_of(core * 2 * STATE, 128), 2 * STATE)
    buf[below, :] = v[:, v_mine].astype(f32)
    buf[above, :] = message[:, :WIDE].astype(f32)
    sbuf[below, :] = s[:, s_mine].astype(f32)
    sbuf[above, :] = message[:, WIDE : WIDE + 2 * STATE].astype(f32)
    halo = halo_a[...].astype(f32) + halo_b[...].astype(f32)
    buf[0:8, :] = halo[8:16, :WIDE]
    sbuf[0:8, :] = halo[8:16, WIDE:]

    def conv(source, tap, off, b, width):
        cols, par = block128(b), block128(b, core * width)
        acc = off[:, par] + tap[0:1, par] * source[5 : 5 + ROWS, cols]
        for j in range(1, CONV):
            acc = acc + tap[j : j + 1, par] * source[5 + j : 5 + j + ROWS, cols]
        sig = sigmoid_by_tanh(acc)
        return acc * sig, sig * (1.0 + acc * (1.0 - sig))

    def state_block(b, carry):
        cols = block128(b)
        post, slope = conv(sbuf, s_tap, s_off, b, 2 * STATE)
        bc_out[:, cols] = post.astype(bf16)
        sbc_out[:, cols] = slope.astype(bf16)
        return carry

    lax.fori_loop(0, 4, state_block, 0)

    def value_block(b, carry):
        cols = block128(b)
        post, slope = conv(buf, v_tap, v_off, b, WIDE)
        post = post.astype(bf16)
        scale = wide[:, cols]
        x_out[:, cols] = post
        sx_out[:, cols] = slope.astype(bf16)
        k_out[:, cols] = (slope * scale).astype(bf16)
        xs_out[:, cols] = (post.astype(f32) * scale).astype(bf16)
        return carry

    lax.fori_loop(0, 16, value_block, 0)

    write_t = bc_out[:, :STATE].astype(f32).T.astype(bf16)
    total_parts = split3(jnp.broadcast_to(total, (8, 128)))
    for slot, out in enumerate((m0, m1, m2, m3)):
        cols = head_columns(ring, slot)
        out[0:STATE, :] = nn(write_t, xs_out[:, cols]).astype(bf16)
        full = nn(total_parts, ones[:, cols])[0:1, :]
        high = full.astype(bf16).astype(f32)
        mid = (full - high).astype(bf16).astype(f32)
        low = full - high - mid
        row = iota((TAIL, PART), 0)
        out[STATE : STATE + TAIL, :] = jnp.where(
            row == 0, high, jnp.where(row == 1, mid, jnp.where(row == 2, low, 0.0))
        ).astype(bf16)


def ring_totals(parts):
    out = []
    for part in parts:
        rows = part[STATE : STATE + TAIL, :].astype(f32)
        out.append(rows[0:1] + rows[1:2] + rows[2:3])
    return out


def between(totals, places, low, high):
    out = jnp.zeros_like(totals[0])
    for total, p in zip(totals, places):
        inside = jnp.logical_and(p > low, p < high)
        out = out + total * jnp.where(inside, 1.0, 0.0)
    return out


def edge_kernel(back, m0, m1, m2, m3, d0, d1, d2, d3, out):
    core, ring = place()
    places = [lax.rem(ring + RING - s, RING) for s in range(RING)]
    totals = ring_totals((m0, m1, m2, m3))
    weights = []
    for p in places:
        low, high = (-1, p) if back else (p, RING)
        weights.append(jnp.exp(between(totals, places, low, high)))
    for c in range(0, PART, 128):
        cols = slice(c, c + 128)
        acc = None
        for src, weight in zip((d0, d1, d2, d3), weights):
            term = weight[:, cols] * src[0:STATE, cols].astype(f32)
            acc = term if acc is None else acc + term
        out[:, cols] = acc.astype(bf16)


def scan_kernel(back, m0, m1, m2, m3, d0, d1, d2, d3, edge, o0, o1, o2, o3):
    core, ring = place()
    places = [lax.rem(ring + RING - s, RING) for s in range(RING)]
    totals = ring_totals((m0, m1, m2, m3))
    weights = []
    for here in places:
        low, high = (here, RING) if back else (-1, here)
        row = [jnp.exp(between(totals, places, low, high))]
        for p in places:
            low, high, live = (here, p, p > here) if back else (p, here, p < here)
            row.append(jnp.exp(between(totals, places, low, high)) * jnp.where(live, 1.0, 0.0))
        weights.append(row)
    for c in range(0, PART, 128):
        cols = slice(c, c + 128)
        for r in range(0, STATE, 64):
            rows = slice(r, r + 64)
            parts = [edge[rows, cols].astype(f32)]
            parts += [src[rows, cols].astype(f32) for src in (d0, d1, d2, d3)]
            for out, row in zip((o0, o1, o2, o3), weights):
                acc = row[0][:, cols] * parts[0]
                for weight, part in zip(row[1:], parts[1:]):
                    acc = acc + weight[:, cols] * part
                out[rows, cols] = acc.astype(bf16)


def second_kernel(g_own, g_in, bc, within, ones, d0, d1, d2, d3, dy_out, dye_out, wide):
    core, ring = place()
    mine, other = rows_of(core)
    dy_out[mine, :] = g_own[...]
    dy_out[other, :] = g_in[...]
    wide[...] = nn(split3(jnp.exp(within[...])), ones[...])
    read_t = bc[:, STATE:].astype(f32).T.astype(bf16)

    def block(b, carry):
        cols = block128(b)
        dye_out[:, cols] = (dy_out[:, cols].astype(f32) * wide[:, cols]).astype(bf16)
        return carry

    lax.fori_loop(0, 16, block, 0)
    for slot, out in enumerate((d0, d1, d2, d3)):
        out[...] = nn(read_t, dye_out[:, head_columns(ring, slot)]).astype(bf16)


def inner_kernel(part, x, dy, bc, delta, within, sx, skip_gain, ones, *refs):
    if part == 0:
        base_out, dbcs, diff_out, vsum_out = refs[:4]
        scratch = refs[4:]
    else:
        dbcs_in, diff_in, vsum_in, base_in = refs[:4]
        base_out, dbc_out, diff_out, vsum_out, top_out = refs[4:9]
        scratch = refs[9:]
        dbcs = scratch[-1]
    wide, skips, within_3, row_sum, bcs = scratch[:5]
    core, ring = place()
    half = ROWS // 2
    low_col, low_head = part * (WIDE // 2), part * (HEADS // 2)
    own = ones[:, low_col : low_col + WIDE // 2]
    wide[...] = nn(split3(delta[...]), own)
    skip = jnp.broadcast_to(tiled_heads(skip_gain[...], core), (8, 128))
    skips[...] = nn(split3(skip), own)
    scaled = within[...] * LOG2E
    lane_part = iota((ROWS, 128), 1) // HEADS
    left = jnp.where(lane_part == 3, 1.0, -split3(scaled).astype(f32)).astype(bf16)
    parts_t = split3(scaled).astype(f32).T
    for h in range(HEADS // 2):
        for piece in range(3):
            at = piece * HEADS + low_head + h
            within_3[h, piece : piece + 1, :] = parts_t[at : at + 1, :]
        within_3[h, 3:8, :] = jnp.zeros((5, ROWS), f32)
    write, read = bc[:, :STATE], bc[:, STATE:]
    bcs[...] = nt(write, read)
    if part == 0:
        dbcs[...] = jnp.zeros_like(dbcs)
        diff_out[...] = jnp.zeros_like(diff_out)
        vsum_out[...] = jnp.zeros_like(vsum_out)
    else:
        dbcs[...] = dbcs_in[...]
        diff_out[...] = diff_in[...]
        vsum_out[...] = vsum_in[...]
    row_sum[...] = jnp.zeros_like(row_sum)
    keep = iota((half, half), 1) >= iota((half, half), 0)
    lanes = iota((ROWS, 128), 1)
    first = lanes < HEAD_DIM
    row_head = iota((96, ROWS), 0) % HEADS
    pad = jnp.zeros((24, ROWS), f32)

    def pair(b, carry):
        cols, here = block128(b, low_col), block128(b)
        xb = x[:, cols].astype(f32)
        xd = (xb * wide[:, here]).astype(bf16)
        grad = dy[:, cols]
        zero = jnp.zeros_like(grad)
        top = jnp.zeros((half, 128), f32)
        bot = jnp.zeros((half, 128), f32)
        col_total = jnp.zeros((ROWS, 128), f32)
        grads_of = [0.0, 0.0, 0.0]
        for e in range(2):
            h = low_head + 2 * b + e
            g = jnp.where(first, grad, zero) if e == 0 else jnp.where(first, zero, grad)
            right = jnp.concatenate(
                [jnp.where(row_head == h, 1.0, 0.0), within_3[2 * b + e], pad], axis=0
            ).astype(bf16)
            gap0 = nn(left[:half], right)
            gap1 = nn(left[half:], right[:, half:])
            dm0 = nt(xd[:half], g)
            dm1 = nt(xd[half:], g[half:])
            blocks = (
                (jnp.where(keep, gap0[:, :half], -jnp.inf), dm0[:, :half], 0, 0),
                (gap0[:, half:], dm0[:, half:], 0, 1),
                (jnp.where(keep, gap1, -jnp.inf), dm1, 1, 1),
            )
            ps, ms = [], []
            for k, (gap, dm, r, c) in enumerate(blocks):
                decay = jnp.exp2(gap)
                m = decay * bcs[r * half : (r + 1) * half, c * half : (c + 1) * half]
                grads_of[k] = grads_of[k] + dm * decay
                ps.append(dm * m)
                ms.append(m.astype(bf16))
            sum_rows = jnp.concatenate(
                [
                    jnp.sum(ps[0], axis=0, keepdims=True),
                    jnp.sum(ps[1] + ps[2], axis=0, keepdims=True),
                ],
                axis=1,
            )
            row_sum[pl.ds(h, 1), :] = sum_rows
            top = top + nn(ms[0], g[:half]) + nn(ms[1], g[half:])
            bot = bot + nn(ms[2], g[half:])
            col = jnp.concatenate(
                [
                    jnp.sum(ps[0] + ps[1], axis=1, keepdims=True),
                    jnp.sum(ps[2], axis=1, keepdims=True),
                ],
                axis=0,
            )
            col_total = col_total + jnp.where(lanes % HEADS == h, col, 0.0)
        for k, (r, c) in enumerate(((0, 0), (0, 1), (1, 1))):
            rs, cs = slice(r * half, (r + 1) * half), slice(c * half, (c + 1) * half)
            dbcs[rs, cs] = dbcs[rs, cs] + grads_of[k]
        u = jnp.concatenate([top, bot], axis=0)
        diff_out[...] = diff_out[...] - col_total
        vsum_out[...] = vsum_out[...] + head_sum(xb * u, ones[:, cols])
        base_out[:, here] = (
            wide[:, here] * u + skips[0:1, here] * grad.astype(f32)
        ) * sx[:, cols].astype(f32)
        return carry

    lax.fori_loop(0, 8, pair, 0)
    for t in range(1, 4):
        row_sum[t * HEADS : (t + 1) * HEADS, :] = row_sum[0:HEADS, :]
    diff_out[...] = diff_out[...] + row_sum[...].T
    if part == 1:
        grad = dbcs[...]
        dbc_out[:, :STATE] = nn(grad.astype(bf16), read)
        dbc_out[:, STATE:] = nn(grad.T.astype(bf16), write)
        top_out[:, : WIDE // 2] = base_in[0:8, :]
        top_out[:, WIDE // 2 :] = base_out[0:8, :]


def carry_kernel(c0, c1, c2, c3, bc, dye, dbc, diff, ones, diff_out, dread_out, carried_out):
    core, ring = place()
    for slot, src in enumerate((c0, c1, c2, c3)):
        carried_out[:, head_columns(ring, slot)] = src[...]
    read = bc[:, STATE:]
    dread_out[...] = dbc[:, STATE:] + nt(dye[...], carried_out[...])
    outer = diff[...]
    for b in range(4):
        cols = slice(b * PART, (b + 1) * PART)
        part = nn(read, carried_out[:, cols]) * dye[:, cols].astype(f32)
        outer = outer + head_sum(part, ones[:, cols])
    diff_out[...] = outer


def last_kernel(
    g0, g1, g2, g3, carried, bc, xs, k, base_0, base_1, sbc, delta, within, sig, diff, vsum,
    dread, dbc, decay_log, v_tap, s_tap, ones,
    vg_own, sg_own, st_own, message,
    gbuf, ebuf, sbuf, dbuf, back, sback,
):
    core, ring = place()
    mine, other = rows_of(core)
    for slot, src in enumerate((g0, g1, g2, g3)):
        gbuf[:, head_columns(ring, slot)] = src[...]
    write = bc[:, :STATE]
    rsum = jnp.zeros((ROWS, 128), f32)
    tsum = jnp.zeros((8, 128), f32)
    ebuf[ROWS : ROWS + 8, :] = jnp.zeros((8, WIDE), f32)
    sbuf[ROWS : ROWS + 8, :] = jnp.zeros((8, 2 * STATE), f32)
    for b in range(4):
        cols = slice(b * PART, (b + 1) * PART)
        grad = gbuf[:, cols]
        through = nn(write, grad)
        rsum = rsum + head_sum(xs[:, cols].astype(f32) * through, ones[:, cols])
        base = (base_0, base_1)[b // 2][:, (b % 2) * PART : (b % 2 + 1) * PART]
        ebuf[0:ROWS, cols] = base + k[:, cols].astype(f32) * through
        both = jnp.sum(
            grad.astype(f32) * carried[:, cols].astype(f32), axis=0, keepdims=True
        )
        tsum = tsum + head_sum(jnp.broadcast_to(both, (8, PART)), ones[:, cols])
    total = within[ROWS - 1 : ROWS, :]
    dtotal = tsum[0:1, :] * jnp.exp(total)
    ra, rb = iota((ROWS, ROWS), 0), iota((ROWS, ROWS), 1)
    later = jnp.where(rb >= ra, 1.0, 0.0).astype(f32)
    earlier = jnp.where(rb < ra, 1.0, 0.0).astype(f32)
    da = nn(later, diff[...], HIGH) + nn(earlier, rsum, HIGH) + dtotal
    rate = -jnp.exp(tiled_heads(decay_log[...], core))
    dbuf[...] = (vsum[...] + rsum / delta[...] + rate * da) * sig[...]
    st_own[...] = dbuf[mine, :].astype(bf16)
    message[:, WIDE + 2 * STATE :] = dbuf[other, :].astype(bf16)

    dwrite = dbc[:, :STATE] + nt(xs[...], gbuf[...])
    sbuf[0:ROWS, :STATE] = dwrite * sbc[:, :STATE].astype(f32)
    sbuf[0:ROWS, STATE:] = dread[...] * sbc[:, STATE:].astype(f32)

    def conv(source, tap, b, width):
        cols, par = block128(b), block128(b, core * width)
        acc = tap[CONV - 1 : CONV, par] * source[0:ROWS, cols]
        for shift in range(1, CONV):
            j = CONV - 1 - shift
            acc = acc + tap[j : j + 1, par] * source[shift : shift + ROWS, cols]
        return acc.astype(bf16)

    def value_block(b, carry):
        back[:, block128(b)] = conv(ebuf, v_tap, b, WIDE)
        return carry

    lax.fori_loop(0, 16, value_block, 0)

    def state_block(b, carry):
        sback[:, block128(b)] = conv(sbuf, s_tap, b, 2 * STATE)
        return carry

    lax.fori_loop(0, 4, state_block, 0)
    vg_own[...] = back[mine, :]
    message[:, :WIDE] = back[other, :]
    sg_own[...] = sback[mine, :]
    message[:, WIDE : WIDE + 2 * STATE] = sback[other, :]


def head_kernel(g0, g1, g2, g3, bc, xs, k, base_top, sbc, dread, dbc, out):
    core, ring = place()
    write = bc[0:TAIL, :STATE]
    dwrite = dbc[0:8, :STATE]
    for slot, src in enumerate((g0, g1, g2, g3)):
        cols = head_columns(ring, slot)
        grad = src[...]
        through = nn(write, grad)[0:8]
        out[:, cols] = base_top[:, cols] + k[0:TAIL, cols].astype(f32)[0:8] * through
        dwrite = dwrite + nt(xs[0:TAIL, cols], grad)[0:8]
    slope = sbc[0:TAIL, :].astype(f32)[0:8]
    out[:, WIDE : WIDE + STATE] = dwrite * slope[:, :STATE]
    out[:, WIDE + STATE :] = dread[0:8, :] * slope[:, STATE:]


def join_kernel(v_own, s_own, t_own, message, e0, e1, v_tap, s_tap, v_out, s_out, t_out):
    core, ring = place()

    def place_in(out, own, arrived, width):
        out[:, pl.ds(pl.multiple_of(core * width, 128), width)] = own
        out[:, pl.ds(pl.multiple_of((1 - core) * width, 128), width)] = arrived

    def patch(out, tap, edge, width, group, start):
        cols = slice(group * width, (group + 1) * width)
        rows = edge[:, start : start + width]
        row = iota((TAIL, width), 0)
        acc = out[TOK - TAIL :, cols].astype(f32)
        for shift in range(1, CONV):
            j = CONV - 1 - shift
            for k in range(shift):
                acc = acc + jnp.where(
                    row == TAIL - shift + k, tap[j : j + 1, cols] * rows[k : k + 1], 0.0
                )
        out[TOK - TAIL :, cols] = acc.astype(bf16)

    place_in(v_out, v_own[...], message[:, :WIDE], WIDE)
    place_in(s_out, s_own[...], message[:, WIDE : WIDE + 2 * STATE], 2 * STATE)

    @pl.when(core == CORES - 1)
    def _():
        for group, edge in enumerate((e0, e1)):
            patch(v_out, v_tap, edge, WIDE, group, 0)
            patch(s_out, s_tap, edge, 2 * STATE, group, WIDE)

    own = t_own[...].astype(f32).T[:HEADS]
    arrived = message[:, WIDE + 2 * STATE :].astype(f32).T[:HEADS]
    low = jnp.where(core == 0, own, arrived)
    high = jnp.where(core == 0, arrived, own)
    t_out[...] = jnp.concatenate([low, high], axis=0).astype(bf16)


def call(kernel, args, outs, scratch=(), name=None, anywhere=(), cost=None):
    vmem = pl.BlockSpec(memory_space=pltpu.VMEM)
    args = [pltpu.with_memory_space_constraint(a, pltpu.HBM) if k in anywhere else a for k, a in enumerate(args)]
    return pl.pallas_call(
        kernel,
        in_specs=[
            pl.BlockSpec(memory_space=pltpu.HBM) if k in anywhere else vmem for k in range(len(args))
        ],
        out_specs=[vmem for _ in outs],
        out_shape=[jax.ShapeDtypeStruct(*o) for o in outs],
        scratch_shapes=[s if not isinstance(s, tuple) else pltpu.VMEM(*s) for s in scratch],
        compiler_params=pltpu.CompilerParams(vmem_limit_bytes=24 * 1024 * 1024),
        cost_estimate=None
        if cost is None
        else pl.CostEstimate(flops=0, transcendentals=0, bytes_accessed=int(cost * 3.0e6)),
        name=name,
    )(*args)


def local(
    value_input, state_input, step_raw, upstream, step_bias, decay_log, skip_gain,
    value_kernel, value_offset, state_kernel, state_offset,
):
    count = lax.axis_size("ctx")
    chips = count // CORES
    per_half = count // HALVES

    def send(x, pairs):
        return lax.ppermute(x, "ctx", pairs)

    swap_pairs = [(i, i ^ 1) for i in range(count)]

    def around(i, shift):
        half, at, c = i // (RING * CORES), (i // CORES) % RING, i % CORES
        return (half * RING + (at + shift) % RING) * CORES + c

    def exchange(parts, sign):
        out = [parts[0]]
        for k in range(1, RING):
            out.append(send(parts[k], [(i, around(i, sign * k)) for i in range(count)]))
        return out

    row = lambda x: x.reshape(1, -1)
    v, s, r, g = value_input[0], state_input[0], step_raw[0].T, upstream[0]
    bias, rate_log, skip = row(step_bias), row(decay_log), row(skip_gain)
    joint = WIDE + 2 * STATE + 128
    tall = (ROWS, WIDE)
    narrow = (ROWS, 128)
    marked = ((STATE + TAIL, PART), bf16)
    state_part = ((STATE, PART), bf16)
    sems = pltpu.SemaphoreType.DMA

    message, halo_a, halo_b = call(
        pack_kernel, [v, s, r],
        [((TOK, joint), bf16), ((TAIL, WIDE + 2 * STATE), bf16), ((TAIL, WIDE + 2 * STATE), bf16)],
        [sems((6,))], "pack", (0, 1),
    )
    message = send(message, swap_pairs)
    halo_a = send(halo_a, [(k * 2 + 1, k * 2 + 3) for k in range(chips - 1)])
    halo_b = send(halo_b, [(k * 2 + 1, k * 2 + 2) for k in range(chips - 1)])
    g_own, g_in = call(
        pack_grad_kernel, [g], [((TOK, WIDE), bf16)] * 2, [sems((2,))], "pack_grad", (0,)
    )
    g_own, g_in, message, halo_a, halo_b = lax.optimization_barrier(
        (g_own, g_in, message, halo_a, halo_b)
    )
    g_own = lax.ppermute(g_own, "pipe", [(0, 1), (1, 0)])
    g_in = lax.ppermute(
        g_in,
        ("pipe", "ctx"),
        [(p * count + i, (1 - p) * count + (i ^ 1)) for p in range(2) for i in range(count)],
    )
    ones = call(ones_kernel, [], [((128, WIDE), bf16)], name="ones")[0]
    (m0, m1, m2, m3, x, xs, sx, k, bc, sbc, delta, within, sig) = call(
        first_kernel,
        [v, s, r, message, halo_a, halo_b, bias, rate_log,
         value_kernel, row(value_offset), state_kernel, row(state_offset), ones],
        [marked] * 4 + [(tall, bf16)] * 4 + [((ROWS, 2 * STATE), bf16)] * 2 + [(narrow, f32)] * 3,
        [((ROWS + 8, WIDE), f32), ((ROWS + 8, 2 * STATE), f32), (narrow, f32), (tall, f32)],
        "first", cost=8,
    )
    marks = exchange((m0, m1, m2, m3), 1)
    d0, d1, d2, d3, dy, dye = call(
        second_kernel, [g_own, g_in, bc, within, ones],
        [state_part] * 4 + [(tall, bf16)] * 2, [(tall, f32)], "second", cost=4,
    )
    grads = exchange((d0, d1, d2, d3), 1)
    edge = call(
        functools.partial(edge_kernel, False), marks + marks, [state_part], (), "edge_forward",
        cost=2,
    )[0]
    edge_in = send(edge, [(i, i + per_half) for i in range(per_half)])
    half_wide = (ROWS, WIDE // 2)
    inner_scratch = [
        (half_wide, f32), ((8, WIDE // 2), f32), ((HEADS // 2, 8, ROWS), f32), ((128, ROWS), f32),
        ((ROWS, ROWS), f32),
    ]
    dy_now, _ = lax.optimization_barrier((dy, edge))
    base_0, dbcs, diff, vsum = call(
        functools.partial(inner_kernel, 0), [x, dy_now, bc, delta, within, sx, skip, ones],
        [(half_wide, f32), ((ROWS, ROWS), f32), (narrow, f32), (narrow, f32)],
        inner_scratch, "inner_0", cost=6,
    )
    edge_in, diff = lax.optimization_barrier((edge_in, diff))
    steps = call(
        functools.partial(scan_kernel, False), marks + marks + [edge_in],
        [state_part] * 4, (), "scan_forward", cost=3,
    )
    carried = exchange(steps, -1)
    edge_back = call(
        functools.partial(edge_kernel, True), marks + grads, [state_part], (), "edge_back", cost=2,
    )[0]
    edge_back = send(edge_back, [(i + per_half, i) for i in range(per_half)])
    steps_back = call(
        functools.partial(scan_kernel, True), marks + grads + [edge_back],
        [state_part] * 4, (), "scan_back", cost=3,
    )
    dy_now, _ = lax.optimization_barrier((dy, steps_back[0]))
    base_1, dbc, diff, vsum, base_top = call(
        functools.partial(inner_kernel, 1),
        [x, dy_now, bc, delta, within, sx, skip, ones, dbcs, diff, vsum, base_0],
        [(half_wide, f32), ((ROWS, 2 * STATE), f32), (narrow, f32), (narrow, f32),
         ((8, WIDE), f32)],
        inner_scratch + [((ROWS, ROWS), f32)], "inner_1", cost=6,
    )
    back = exchange(steps_back, -1)
    diff, dread, held = call(
        carry_kernel, list(carried) + [bc, dye, dbc, diff, ones],
        [(narrow, f32), ((ROWS, STATE), f32), ((STATE, WIDE), bf16)], (), "carry", cost=4,
    )
    head = call(
        head_kernel, list(back) + [bc, xs, k, base_top, sbc, dread, dbc],
        [((8, WIDE + 2 * STATE), f32)], (), "head", cost=1,
    )[0]
    back[0], head = lax.optimization_barrier((back[0], head))
    e0 = send(head, [(j * 2, j * 2 - 1) for j in range(1, chips)])
    e1 = send(head, [(j * 2 + 1, j * 2 - 1) for j in range(1, chips)])
    vg_own, sg_own, st_own, message = call(
        last_kernel,
        list(back)
        + [held, bc, xs, k, base_0, base_1, sbc, delta, within, sig, diff, vsum, dread, dbc,
           rate_log, value_kernel, state_kernel, ones],
        [((TOK, WIDE), bf16), ((TOK, 2 * STATE), bf16), ((TOK, 128), bf16),
         ((TOK, joint), bf16)],
        [((STATE, WIDE), bf16), ((ROWS + 8, WIDE), f32), ((ROWS + 8, 2 * STATE), f32),
         (narrow, f32), (tall, bf16), ((ROWS, 2 * STATE), bf16)],
        "last", cost=8,
    )
    message, e0, e1 = lax.optimization_barrier((message, e0, e1))
    message = send(message, swap_pairs)
    value_out, state_out, step_out = call(
        join_kernel,
        [vg_own, sg_own, st_own, message, e0, e1, value_kernel, state_kernel],
        [((TOK, 2 * WIDE), bf16), ((TOK, 4 * STATE), bf16), ((2 * HEADS, TOK), bf16)],
        (), "join",
    )
    return value_out[None], state_out[None], step_out.T[None]


def solution(mesh):
    wide = P("pipe", "ctx", "tp")
    placed = (wide, wide, wide, wide, P("tp"), P("tp"), P("tp"), P(None, "tp"), P("tp"), P(None, "tp"), P("tp"))
    return jax.shard_map(
        local, mesh=mesh, in_specs=placed, out_specs=(wide, wide, wide), check_vma=False
    )
```

```python
import functools

import jax
import jax.numpy as jnp
from jax import lax
from jax.experimental import pallas as pl
from jax.experimental.pallas import tpu as pltpu
from jax.sharding import PartitionSpec as P

HEAD_DIM = 64
STATE = 256
CONV = 4
CORES = 2
RING = 4
HALVES = 2
f32 = jnp.float32
bf16 = jnp.bfloat16
HIGH = lax.Precision.HIGHEST

TOK = 128
ROWS = TOK * CORES
HEADS = 32
WIDE = HEADS * HEAD_DIM
PART = WIDE // RING
TAIL = 16
HALO = 8
LOG2E = 1.4426950408889634


def place():
    index = lax.axis_index("ctx")
    return lax.rem(index, CORES), lax.rem(lax.div(index, CORES), RING)


def rows_of(core):
    return (
        pl.ds(pl.multiple_of(core * TOK, TOK), TOK),
        pl.ds(pl.multiple_of((1 - core) * TOK, TOK), TOK),
    )


def block128(b, start=0):
    return pl.ds(pl.multiple_of(start + b * 128, 128), 128)


def head_columns(ring, slot):
    return pl.ds(pl.multiple_of(lax.rem(ring + slot, RING) * PART, PART), PART)


def nn(a, b, precision=None):
    return lax.dot_general(
        a, b, (((1,), (0,)), ((), ())), precision=precision, preferred_element_type=f32
    )


def nt(a, b):
    return lax.dot_general(a, b, (((1,), (1,)), ((), ())), preferred_element_type=f32)


def iota(shape, axis):
    return lax.broadcasted_iota(jnp.int32, shape, axis)


def split3(x):
    high = x.astype(bf16).astype(f32)
    rest = x - high
    mid = rest.astype(bf16).astype(f32)
    low = rest - mid
    part = iota(x.shape, 1) // HEADS
    picked = jnp.where(part == 0, high, jnp.where(part == 1, mid, jnp.where(part == 2, low, 0.0)))
    return picked.astype(bf16)


def head_sum(x, ones):
    high = x.astype(bf16)
    low = (x - high.astype(f32)).astype(bf16)
    return nt(high, ones) + nt(low, ones)


def tiled_heads(x, group):
    x = x.astype(f32)
    mine = jnp.where(group == 0, x[:, :HEADS], x[:, HEADS:])
    return jnp.concatenate([mine] * 4, axis=1)


def tiled_steps(x, group):
    x = x.astype(f32)
    mine = jnp.where(group == 0, x[:HEADS], x[HEADS:])
    return jnp.concatenate([mine] * 4, axis=0).T


def softplus(x):
    u = jnp.exp(-jnp.abs(x))
    small = u * (1.0 - u * (0.5 - u * (1.0 / 3.0 - u * 0.25)))
    return jnp.maximum(x, 0.0) + jnp.where(u < 0.01, small, jnp.log(1.0 + u))


def sigmoid(x):
    return 1.0 / (1.0 + jnp.exp(-x))


def sigmoid_by_tanh(x):
    return 0.5 + 0.5 * jnp.tanh(0.5 * x)


def run_copies(pairs, sems):
    copies = [pltpu.make_async_copy(a, b, sems.at[k]) for k, (a, b) in enumerate(pairs)]
    for copy in copies:
        copy.start()
    return copies


def pack_kernel(v, s, r, message, halo_a, halo_b, halos, r_here, sems):
    core, ring = place()
    there = 1 - core
    pairs = []
    rows = pl.ds(TOK - HALO, HALO)
    for group, halo in ((1, halo_a), (0, halo_b)):
        pairs.append((v.at[rows, pl.ds(group * WIDE, WIDE)], halo.at[:, pl.ds(0, WIDE)]))
        pairs.append(
            (s.at[rows, pl.ds(group * 2 * STATE, 2 * STATE)], halo.at[:, pl.ds(WIDE, 2 * STATE)])
        )
    v_there = pl.ds(pl.multiple_of(there * WIDE, 128), WIDE)
    s_there = pl.ds(pl.multiple_of(there * 2 * STATE, 128), 2 * STATE)
    for k, group in enumerate((1, 0)):
        at = pl.ds(k * HALO, HALO)
        pairs.append((v.at[rows, pl.ds(group * WIDE, WIDE)], halos.at[at, pl.ds(0, WIDE)]))
        pairs.append(
            (s.at[rows, pl.ds(group * 2 * STATE, 2 * STATE)], halos.at[at, pl.ds(WIDE, 2 * STATE)])
        )
    pairs.append((v.at[:, v_there], message.at[:, pl.ds(0, WIDE)]))
    pairs.append((s.at[:, s_there], message.at[:, pl.ds(WIDE, 2 * STATE)]))
    pairs.append((r, r_here))
    copies = run_copies(pairs, sems)
    copies.pop().wait()
    message[:, WIDE + 2 * STATE :] = tiled_steps(r_here[...], there).astype(bf16)
    for copy in copies:
        copy.wait()


def relay_kernel(halo_a, halo_b, relayed, out_a, out_b):
    index = lax.axis_index("ctx")
    handing = index == CORES * RING - 1
    out_a[...] = jnp.where(
        handing, relayed[:HALO].astype(f32), halo_a[...].astype(f32)
    ).astype(bf16)
    out_b[...] = jnp.where(
        handing, relayed[HALO:].astype(f32), halo_b[...].astype(f32)
    ).astype(bf16)


def pack_grad_kernel(g, own, across, sems):
    core, ring = place()
    copies = [
        pltpu.make_async_copy(
            g.at[:, pl.ds(pl.multiple_of(group * WIDE, 128), WIDE)], out, sems.at[k]
        )
        for k, (group, out) in enumerate(((core, own), (1 - core, across)))
    ]
    for copy in copies:
        copy.start()
    for copy in copies:
        copy.wait()


def ones_kernel(out):
    rows = iota((128, WIDE), 0) % HEADS
    cols = iota((128, WIDE), 1) // HEAD_DIM
    out[...] = jnp.where(rows == cols, 1.0, 0.0).astype(bf16)


def first_kernel(
    v, s, r, message, halo_a, halo_b, step_bias, decay_log, v_tap, v_off, s_tap, s_off, ones,
    m0, m1, m2, m3, x_out, xs_out, bc_out, pre_out, spre_out, wide, delta_out, within_out, sig_out,
    buf, sbuf, raw,
):
    core, ring = place()
    mine, other = rows_of(core)
    raw[mine, :] = tiled_steps(r[...], core)
    raw[other, :] = message[:, WIDE + 2 * STATE :].astype(f32)
    pre = raw[...] + tiled_heads(step_bias[...], core)
    delta = softplus(pre)
    rate = -jnp.exp(tiled_heads(decay_log[...], core))
    lower = jnp.where(iota((ROWS, ROWS), 0) >= iota((ROWS, ROWS), 1), 1.0, 0.0).astype(f32)
    within = nn(lower, delta * rate, HIGH)
    delta_out[...] = delta
    within_out[...] = within
    sig_out[...] = sigmoid(pre)
    total = within[ROWS - 1 : ROWS, :]
    wide[...] = nn(split3(delta * jnp.exp(total - within)), ones[...])

    below = pl.ds(pl.multiple_of(8 + core * TOK, 8), TOK)
    above = pl.ds(pl.multiple_of(8 + (1 - core) * TOK, 8), TOK)
    v_mine = pl.ds(pl.multiple_of(core * WIDE, 128), WIDE)
    s_mine = pl.ds(pl.multiple_of(core * 2 * STATE, 128), 2 * STATE)
    buf[below, :] = v[:, v_mine].astype(f32)
    buf[above, :] = message[:, :WIDE].astype(f32)
    sbuf[below, :] = s[:, s_mine].astype(f32)
    sbuf[above, :] = message[:, WIDE : WIDE + 2 * STATE].astype(f32)
    halo = halo_a[...].astype(f32) + halo_b[...].astype(f32)
    buf[0:8, :] = halo[:, :WIDE]
    sbuf[0:8, :] = halo[:, WIDE:]

    def conv(source, tap, off, b, width):
        cols, par = block128(b), block128(b, core * width)
        acc = off[:, par] + tap[0:1, par] * source[5 : 5 + ROWS, cols]
        for j in range(1, CONV):
            acc = acc + tap[j : j + 1, par] * source[5 + j : 5 + j + ROWS, cols]
        return acc

    def state_block(b, carry):
        cols = block128(b)
        acc = conv(sbuf, s_tap, s_off, b, 2 * STATE)
        spre_out[:, cols] = acc
        bc_out[:, cols] = (acc * sigmoid_by_tanh(acc)).astype(bf16)
        return carry

    lax.fori_loop(0, 4, state_block, 0)

    def value_block(b, carry):
        cols = block128(b)
        acc = conv(buf, v_tap, v_off, b, WIDE)
        pre_out[:, cols] = acc
        post = (acc * sigmoid_by_tanh(acc)).astype(bf16)
        x_out[:, cols] = post
        xs_out[:, cols] = (post.astype(f32) * wide[:, cols]).astype(bf16)
        return carry

    lax.fori_loop(0, 16, value_block, 0)

    write_t = bc_out[:, :STATE].astype(f32).T.astype(bf16)
    total_parts = split3(jnp.broadcast_to(total, (8, 128)))
    for slot, out in enumerate((m0, m1, m2, m3)):
        cols = head_columns(ring, slot)
        out[0:STATE, :] = nn(write_t, xs_out[:, cols]).astype(bf16)
        full = nn(total_parts, ones[:, cols])[0:1, :]
        high = full.astype(bf16).astype(f32)
        mid = (full - high).astype(bf16).astype(f32)
        low = full - high - mid
        row = iota((TAIL, PART), 0)
        out[STATE : STATE + TAIL, :] = jnp.where(
            row == 0, high, jnp.where(row == 1, mid, jnp.where(row == 2, low, 0.0))
        ).astype(bf16)


def slope_kernel(pre, spre, wide, sx_out, k_out, sbc_out):
    def slope(acc):
        sig = sigmoid_by_tanh(acc)
        return sig * (1.0 + acc * (1.0 - sig))

    def value_block(b, carry):
        cols = block128(b)
        out = slope(pre[:, cols])
        sx_out[:, cols] = out.astype(bf16)
        k_out[:, cols] = (out * wide[:, cols]).astype(bf16)
        return carry

    lax.fori_loop(0, 16, value_block, 0)

    def state_block(b, carry):
        cols = block128(b)
        sbc_out[:, cols] = slope(spre[:, cols]).astype(bf16)
        return carry

    lax.fori_loop(0, 4, state_block, 0)


def ring_totals(parts):
    out = []
    for part in parts:
        rows = part[STATE : STATE + TAIL, :].astype(f32)
        out.append(rows[0:1] + rows[1:2] + rows[2:3])
    return out


def between(totals, places, low, high):
    out = jnp.zeros_like(totals[0])
    for total, p in zip(totals, places):
        inside = jnp.logical_and(p > low, p < high)
        out = out + total * jnp.where(inside, 1.0, 0.0)
    return out


def edge_kernel(back, m0, m1, m2, m3, d0, d1, d2, d3, out):
    core, ring = place()
    places = [lax.rem(ring + RING - s, RING) for s in range(RING)]
    totals = ring_totals((m0, m1, m2, m3))
    weights = []
    for p in places:
        low, high = (-1, p) if back else (p, RING)
        weights.append(jnp.exp(between(totals, places, low, high)))
    for c in range(0, PART, 128):
        cols = slice(c, c + 128)
        acc = None
        for src, weight in zip((d0, d1, d2, d3), weights):
            term = weight[:, cols] * src[0:STATE, cols].astype(f32)
            acc = term if acc is None else acc + term
        out[:, cols] = acc.astype(bf16)


def scan_kernel(back, m0, m1, m2, m3, d0, d1, d2, d3, edge, o0, o1, o2, o3):
    core, ring = place()
    places = [lax.rem(ring + RING - s, RING) for s in range(RING)]
    totals = ring_totals((m0, m1, m2, m3))
    weights = []
    for here in places:
        low, high = (here, RING) if back else (-1, here)
        row = [jnp.exp(between(totals, places, low, high))]
        for p in places:
            low, high, live = (here, p, p > here) if back else (p, here, p < here)
            row.append(jnp.exp(between(totals, places, low, high)) * jnp.where(live, 1.0, 0.0))
        weights.append(row)
    for c in range(0, PART, 128):
        cols = slice(c, c + 128)
        for r in range(0, STATE, 64):
            rows = slice(r, r + 64)
            parts = [edge[rows, cols].astype(f32)]
            parts += [src[rows, cols].astype(f32) for src in (d0, d1, d2, d3)]
            for out, row in zip((o0, o1, o2, o3), weights):
                acc = row[0][:, cols] * parts[0]
                for weight, part in zip(row[1:], parts[1:]):
                    acc = acc + weight[:, cols] * part
                out[rows, cols] = acc.astype(bf16)


def second_kernel(g_own, g_in, bc, within, ones, d0, d1, d2, d3, dy_out, dye_out, wide):
    core, ring = place()
    mine, other = rows_of(core)
    dy_out[mine, :] = g_own[...]
    dy_out[other, :] = g_in[...]
    wide[...] = nn(split3(jnp.exp(within[...])), ones[...])
    read_t = bc[:, STATE:].astype(f32).T.astype(bf16)

    def block(b, carry):
        cols = block128(b)
        dye_out[:, cols] = (dy_out[:, cols].astype(f32) * wide[:, cols]).astype(bf16)
        return carry

    lax.fori_loop(0, 16, block, 0)
    for slot, out in enumerate((d0, d1, d2, d3)):
        out[...] = nn(read_t, dye_out[:, head_columns(ring, slot)]).astype(bf16)


def inner_kernel(part, x, dy, bc, delta, within, sx, skip_gain, ones, *refs):
    if part == 0:
        base_out, dbcs, diff_out, vsum_out = refs[:4]
        scratch = refs[4:]
    else:
        dbcs_in, diff_in, vsum_in, base_in = refs[:4]
        base_out, dbc_out, diff_out, vsum_out, top_out = refs[4:9]
        scratch = refs[9:]
        dbcs = scratch[-1]
    wide, skips, within_3, row_sum, bcs = scratch[:5]
    core, ring = place()
    half = ROWS // 2
    low_col, low_head = part * (WIDE // 2), part * (HEADS // 2)
    own = ones[:, low_col : low_col + WIDE // 2]
    wide[...] = nn(split3(delta[...]), own)
    skip = jnp.broadcast_to(tiled_heads(skip_gain[...], core), (8, 128))
    skips[...] = nn(split3(skip), own)
    scaled = within[...] * LOG2E
    lane_part = iota((ROWS, 128), 1) // HEADS
    left = jnp.where(lane_part == 3, 1.0, -split3(scaled).astype(f32)).astype(bf16)
    parts_t = split3(scaled).astype(f32).T
    for h in range(HEADS // 2):
        for piece in range(3):
            at = piece * HEADS + low_head + h
            within_3[h, piece : piece + 1, :] = parts_t[at : at + 1, :]
        within_3[h, 3:8, :] = jnp.zeros((5, ROWS), f32)
    write, read = bc[:, :STATE], bc[:, STATE:]
    bcs[...] = nt(write, read)
    if part == 0:
        dbcs[...] = jnp.zeros_like(dbcs)
        diff_out[...] = jnp.zeros_like(diff_out)
        vsum_out[...] = jnp.zeros_like(vsum_out)
    else:
        dbcs[...] = dbcs_in[...]
        diff_out[...] = diff_in[...]
        vsum_out[...] = vsum_in[...]
    row_sum[...] = jnp.zeros_like(row_sum)
    keep = iota((half, half), 1) >= iota((half, half), 0)
    lanes = iota((ROWS, 128), 1)
    first = lanes < HEAD_DIM
    row_head = iota((96, ROWS), 0) % HEADS
    pad = jnp.zeros((24, ROWS), f32)

    def pair(b, carry):
        cols, here = block128(b, low_col), block128(b)
        xb = x[:, cols].astype(f32)
        xd = (xb * wide[:, here]).astype(bf16)
        grad = dy[:, cols]
        zero = jnp.zeros_like(grad)
        top = jnp.zeros((half, 128), f32)
        bot = jnp.zeros((half, 128), f32)
        col_total = jnp.zeros((ROWS, 128), f32)
        grads_of = [0.0, 0.0, 0.0]
        for e in range(2):
            h = low_head + 2 * b + e
            g = jnp.where(first, grad, zero) if e == 0 else jnp.where(first, zero, grad)
            right = jnp.concatenate(
                [jnp.where(row_head == h, 1.0, 0.0), within_3[2 * b + e], pad], axis=0
            ).astype(bf16)
            gap0 = nn(left[:half], right)
            gap1 = nn(left[half:], right[:, half:])
            dm0 = nt(xd[:half], g)
            dm1 = nt(xd[half:], g[half:])
            blocks = (
                (jnp.where(keep, gap0[:, :half], -jnp.inf), dm0[:, :half], 0, 0),
                (gap0[:, half:], dm0[:, half:], 0, 1),
                (jnp.where(keep, gap1, -jnp.inf), dm1, 1, 1),
            )
            ps, ms = [], []
            for k, (gap, dm, r, c) in enumerate(blocks):
                decay = jnp.exp2(gap)
                m = decay * bcs[r * half : (r + 1) * half, c * half : (c + 1) * half]
                grads_of[k] = grads_of[k] + dm * decay
                ps.append(dm * m)
                ms.append(m.astype(bf16))
            sum_rows = jnp.concatenate(
                [
                    jnp.sum(ps[0], axis=0, keepdims=True),
                    jnp.sum(ps[1] + ps[2], axis=0, keepdims=True),
                ],
                axis=1,
            )
            row_sum[pl.ds(h, 1), :] = sum_rows
            top = top + nn(ms[0], g[:half]) + nn(ms[1], g[half:])
            bot = bot + nn(ms[2], g[half:])
            col = jnp.concatenate(
                [
                    jnp.sum(ps[0] + ps[1], axis=1, keepdims=True),
                    jnp.sum(ps[2], axis=1, keepdims=True),
                ],
                axis=0,
            )
            col_total = col_total + jnp.where(lanes % HEADS == h, col, 0.0)
        for k, (r, c) in enumerate(((0, 0), (0, 1), (1, 1))):
            rs, cs = slice(r * half, (r + 1) * half), slice(c * half, (c + 1) * half)
            dbcs[rs, cs] = dbcs[rs, cs] + grads_of[k]
        u = jnp.concatenate([top, bot], axis=0)
        diff_out[...] = diff_out[...] - col_total
        vsum_out[...] = vsum_out[...] + head_sum(xb * u, ones[:, cols])
        base_out[:, here] = (
            wide[:, here] * u + skips[0:1, here] * grad.astype(f32)
        ) * sx[:, cols].astype(f32)
        return carry

    lax.fori_loop(0, 8, pair, 0)
    for t in range(1, 4):
        row_sum[t * HEADS : (t + 1) * HEADS, :] = row_sum[0:HEADS, :]
    diff_out[...] = diff_out[...] + row_sum[...].T
    if part == 1:
        grad = dbcs[...]
        dbc_out[:, :STATE] = nn(grad.astype(bf16), read)
        dbc_out[:, STATE:] = nn(grad.T.astype(bf16), write)
        top_out[:, : WIDE // 2] = base_in[0:8, :]
        top_out[:, WIDE // 2 :] = base_out[0:8, :]


def carry_kernel(c0, c1, c2, c3, bc, dye, dbc, diff, ones, diff_out, dread_out, carried_out):
    core, ring = place()
    for slot, src in enumerate((c0, c1, c2, c3)):
        carried_out[:, head_columns(ring, slot)] = src[...]
    read = bc[:, STATE:]
    dread_out[...] = dbc[:, STATE:] + nt(dye[...], carried_out[...])
    outer = diff[...]
    for b in range(4):
        cols = slice(b * PART, (b + 1) * PART)
        part = nn(read, carried_out[:, cols]) * dye[:, cols].astype(f32)
        outer = outer + head_sum(part, ones[:, cols])
    diff_out[...] = outer


def last_kernel(
    g0, g1, g2, g3, carried, bc, xs, k, base_0, base_1, sbc, delta, within, sig, diff, vsum,
    dread, dbc, decay_log, ones,
    e_out, es_out, steps_out,
    gbuf,
):
    core, ring = place()
    for slot, src in enumerate((g0, g1, g2, g3)):
        gbuf[:, head_columns(ring, slot)] = src[...]
    write = bc[:, :STATE]
    rsum = jnp.zeros((ROWS, 128), f32)
    tsum = jnp.zeros((8, 128), f32)
    for b in range(4):
        cols = slice(b * PART, (b + 1) * PART)
        grad = gbuf[:, cols]
        through = nn(write, grad)
        rsum = rsum + head_sum(xs[:, cols].astype(f32) * through, ones[:, cols])
        base = (base_0, base_1)[b // 2][:, (b % 2) * PART : (b % 2 + 1) * PART]
        e_out[:, cols] = base + k[:, cols].astype(f32) * through
        both = jnp.sum(
            grad.astype(f32) * carried[:, cols].astype(f32), axis=0, keepdims=True
        )
        tsum = tsum + head_sum(jnp.broadcast_to(both, (8, PART)), ones[:, cols])
    total = within[ROWS - 1 : ROWS, :]
    dtotal = tsum[0:1, :] * jnp.exp(total)
    ra, rb = iota((ROWS, ROWS), 0), iota((ROWS, ROWS), 1)
    later = jnp.where(rb >= ra, 1.0, 0.0).astype(f32)
    earlier = jnp.where(rb < ra, 1.0, 0.0).astype(f32)
    da = nn(later, diff[...], HIGH) + nn(earlier, rsum, HIGH) + dtotal
    rate = -jnp.exp(tiled_heads(decay_log[...], core))
    steps_out[...] = (vsum[...] + rsum / delta[...] + rate * da) * sig[...]
    dwrite = dbc[:, :STATE] + nt(xs[...], gbuf[...])
    es_out[:, :STATE] = dwrite * sbc[:, :STATE].astype(f32)
    es_out[:, STATE:] = dread[...] * sbc[:, STATE:].astype(f32)


def back_kernel(
    e, es, steps, head, v_tap, s_tap, vg_own, sg_own, st_own, message, back, sback
):
    core, ring = place()
    mine, other = rows_of(core)
    body = ROWS - TAIL

    def conv(source, start, tap, b, width, out):
        cols, par = block128(b), block128(b, core * width)
        edge = jnp.concatenate(
            [source[body:, cols], head[:, block128(b, start)].astype(f32)], axis=0
        )
        acc = tap[CONV - 1 : CONV, par] * source[0:body, cols]
        end = tap[CONV - 1 : CONV, par] * edge[0:TAIL]
        for shift in range(1, CONV):
            weight = tap[CONV - 1 - shift : CONV - shift, par]
            acc = acc + weight * source[shift : shift + body, cols]
            end = end + weight * edge[shift : shift + TAIL]
        out[0:body, cols] = acc.astype(bf16)
        out[body:, cols] = end.astype(bf16)

    def value_block(b, carry):
        conv(e, 0, v_tap, b, WIDE, back)
        return carry

    lax.fori_loop(0, 16, value_block, 0)

    def state_block(b, carry):
        conv(es, WIDE, s_tap, b, 2 * STATE, sback)
        return carry

    lax.fori_loop(0, 4, state_block, 0)
    vg_own[...] = back[mine, :]
    message[:, :WIDE] = back[other, :]
    sg_own[...] = sback[mine, :]
    message[:, WIDE : WIDE + 2 * STATE] = sback[other, :]
    st_own[...] = steps[mine, :].astype(bf16)
    message[:, WIDE + 2 * STATE :] = steps[other, :].astype(bf16)


def head_kernel(g0, g1, g2, g3, bc, xs, k, base_top, sbc, dread, dbc, out):
    core, ring = place()
    write = bc[0:TAIL, :STATE]
    dwrite = dbc[0:8, :STATE]
    for slot, src in enumerate((g0, g1, g2, g3)):
        cols = head_columns(ring, slot)
        grad = src[...]
        through = nn(write, grad)[0:8]
        out[:, cols] = (
            base_top[:, cols] + k[0:TAIL, cols].astype(f32)[0:8] * through
        ).astype(bf16)
        dwrite = dwrite + nt(xs[0:TAIL, cols], grad)[0:8]
    slope = sbc[0:TAIL, :].astype(f32)[0:8]
    out[:, WIDE : WIDE + STATE] = (dwrite * slope[:, :STATE]).astype(bf16)
    out[:, WIDE + STATE :] = (dread[0:8, :] * slope[:, STATE:]).astype(bf16)


def join_kernel(v_own, s_own, t_own, message, v_out, s_out, t_out):
    core, ring = place()

    def place_in(out, own, arrived, width):
        out[:, pl.ds(pl.multiple_of(core * width, 128), width)] = own
        out[:, pl.ds(pl.multiple_of((1 - core) * width, 128), width)] = arrived

    place_in(v_out, v_own[...], message[:, :WIDE], WIDE)
    place_in(s_out, s_own[...], message[:, WIDE : WIDE + 2 * STATE], 2 * STATE)
    own = t_own[...].astype(f32).T[:HEADS]
    arrived = message[:, WIDE + 2 * STATE :].astype(f32).T[:HEADS]
    low = jnp.where(core == 0, own, arrived)
    high = jnp.where(core == 0, arrived, own)
    t_out[...] = jnp.concatenate([low, high], axis=0).astype(bf16)


def call(kernel, args, outs, scratch=(), name=None, anywhere=(), cost=None):
    vmem = pl.BlockSpec(memory_space=pltpu.VMEM)
    args = [pltpu.with_memory_space_constraint(a, pltpu.HBM) if k in anywhere else a for k, a in enumerate(args)]
    return pl.pallas_call(
        kernel,
        in_specs=[
            pl.BlockSpec(memory_space=pltpu.HBM) if k in anywhere else vmem for k in range(len(args))
        ],
        out_specs=[vmem for _ in outs],
        out_shape=[jax.ShapeDtypeStruct(*o) for o in outs],
        scratch_shapes=[s if not isinstance(s, tuple) else pltpu.VMEM(*s) for s in scratch],
        compiler_params=pltpu.CompilerParams(vmem_limit_bytes=24 * 1024 * 1024),
        cost_estimate=None
        if cost is None
        else pl.CostEstimate(flops=0, transcendentals=0, bytes_accessed=int(cost * 3.0e6)),
        name=name,
    )(*args)


def local(
    value_input, state_input, step_raw, upstream, step_bias, decay_log, skip_gain,
    value_kernel, value_offset, state_kernel, state_offset,
):
    count = lax.axis_size("ctx")
    chips = count // CORES
    per_half = count // HALVES

    def send(x, pairs):
        return lax.ppermute(x, "ctx", pairs)

    swap_pairs = [(i, i ^ 1) for i in range(count)]

    def around(i, shift):
        half, at, c = i // (RING * CORES), (i // CORES) % RING, i % CORES
        return (half * RING + (at + shift) % RING) * CORES + c

    def exchange(parts, sign):
        out = list(parts)
        for k in (2, 1, 3):
            out[k] = send(parts[k], [(i, around(i, sign * k)) for i in range(count)])
        return out

    row = lambda x: x.reshape(1, -1)
    v, s, r, g = value_input[0], state_input[0], step_raw[0].T, upstream[0]
    bias, rate_log, skip = row(step_bias), row(decay_log), row(skip_gain)
    joint = WIDE + 2 * STATE + 128
    tall = (ROWS, WIDE)
    narrow = (ROWS, 128)
    marked = ((STATE + TAIL, PART), bf16)
    state_part = ((STATE, PART), bf16)
    sems = pltpu.SemaphoreType.DMA

    message, halo_a, halo_b, halos = call(
        pack_kernel, [v, s, r],
        [((TOK, joint), bf16), ((HALO, WIDE + 2 * STATE), bf16), ((HALO, WIDE + 2 * STATE), bf16),
         ((2 * HALO, WIDE + 2 * STATE), bf16)],
        [((2 * HEADS, TOK), bf16), sems((11,))], "pack", (0, 1, 2),
    )
    middle = per_half - 1
    relayed = lax.ppermute(
        halos, ("pipe", "ctx"),
        [(p * count + middle, (1 - p) * count + middle) for p in range(2)],
    )
    message = send(message, swap_pairs)
    halo_a, halo_b = call(
        relay_kernel, [halo_a, halo_b, relayed], [((HALO, WIDE + 2 * STATE), bf16)] * 2, (), "relay"
    )

    def onward(x, step):
        pairs = []
        for p in range(2):
            for k in range(chips - 1):
                source = k * CORES + 1
                held = 1 - p if source == middle else p
                pairs.append((held * count + source, p * count + source + step))
        return lax.ppermute(x, ("pipe", "ctx"), pairs)

    g_own, g_in = call(
        pack_grad_kernel, [g], [((TOK, WIDE), bf16)] * 2, [sems((2,))], "pack_grad", (0,)
    )
    g_own, g_in, halo_a, halo_b = lax.optimization_barrier((g_own, g_in, halo_a, halo_b))
    halo_a = onward(halo_a, 2)
    halo_b = onward(halo_b, 1)
    g_own = lax.ppermute(g_own, "pipe", [(0, 1), (1, 0)])
    g_in = lax.ppermute(
        g_in,
        ("pipe", "ctx"),
        [(p * count + i, (1 - p) * count + (i ^ 1)) for p in range(2) for i in range(count)],
    )
    ones = call(ones_kernel, [], [((128, WIDE), bf16)], name="ones")[0]
    (m0, m1, m2, m3, x, xs, bc, pre, spre, spread_scale, delta, within, sig) = call(
        first_kernel,
        [v, s, r, message, halo_a, halo_b, bias, rate_log,
         value_kernel, row(value_offset), state_kernel, row(state_offset), ones],
        [marked] * 4 + [(tall, bf16)] * 2
        + [((ROWS, 2 * STATE), bf16), (tall, f32), ((ROWS, 2 * STATE), f32), (tall, f32)]
        + [(narrow, f32)] * 3,
        [((ROWS + 8, WIDE), f32), ((ROWS + 8, 2 * STATE), f32), (narrow, f32)],
        "first", cost=8,
    )
    marks = exchange((m0, m1, m2, m3), 1)
    sx, k, sbc = call(
        slope_kernel, [pre, spre, spread_scale],
        [(tall, bf16), (tall, bf16), ((ROWS, 2 * STATE), bf16)], (), "slopes", cost=2,
    )
    g_own, sx = lax.optimization_barrier((g_own, sx))
    d0, d1, d2, d3, dy, dye = call(
        second_kernel, [g_own, g_in, bc, within, ones],
        [state_part] * 4 + [(tall, bf16)] * 2, [(tall, f32)], "second", cost=4,
    )
    grads = exchange((d0, d1, d2, d3), 1)
    edge = call(
        functools.partial(edge_kernel, False), marks + marks, [state_part], (), "edge_forward",
        cost=2,
    )[0]
    edge_in = send(edge, [(i, i + per_half) for i in range(per_half)])
    half_wide = (ROWS, WIDE // 2)
    inner_scratch = [
        (half_wide, f32), ((8, WIDE // 2), f32), ((HEADS // 2, 8, ROWS), f32), ((128, ROWS), f32),
        ((ROWS, ROWS), f32),
    ]
    dy_now, _ = lax.optimization_barrier((dy, edge))
    base_0, dbcs, diff, vsum = call(
        functools.partial(inner_kernel, 0), [x, dy_now, bc, delta, within, sx, skip, ones],
        [(half_wide, f32), ((ROWS, ROWS), f32), (narrow, f32), (narrow, f32)],
        inner_scratch, "inner_0", cost=6,
    )
    edge_in, diff = lax.optimization_barrier((edge_in, diff))
    steps = call(
        functools.partial(scan_kernel, False), marks + marks + [edge_in],
        [state_part] * 4, (), "scan_forward", cost=3,
    )
    carried = exchange(steps, -1)
    *grads, _ = lax.optimization_barrier((*grads, base_0))
    edge_back = call(
        functools.partial(edge_kernel, True), marks + grads, [state_part], (), "edge_back", cost=2,
    )[0]
    edge_back = send(edge_back, [(i + per_half, i) for i in range(per_half)])
    steps_back = call(
        functools.partial(scan_kernel, True), marks + grads + [edge_back],
        [state_part] * 4, (), "scan_back", cost=3,
    )
    dy_now, _ = lax.optimization_barrier((dy, steps_back[0]))
    base_1, dbc, diff, vsum, base_top = call(
        functools.partial(inner_kernel, 1),
        [x, dy_now, bc, delta, within, sx, skip, ones, dbcs, diff, vsum, base_0],
        [(half_wide, f32), ((ROWS, 2 * STATE), f32), (narrow, f32), (narrow, f32),
         ((8, WIDE), f32)],
        inner_scratch + [((ROWS, ROWS), f32)], "inner_1", cost=6,
    )
    back = exchange(steps_back, -1)
    diff, dread, held = call(
        carry_kernel, list(carried) + [bc, dye, dbc, diff, ones],
        [(narrow, f32), ((ROWS, STATE), f32), ((STATE, WIDE), bf16)], (), "carry", cost=4,
    )
    head = call(
        head_kernel, list(back) + [bc, xs, k, base_top, sbc, dread, dbc],
        [((8, WIDE + 2 * STATE), bf16)], (), "head", cost=1,
    )[0]
    back[0], head = lax.optimization_barrier((back[0], head))
    head = send(head, [(i, i - CORES) for i in range(CORES, count)])
    e, es, steps = call(
        last_kernel,
        list(back)
        + [held, bc, xs, k, base_0, base_1, sbc, delta, within, sig, diff, vsum, dread, dbc,
           rate_log, ones],
        [(tall, f32), ((ROWS, 2 * STATE), f32), (narrow, f32)],
        [((STATE, WIDE), bf16)], "last", cost=5,
    )
    vg_own, sg_own, st_own, message = call(
        back_kernel, [e, es, steps, head, value_kernel, state_kernel],
        [((TOK, WIDE), bf16), ((TOK, 2 * STATE), bf16), ((TOK, 128), bf16),
         ((TOK, joint), bf16)],
        [(tall, bf16), ((ROWS, 2 * STATE), bf16)], "back", cost=3,
    )
    message = send(message, swap_pairs)
    value_out, state_out, step_out = call(
        join_kernel, [vg_own, sg_own, st_own, message],
        [((TOK, 2 * WIDE), bf16), ((TOK, 4 * STATE), bf16), ((2 * HEADS, TOK), bf16)],
        (), "join",
    )
    return value_out[None], state_out[None], step_out.T[None]


def solution(mesh):
    wide = P("pipe", "ctx", "tp")
    placed = (wide, wide, wide, wide, P("tp"), P("tp"), P("tp"), P(None, "tp"), P("tp"), P(None, "tp"), P("tp"))
    return jax.shard_map(
        local, mesh=mesh, in_specs=placed, out_specs=(wide, wide, wide), check_vma=False
    )
```

```python
import functools

import jax
import jax.numpy as jnp
from jax import lax
from jax.experimental import pallas as pl
from jax.experimental.pallas import tpu as pltpu
from jax.sharding import PartitionSpec as P

HEAD_DIM = 64
STATE = 256
CONV = 4
CORES = 2
RING = 4
HALVES = 2
f32 = jnp.float32
bf16 = jnp.bfloat16
HIGH = lax.Precision.HIGHEST

TOK = 128
ROWS = TOK * CORES
HEADS = 32
WIDE = HEADS * HEAD_DIM
PART = WIDE // RING
TAIL = 16
HALO = 8
LOG2E = 1.4426950408889634


def place():
    index = lax.axis_index("ctx")
    return lax.rem(index, CORES), lax.rem(lax.div(index, CORES), RING)


def rows_of(core):
    return (
        pl.ds(pl.multiple_of(core * TOK, TOK), TOK),
        pl.ds(pl.multiple_of((1 - core) * TOK, TOK), TOK),
    )


def block128(b, start=0):
    return pl.ds(pl.multiple_of(start + b * 128, 128), 128)


def head_columns(ring, slot):
    return pl.ds(pl.multiple_of(lax.rem(ring + slot, RING) * PART, PART), PART)


def nn(a, b, precision=None):
    return lax.dot_general(
        a, b, (((1,), (0,)), ((), ())), precision=precision, preferred_element_type=f32
    )


def nt(a, b):
    return lax.dot_general(a, b, (((1,), (1,)), ((), ())), preferred_element_type=f32)


def iota(shape, axis):
    return lax.broadcasted_iota(jnp.int32, shape, axis)


def split3(x):
    high = x.astype(bf16).astype(f32)
    rest = x - high
    mid = rest.astype(bf16).astype(f32)
    low = rest - mid
    part = iota(x.shape, 1) // HEADS
    picked = jnp.where(part == 0, high, jnp.where(part == 1, mid, jnp.where(part == 2, low, 0.0)))
    return picked.astype(bf16)


def head_sum(x, ones):
    high = x.astype(bf16)
    low = (x - high.astype(f32)).astype(bf16)
    return nt(high, ones) + nt(low, ones)


def tiled_heads(x, group):
    x = x.astype(f32)
    mine = jnp.where(group == 0, x[:, :HEADS], x[:, HEADS:])
    return jnp.concatenate([mine] * 4, axis=1)


def tiled_steps(x, group):
    x = x.astype(f32)
    mine = jnp.where(group == 0, x[:HEADS], x[HEADS:])
    return jnp.concatenate([mine] * 4, axis=0).T


def softplus(x):
    u = jnp.exp(-jnp.abs(x))
    small = u * (1.0 - u * (0.5 - u * (1.0 / 3.0 - u * 0.25)))
    return jnp.maximum(x, 0.0) + jnp.where(u < 0.01, small, jnp.log(1.0 + u))


def sigmoid(x):
    return 1.0 / (1.0 + jnp.exp(-x))


def sigmoid_by_tanh(x):
    return 0.5 + 0.5 * jnp.tanh(0.5 * x)


def run_copies(pairs, sems):
    copies = [pltpu.make_async_copy(a, b, sems.at[k]) for k, (a, b) in enumerate(pairs)]
    for copy in copies:
        copy.start()
    return copies


def pack_kernel(v, s, r, message, halo_a, halo_b, halos, r_here, sems):
    core, ring = place()
    there = 1 - core
    pairs = []
    rows = pl.ds(TOK - HALO, HALO)
    for group, halo in ((1, halo_a), (0, halo_b)):
        pairs.append((v.at[rows, pl.ds(group * WIDE, WIDE)], halo.at[:, pl.ds(0, WIDE)]))
        pairs.append(
            (s.at[rows, pl.ds(group * 2 * STATE, 2 * STATE)], halo.at[:, pl.ds(WIDE, 2 * STATE)])
        )
    v_there = pl.ds(pl.multiple_of(there * WIDE, 128), WIDE)
    s_there = pl.ds(pl.multiple_of(there * 2 * STATE, 128), 2 * STATE)
    for k, group in enumerate((1, 0)):
        at = pl.ds(k * HALO, HALO)
        pairs.append((v.at[rows, pl.ds(group * WIDE, WIDE)], halos.at[at, pl.ds(0, WIDE)]))
        pairs.append(
            (s.at[rows, pl.ds(group * 2 * STATE, 2 * STATE)], halos.at[at, pl.ds(WIDE, 2 * STATE)])
        )
    pairs.append((v.at[:, v_there], message.at[:, pl.ds(0, WIDE)]))
    pairs.append((s.at[:, s_there], message.at[:, pl.ds(WIDE, 2 * STATE)]))
    pairs.append((r, r_here))
    copies = run_copies(pairs, sems)
    copies.pop().wait()
    message[:, WIDE + 2 * STATE :] = tiled_steps(r_here[...], there).astype(bf16)
    for copy in copies:
        copy.wait()


def relay_kernel(halo_a, halo_b, relayed, out_a, out_b):
    index = lax.axis_index("ctx")
    handing = index == CORES * RING - 1
    out_a[...] = jnp.where(
        handing, relayed[:HALO].astype(f32), halo_a[...].astype(f32)
    ).astype(bf16)
    out_b[...] = jnp.where(
        handing, relayed[HALO:].astype(f32), halo_b[...].astype(f32)
    ).astype(bf16)


def pack_grad_kernel(g, own, across, sems):
    core, ring = place()
    copies = [
        pltpu.make_async_copy(
            g.at[:, pl.ds(pl.multiple_of(group * WIDE, 128), WIDE)], out, sems.at[k]
        )
        for k, (group, out) in enumerate(((core, own), (1 - core, across)))
    ]
    for copy in copies:
        copy.start()
    for copy in copies:
        copy.wait()


def ones_kernel(out):
    rows = iota((128, WIDE), 0) % HEADS
    cols = iota((128, WIDE), 1) // HEAD_DIM
    out[...] = jnp.where(rows == cols, 1.0, 0.0).astype(bf16)


def first_kernel(
    v, s, r, message, step_bias, decay_log, v_tap, v_off, s_tap, s_off, ones,
    x_out, xs_out, bc_out, pre_out, spre_out, wide, delta_out, within_out, sig_out, top_out,
    stop_out,
    buf, sbuf, raw,
):
    core, ring = place()
    mine, other = rows_of(core)
    raw[mine, :] = tiled_steps(r[...], core)
    raw[other, :] = message[:, WIDE + 2 * STATE :].astype(f32)
    pre = raw[...] + tiled_heads(step_bias[...], core)
    delta = softplus(pre)
    rate = -jnp.exp(tiled_heads(decay_log[...], core))
    lower = jnp.where(iota((ROWS, ROWS), 0) >= iota((ROWS, ROWS), 1), 1.0, 0.0).astype(f32)
    within = nn(lower, delta * rate, HIGH)
    delta_out[...] = delta
    within_out[...] = within
    sig_out[...] = sigmoid(pre)
    total = within[ROWS - 1 : ROWS, :]
    wide[...] = nn(split3(delta * jnp.exp(total - within)), ones[...])

    below = pl.ds(pl.multiple_of(8 + core * TOK, 8), TOK)
    above = pl.ds(pl.multiple_of(8 + (1 - core) * TOK, 8), TOK)
    v_mine = pl.ds(pl.multiple_of(core * WIDE, 128), WIDE)
    s_mine = pl.ds(pl.multiple_of(core * 2 * STATE, 128), 2 * STATE)
    buf[below, :] = v[:, v_mine].astype(f32)
    buf[above, :] = message[:, :WIDE].astype(f32)
    sbuf[below, :] = s[:, s_mine].astype(f32)
    sbuf[above, :] = message[:, WIDE : WIDE + 2 * STATE].astype(f32)
    buf[0:8, :] = jnp.zeros((8, WIDE), f32)
    sbuf[0:8, :] = jnp.zeros((8, 2 * STATE), f32)
    top_out[...] = buf[8 : 8 + TAIL, :]
    stop_out[...] = sbuf[8 : 8 + TAIL, :]

    def conv(source, tap, off, b, width):
        cols, par = block128(b), block128(b, core * width)
        acc = off[:, par] + tap[0:1, par] * source[5 : 5 + ROWS, cols]
        for j in range(1, CONV):
            acc = acc + tap[j : j + 1, par] * source[5 + j : 5 + j + ROWS, cols]
        return acc

    def state_block(b, carry):
        cols = block128(b)
        acc = conv(sbuf, s_tap, s_off, b, 2 * STATE)
        spre_out[:, cols] = acc
        bc_out[:, cols] = (acc * sigmoid_by_tanh(acc)).astype(bf16)
        return carry

    lax.fori_loop(0, 4, state_block, 0)

    def value_block(b, carry):
        cols = block128(b)
        acc = conv(buf, v_tap, v_off, b, WIDE)
        pre_out[:, cols] = acc
        post = (acc * sigmoid_by_tanh(acc)).astype(bf16)
        x_out[:, cols] = post
        xs_out[:, cols] = (post.astype(f32) * wide[:, cols]).astype(bf16)
        return carry

    lax.fori_loop(0, 16, value_block, 0)


def state_kernel_body(
    halo_a, halo_b, top, stop, wide, within, v_tap, v_off, s_tap, s_off, ones,
    x_in, xs_in, bc_in, pre_in, spre_in,
    m0, m1, m2, m3, x_out, xs_out, bc_out, pre_out, spre_out,
):
    core, ring = place()
    halo = halo_a[...].astype(f32) + halo_b[...].astype(f32)

    def first_rows(source, start, tap, off, c, width):
        par = pl.ds(pl.multiple_of(core * width + c, 128), PART)
        both = jnp.concatenate(
            [halo[:, start + c : start + c + PART], source[:, c : c + PART]], axis=0
        )
        acc = off[:, par] + tap[0:1, par] * both[5 : 5 + TAIL]
        for j in range(1, CONV):
            acc = acc + tap[j : j + 1, par] * both[5 + j : 5 + j + TAIL]
        return acc, (acc * sigmoid_by_tanh(acc)).astype(bf16)

    for c in range(0, WIDE, PART):
        cols = slice(c, c + PART)
        acc, post = first_rows(top, 0, v_tap, v_off, c, WIDE)
        pre_out[0:TAIL, cols] = acc
        x_out[0:TAIL, cols] = post
        xs_out[0:TAIL, cols] = (post.astype(f32) * wide[0:TAIL, cols]).astype(bf16)
    acc, post = first_rows(stop, WIDE, s_tap, s_off, 0, 2 * STATE)
    spre_out[0:TAIL, :] = acc
    bc_out[0:TAIL, :] = post
    total = within[ROWS - 1 : ROWS, :]
    write_t = bc_out[:, :STATE].astype(f32).T.astype(bf16)
    total_parts = split3(jnp.broadcast_to(total, (8, 128)))
    for slot, out in enumerate((m0, m1, m2, m3)):
        cols = head_columns(ring, slot)
        out[0:STATE, :] = nn(write_t, xs_out[:, cols]).astype(bf16)
        full = nn(total_parts, ones[:, cols])[0:1, :]
        high = full.astype(bf16).astype(f32)
        mid = (full - high).astype(bf16).astype(f32)
        low = full - high - mid
        row = iota((TAIL, PART), 0)
        out[STATE : STATE + TAIL, :] = jnp.where(
            row == 0, high, jnp.where(row == 1, mid, jnp.where(row == 2, low, 0.0))
        ).astype(bf16)


def slope_kernel(pre, spre, wide, sx_out, k_out, sbc_out):
    def slope(acc):
        sig = sigmoid_by_tanh(acc)
        return sig * (1.0 + acc * (1.0 - sig))

    def value_block(b, carry):
        cols = block128(b)
        out = slope(pre[:, cols])
        sx_out[:, cols] = out.astype(bf16)
        k_out[:, cols] = (out * wide[:, cols]).astype(bf16)
        return carry

    lax.fori_loop(0, 16, value_block, 0)

    def state_block(b, carry):
        cols = block128(b)
        sbc_out[:, cols] = slope(spre[:, cols]).astype(bf16)
        return carry

    lax.fori_loop(0, 4, state_block, 0)


def ring_totals(parts):
    out = []
    for part in parts:
        rows = part[STATE : STATE + TAIL, :].astype(f32)
        out.append(rows[0:1] + rows[1:2] + rows[2:3])
    return out


def between(totals, places, low, high):
    out = jnp.zeros_like(totals[0])
    for total, p in zip(totals, places):
        inside = jnp.logical_and(p > low, p < high)
        out = out + total * jnp.where(inside, 1.0, 0.0)
    return out


def edge_kernel(back, m0, m1, m2, m3, d0, d1, d2, d3, out):
    core, ring = place()
    places = [lax.rem(ring + RING - s, RING) for s in range(RING)]
    totals = ring_totals((m0, m1, m2, m3))
    weights = []
    for p in places:
        low, high = (-1, p) if back else (p, RING)
        weights.append(jnp.exp(between(totals, places, low, high)))
    for c in range(0, PART, 128):
        cols = slice(c, c + 128)
        acc = None
        for src, weight in zip((d0, d1, d2, d3), weights):
            term = weight[:, cols] * src[0:STATE, cols].astype(f32)
            acc = term if acc is None else acc + term
        out[:, cols] = acc.astype(bf16)


def scan_kernel(back, m0, m1, m2, m3, d0, d1, d2, d3, edge, o0, o1, o2, o3):
    core, ring = place()
    places = [lax.rem(ring + RING - s, RING) for s in range(RING)]
    totals = ring_totals((m0, m1, m2, m3))
    weights = []
    for here in places:
        low, high = (here, RING) if back else (-1, here)
        row = [jnp.exp(between(totals, places, low, high))]
        for p in places:
            low, high, live = (here, p, p > here) if back else (p, here, p < here)
            row.append(jnp.exp(between(totals, places, low, high)) * jnp.where(live, 1.0, 0.0))
        weights.append(row)
    for c in range(0, PART, 128):
        cols = slice(c, c + 128)
        for r in range(0, STATE, 64):
            rows = slice(r, r + 64)
            parts = [edge[rows, cols].astype(f32)]
            parts += [src[rows, cols].astype(f32) for src in (d0, d1, d2, d3)]
            for out, row in zip((o0, o1, o2, o3), weights):
                acc = row[0][:, cols] * parts[0]
                for weight, part in zip(row[1:], parts[1:]):
                    acc = acc + weight[:, cols] * part
                out[rows, cols] = acc.astype(bf16)


def second_kernel(g_own, g_in, bc, within, ones, d0, d1, d2, d3, dy_out, dye_out, wide):
    core, ring = place()
    mine, other = rows_of(core)
    dy_out[mine, :] = g_own[...]
    dy_out[other, :] = g_in[...]
    wide[...] = nn(split3(jnp.exp(within[...])), ones[...])
    read_t = bc[:, STATE:].astype(f32).T.astype(bf16)

    def block(b, carry):
        cols = block128(b)
        dye_out[:, cols] = (dy_out[:, cols].astype(f32) * wide[:, cols]).astype(bf16)
        return carry

    lax.fori_loop(0, 16, block, 0)
    for slot, out in enumerate((d0, d1, d2, d3)):
        out[...] = nn(read_t, dye_out[:, head_columns(ring, slot)]).astype(bf16)


def inner_kernel(part, x, dy, bc, delta, within, sx, skip_gain, ones, *refs):
    if part == 0:
        base_out, dbcs, diff_out, vsum_out = refs[:4]
        scratch = refs[4:]
    else:
        dbcs_in, diff_in, vsum_in, base_in = refs[:4]
        base_out, dbc_out, diff_out, vsum_out, top_out = refs[4:9]
        scratch = refs[9:]
        dbcs = scratch[-1]
    wide, skips, within_3, row_sum, bcs = scratch[:5]
    core, ring = place()
    half = ROWS // 2
    low_col, low_head = part * (WIDE // 2), part * (HEADS // 2)
    own = ones[:, low_col : low_col + WIDE // 2]
    wide[...] = nn(split3(delta[...]), own)
    skip = jnp.broadcast_to(tiled_heads(skip_gain[...], core), (8, 128))
    skips[...] = nn(split3(skip), own)
    scaled = within[...] * LOG2E
    lane_part = iota((ROWS, 128), 1) // HEADS
    left = jnp.where(lane_part == 3, 1.0, -split3(scaled).astype(f32)).astype(bf16)
    parts_t = split3(scaled).astype(f32).T
    for h in range(HEADS // 2):
        for piece in range(3):
            at = piece * HEADS + low_head + h
            within_3[h, piece : piece + 1, :] = parts_t[at : at + 1, :]
        within_3[h, 3:8, :] = jnp.zeros((5, ROWS), f32)
    write, read = bc[:, :STATE], bc[:, STATE:]
    bcs[...] = nt(write, read)
    if part == 0:
        dbcs[...] = jnp.zeros_like(dbcs)
        diff_out[...] = jnp.zeros_like(diff_out)
        vsum_out[...] = jnp.zeros_like(vsum_out)
    else:
        dbcs[...] = dbcs_in[...]
        diff_out[...] = diff_in[...]
        vsum_out[...] = vsum_in[...]
    row_sum[...] = jnp.zeros_like(row_sum)
    keep = iota((half, half), 1) >= iota((half, half), 0)
    lanes = iota((ROWS, 128), 1)
    first = lanes < HEAD_DIM
    row_head = iota((96, ROWS), 0) % HEADS
    pad = jnp.zeros((24, ROWS), f32)

    def pair(b, carry):
        cols, here = block128(b, low_col), block128(b)
        xb = x[:, cols].astype(f32)
        xd = (xb * wide[:, here]).astype(bf16)
        grad = dy[:, cols]
        zero = jnp.zeros_like(grad)
        top = jnp.zeros((half, 128), f32)
        bot = jnp.zeros((half, 128), f32)
        col_total = jnp.zeros((ROWS, 128), f32)
        grads_of = [0.0, 0.0, 0.0]
        for e in range(2):
            h = low_head + 2 * b + e
            g = jnp.where(first, grad, zero) if e == 0 else jnp.where(first, zero, grad)
            right = jnp.concatenate(
                [jnp.where(row_head == h, 1.0, 0.0), within_3[2 * b + e], pad], axis=0
            ).astype(bf16)
            gap0 = nn(left[:half], right)
            gap1 = nn(left[half:], right[:, half:])
            dm0 = nt(xd[:half], g)
            dm1 = nt(xd[half:], g[half:])
            blocks = (
                (jnp.where(keep, gap0[:, :half], -jnp.inf), dm0[:, :half], 0, 0),
                (gap0[:, half:], dm0[:, half:], 0, 1),
                (jnp.where(keep, gap1, -jnp.inf), dm1, 1, 1),
            )
            ps, ms = [], []
            for k, (gap, dm, r, c) in enumerate(blocks):
                decay = jnp.exp2(gap)
                m = decay * bcs[r * half : (r + 1) * half, c * half : (c + 1) * half]
                grads_of[k] = grads_of[k] + dm * decay
                ps.append(dm * m)
                ms.append(m.astype(bf16))
            sum_rows = jnp.concatenate(
                [
                    jnp.sum(ps[0], axis=0, keepdims=True),
                    jnp.sum(ps[1] + ps[2], axis=0, keepdims=True),
                ],
                axis=1,
            )
            row_sum[pl.ds(h, 1), :] = sum_rows
            top = top + nn(ms[0], g[:half]) + nn(ms[1], g[half:])
            bot = bot + nn(ms[2], g[half:])
            col = jnp.concatenate(
                [
                    jnp.sum(ps[0] + ps[1], axis=1, keepdims=True),
                    jnp.sum(ps[2], axis=1, keepdims=True),
                ],
                axis=0,
            )
            col_total = col_total + jnp.where(lanes % HEADS == h, col, 0.0)
        for k, (r, c) in enumerate(((0, 0), (0, 1), (1, 1))):
            rs, cs = slice(r * half, (r + 1) * half), slice(c * half, (c + 1) * half)
            dbcs[rs, cs] = dbcs[rs, cs] + grads_of[k]
        u = jnp.concatenate([top, bot], axis=0)
        diff_out[...] = diff_out[...] - col_total
        vsum_out[...] = vsum_out[...] + head_sum(xb * u, ones[:, cols])
        base_out[:, here] = (
            wide[:, here] * u + skips[0:1, here] * grad.astype(f32)
        ) * sx[:, cols].astype(f32)
        return carry

    lax.fori_loop(0, 8, pair, 0)
    for t in range(1, 4):
        row_sum[t * HEADS : (t + 1) * HEADS, :] = row_sum[0:HEADS, :]
    diff_out[...] = diff_out[...] + row_sum[...].T
    if part == 1:
        grad = dbcs[...]
        dbc_out[:, :STATE] = nn(grad.astype(bf16), read)
        dbc_out[:, STATE:] = nn(grad.T.astype(bf16), write)
        top_out[:, : WIDE // 2] = base_in[0:8, :]
        top_out[:, WIDE // 2 :] = base_out[0:8, :]


def carry_kernel(c0, c1, c2, c3, bc, dye, dbc, diff, ones, diff_out, dread_out, carried_out):
    core, ring = place()
    for slot, src in enumerate((c0, c1, c2, c3)):
        carried_out[:, head_columns(ring, slot)] = src[...]
    read = bc[:, STATE:]
    dread_out[...] = dbc[:, STATE:] + nt(dye[...], carried_out[...])
    outer = diff[...]
    for b in range(4):
        cols = slice(b * PART, (b + 1) * PART)
        part = nn(read, carried_out[:, cols]) * dye[:, cols].astype(f32)
        outer = outer + head_sum(part, ones[:, cols])
    diff_out[...] = outer


def last_kernel(
    g0, g1, g2, g3, carried, bc, xs, k, base_0, base_1, sbc, delta, within, sig, diff, vsum,
    dread, dbc, decay_log, ones,
    e_out, es_out, steps_out,
    gbuf,
):
    core, ring = place()
    for slot, src in enumerate((g0, g1, g2, g3)):
        gbuf[:, head_columns(ring, slot)] = src[...]
    write = bc[:, :STATE]
    rsum = jnp.zeros((ROWS, 128), f32)
    tsum = jnp.zeros((8, 128), f32)
    for b in range(4):
        cols = slice(b * PART, (b + 1) * PART)
        grad = gbuf[:, cols]
        through = nn(write, grad)
        rsum = rsum + head_sum(xs[:, cols].astype(f32) * through, ones[:, cols])
        base = (base_0, base_1)[b // 2][:, (b % 2) * PART : (b % 2 + 1) * PART]
        e_out[:, cols] = base + k[:, cols].astype(f32) * through
        both = jnp.sum(
            grad.astype(f32) * carried[:, cols].astype(f32), axis=0, keepdims=True
        )
        tsum = tsum + head_sum(jnp.broadcast_to(both, (8, PART)), ones[:, cols])
    total = within[ROWS - 1 : ROWS, :]
    dtotal = tsum[0:1, :] * jnp.exp(total)
    ra, rb = iota((ROWS, ROWS), 0), iota((ROWS, ROWS), 1)
    later = jnp.where(rb >= ra, 1.0, 0.0).astype(f32)
    earlier = jnp.where(rb < ra, 1.0, 0.0).astype(f32)
    da = nn(later, diff[...], HIGH) + nn(earlier, rsum, HIGH) + dtotal
    rate = -jnp.exp(tiled_heads(decay_log[...], core))
    steps_out[...] = (vsum[...] + rsum / delta[...] + rate * da) * sig[...]
    dwrite = dbc[:, :STATE] + nt(xs[...], gbuf[...])
    es_out[:, :STATE] = dwrite * sbc[:, :STATE].astype(f32)
    es_out[:, STATE:] = dread[...] * sbc[:, STATE:].astype(f32)


def back_kernel(
    e, es, steps, head, v_tap, s_tap, vg_own, sg_own, st_own, message, back, sback
):
    core, ring = place()
    mine, other = rows_of(core)
    body = ROWS - TAIL

    def conv(source, start, tap, b, width, out):
        cols, par = block128(b), block128(b, core * width)
        edge = jnp.concatenate(
            [source[body:, cols], head[:, block128(b, start)].astype(f32)], axis=0
        )
        acc = tap[CONV - 1 : CONV, par] * source[0:body, cols]
        end = tap[CONV - 1 : CONV, par] * edge[0:TAIL]
        for shift in range(1, CONV):
            weight = tap[CONV - 1 - shift : CONV - shift, par]
            acc = acc + weight * source[shift : shift + body, cols]
            end = end + weight * edge[shift : shift + TAIL]
        out[0:body, cols] = acc.astype(bf16)
        out[body:, cols] = end.astype(bf16)

    def value_block(b, carry):
        conv(e, 0, v_tap, b, WIDE, back)
        return carry

    lax.fori_loop(0, 16, value_block, 0)

    def state_block(b, carry):
        conv(es, WIDE, s_tap, b, 2 * STATE, sback)
        return carry

    lax.fori_loop(0, 4, state_block, 0)
    vg_own[...] = back[mine, :]
    message[:, :WIDE] = back[other, :]
    sg_own[...] = sback[mine, :]
    message[:, WIDE : WIDE + 2 * STATE] = sback[other, :]
    st_own[...] = steps[mine, :].astype(bf16)
    message[:, WIDE + 2 * STATE :] = steps[other, :].astype(bf16)


def head_kernel(g0, g1, g2, g3, bc, xs, k, base_top, sbc, dread, dbc, out):
    core, ring = place()
    write = bc[0:TAIL, :STATE]
    dwrite = dbc[0:8, :STATE]
    for slot, src in enumerate((g0, g1, g2, g3)):
        cols = head_columns(ring, slot)
        grad = src[...]
        through = nn(write, grad)[0:8]
        out[:, cols] = (
            base_top[:, cols] + k[0:TAIL, cols].astype(f32)[0:8] * through
        ).astype(bf16)
        dwrite = dwrite + nt(xs[0:TAIL, cols], grad)[0:8]
    slope = sbc[0:TAIL, :].astype(f32)[0:8]
    out[:, WIDE : WIDE + STATE] = (dwrite * slope[:, :STATE]).astype(bf16)
    out[:, WIDE + STATE :] = (dread[0:8, :] * slope[:, STATE:]).astype(bf16)


def join_kernel(v_own, s_own, t_own, message, v_out, s_out, t_out):
    core, ring = place()

    def place_in(out, own, arrived, width):
        out[:, pl.ds(pl.multiple_of(core * width, 128), width)] = own
        out[:, pl.ds(pl.multiple_of((1 - core) * width, 128), width)] = arrived

    place_in(v_out, v_own[...], message[:, :WIDE], WIDE)
    place_in(s_out, s_own[...], message[:, WIDE : WIDE + 2 * STATE], 2 * STATE)
    own = t_own[...].astype(f32).T[:HEADS]
    arrived = message[:, WIDE + 2 * STATE :].astype(f32).T[:HEADS]
    low = jnp.where(core == 0, own, arrived)
    high = jnp.where(core == 0, arrived, own)
    t_out[...] = jnp.concatenate([low, high], axis=0).astype(bf16)


def call(kernel, args, outs, scratch=(), name=None, anywhere=(), cost=None, aliases={}):
    vmem = pl.BlockSpec(memory_space=pltpu.VMEM)
    args = [pltpu.with_memory_space_constraint(a, pltpu.HBM) if k in anywhere else a for k, a in enumerate(args)]
    return pl.pallas_call(
        kernel,
        in_specs=[
            pl.BlockSpec(memory_space=pltpu.HBM) if k in anywhere else vmem for k in range(len(args))
        ],
        out_specs=[vmem for _ in outs],
        out_shape=[jax.ShapeDtypeStruct(*o) for o in outs],
        scratch_shapes=[s if not isinstance(s, tuple) else pltpu.VMEM(*s) for s in scratch],
        compiler_params=pltpu.CompilerParams(vmem_limit_bytes=24 * 1024 * 1024),
        cost_estimate=None
        if cost is None
        else pl.CostEstimate(flops=0, transcendentals=0, bytes_accessed=int(cost * 3.0e6)),
        input_output_aliases=aliases,
        name=name,
    )(*args)


def local(
    value_input, state_input, step_raw, upstream, step_bias, decay_log, skip_gain,
    value_kernel, value_offset, state_kernel, state_offset,
):
    count = lax.axis_size("ctx")
    chips = count // CORES
    per_half = count // HALVES

    def send(x, pairs):
        return lax.ppermute(x, "ctx", pairs)

    swap_pairs = [(i, i ^ 1) for i in range(count)]

    def around(i, shift):
        half, at, c = i // (RING * CORES), (i // CORES) % RING, i % CORES
        return (half * RING + (at + shift) % RING) * CORES + c

    def exchange(parts, sign):
        out = list(parts)
        for k in (2, 1, 3):
            out[k] = send(parts[k], [(i, around(i, sign * k)) for i in range(count)])
        return out

    row = lambda x: x.reshape(1, -1)
    v, s, r, g = value_input[0], state_input[0], step_raw[0].T, upstream[0]
    bias, rate_log, skip = row(step_bias), row(decay_log), row(skip_gain)
    joint = WIDE + 2 * STATE + 128
    tall = (ROWS, WIDE)
    narrow = (ROWS, 128)
    marked = ((STATE + TAIL, PART), bf16)
    state_part = ((STATE, PART), bf16)
    sems = pltpu.SemaphoreType.DMA

    message, halo_a, halo_b, halos = call(
        pack_kernel, [v, s, r],
        [((TOK, joint), bf16), ((HALO, WIDE + 2 * STATE), bf16), ((HALO, WIDE + 2 * STATE), bf16),
         ((2 * HALO, WIDE + 2 * STATE), bf16)],
        [((2 * HEADS, TOK), bf16), sems((11,))], "pack", (0, 1, 2),
    )
    middle = per_half - 1
    relayed = lax.ppermute(
        halos, ("pipe", "ctx"),
        [(p * count + middle, (1 - p) * count + middle) for p in range(2)],
    )
    message = send(message, swap_pairs)
    halo_a, halo_b = call(
        relay_kernel, [halo_a, halo_b, relayed], [((HALO, WIDE + 2 * STATE), bf16)] * 2, (), "relay"
    )

    def onward(x, step):
        pairs = []
        for p in range(2):
            for k in range(chips - 1):
                source = k * CORES + 1
                held = 1 - p if source == middle else p
                pairs.append((held * count + source, p * count + source + step))
        return lax.ppermute(x, ("pipe", "ctx"), pairs)

    g_own, g_in = call(
        pack_grad_kernel, [g], [((TOK, WIDE), bf16)] * 2, [sems((2,))], "pack_grad", (0,)
    )
    g_own, g_in, halo_a, halo_b = lax.optimization_barrier((g_own, g_in, halo_a, halo_b))
    halo_a = onward(halo_a, 2)
    halo_b = onward(halo_b, 1)
    g_own = lax.ppermute(g_own, "pipe", [(0, 1), (1, 0)])
    g_in = lax.ppermute(
        g_in,
        ("pipe", "ctx"),
        [(p * count + i, (1 - p) * count + (i ^ 1)) for p in range(2) for i in range(count)],
    )
    ones = call(ones_kernel, [], [((128, WIDE), bf16)], name="ones")[0]
    taps = [value_kernel, row(value_offset), state_kernel, row(state_offset)]
    half_done = [
        (tall, bf16), (tall, bf16), ((ROWS, 2 * STATE), bf16), (tall, f32),
        ((ROWS, 2 * STATE), f32),
    ]
    *begun, spread_scale, delta, within, sig, top, stop = call(
        first_kernel,
        [v, s, r, message, bias, rate_log] + taps + [ones],
        half_done + [(tall, f32)] + [(narrow, f32)] * 3
        + [((TAIL, WIDE), f32), ((TAIL, 2 * STATE), f32)],
        [((ROWS + 8, WIDE), f32), ((ROWS + 8, 2 * STATE), f32), (narrow, f32)],
        "first", cost=8,
    )
    m0, m1, m2, m3, x, xs, bc, pre, spre = call(
        state_kernel_body,
        [halo_a, halo_b, top, stop, spread_scale, within] + taps + [ones] + begun,
        [marked] * 4 + half_done, (), "states", cost=2,
        aliases={11 + j: 4 + j for j in range(5)},
    )
    marks = exchange((m0, m1, m2, m3), 1)
    sx, k, sbc = call(
        slope_kernel, [pre, spre, spread_scale],
        [(tall, bf16), (tall, bf16), ((ROWS, 2 * STATE), bf16)], (), "slopes", cost=2,
    )
    g_own, sx = lax.optimization_barrier((g_own, sx))
    d0, d1, d2, d3, dy, dye = call(
        second_kernel, [g_own, g_in, bc, within, ones],
        [state_part] * 4 + [(tall, bf16)] * 2, [(tall, f32)], "second", cost=4,
    )
    grads = exchange((d0, d1, d2, d3), 1)
    edge = call(
        functools.partial(edge_kernel, False), marks + marks, [state_part], (), "edge_forward",
        cost=2,
    )[0]
    edge_in = send(edge, [(i, i + per_half) for i in range(per_half)])
    half_wide = (ROWS, WIDE // 2)
    inner_scratch = [
        (half_wide, f32), ((8, WIDE // 2), f32), ((HEADS // 2, 8, ROWS), f32), ((128, ROWS), f32),
        ((ROWS, ROWS), f32),
    ]
    dy_now, _ = lax.optimization_barrier((dy, edge))
    base_0, dbcs, diff, vsum = call(
        functools.partial(inner_kernel, 0), [x, dy_now, bc, delta, within, sx, skip, ones],
        [(half_wide, f32), ((ROWS, ROWS), f32), (narrow, f32), (narrow, f32)],
        inner_scratch, "inner_0", cost=6,
    )
    edge_in, diff = lax.optimization_barrier((edge_in, diff))
    steps = call(
        functools.partial(scan_kernel, False), marks + marks + [edge_in],
        [state_part] * 4, (), "scan_forward", cost=3,
    )
    carried = exchange(steps, -1)
    *grads, _ = lax.optimization_barrier((*grads, base_0))
    edge_back = call(
        functools.partial(edge_kernel, True), marks + grads, [state_part], (), "edge_back", cost=2,
    )[0]
    edge_back = send(edge_back, [(i + per_half, i) for i in range(per_half)])
    steps_back = call(
        functools.partial(scan_kernel, True), marks + grads + [edge_back],
        [state_part] * 4, (), "scan_back", cost=3,
    )
    dy_now, _ = lax.optimization_barrier((dy, steps_back[0]))
    base_1, dbc, diff, vsum, base_top = call(
        functools.partial(inner_kernel, 1),
        [x, dy_now, bc, delta, within, sx, skip, ones, dbcs, diff, vsum, base_0],
        [(half_wide, f32), ((ROWS, 2 * STATE), f32), (narrow, f32), (narrow, f32),
         ((8, WIDE), f32)],
        inner_scratch + [((ROWS, ROWS), f32)], "inner_1", cost=6,
    )
    back = exchange(steps_back, -1)
    diff, dread, held = call(
        carry_kernel, list(carried) + [bc, dye, dbc, diff, ones],
        [(narrow, f32), ((ROWS, STATE), f32), ((STATE, WIDE), bf16)], (), "carry", cost=4,
    )
    head = call(
        head_kernel, list(back) + [bc, xs, k, base_top, sbc, dread, dbc],
        [((8, WIDE + 2 * STATE), bf16)], (), "head", cost=1,
    )[0]
    back[0], head = lax.optimization_barrier((back[0], head))
    head = send(head, [(i, i - CORES) for i in range(CORES, count)])
    e, es, steps = call(
        last_kernel,
        list(back)
        + [held, bc, xs, k, base_0, base_1, sbc, delta, within, sig, diff, vsum, dread, dbc,
           rate_log, ones],
        [(tall, f32), ((ROWS, 2 * STATE), f32), (narrow, f32)],
        [((STATE, WIDE), bf16)], "last", cost=5,
    )
    vg_own, sg_own, st_own, message = call(
        back_kernel, [e, es, steps, head, value_kernel, state_kernel],
        [((TOK, WIDE), bf16), ((TOK, 2 * STATE), bf16), ((TOK, 128), bf16),
         ((TOK, joint), bf16)],
        [(tall, bf16), ((ROWS, 2 * STATE), bf16)], "back", cost=3,
    )
    message = send(message, swap_pairs)
    value_out, state_out, step_out = call(
        join_kernel, [vg_own, sg_own, st_own, message],
        [((TOK, 2 * WIDE), bf16), ((TOK, 4 * STATE), bf16), ((2 * HEADS, TOK), bf16)],
        (), "join",
    )
    return value_out[None], state_out[None], step_out.T[None]


def solution(mesh):
    wide = P("pipe", "ctx", "tp")
    placed = (wide, wide, wide, wide, P("tp"), P("tp"), P("tp"), P(None, "tp"), P("tp"), P(None, "tp"), P("tp"))
    return jax.shard_map(
        local, mesh=mesh, in_specs=placed, out_specs=(wide, wide, wide), check_vma=False
    )
```

```python
import functools

import jax
import jax.numpy as jnp
from jax import lax
from jax.experimental import pallas as pl
from jax.experimental.pallas import tpu as pltpu
from jax.sharding import PartitionSpec as P

HEAD_DIM = 64
STATE = 256
CONV = 4
CORES = 2
RING = 4
HALVES = 2
f32 = jnp.float32
bf16 = jnp.bfloat16
HIGH = lax.Precision.HIGHEST

TOK = 128
ROWS = TOK * CORES
HEADS = 32
WIDE = HEADS * HEAD_DIM
PART = WIDE // RING
TAIL = 16
HALO = 8
LOG2E = 1.4426950408889634


def place():
    index = lax.axis_index("ctx")
    return lax.rem(index, CORES), lax.rem(lax.div(index, CORES), RING)


def rows_of(core):
    return (
        pl.ds(pl.multiple_of(core * TOK, TOK), TOK),
        pl.ds(pl.multiple_of((1 - core) * TOK, TOK), TOK),
    )


def block128(b, start=0):
    return pl.ds(pl.multiple_of(start + b * 128, 128), 128)


def head_columns(ring, slot):
    return pl.ds(pl.multiple_of(lax.rem(ring + slot, RING) * PART, PART), PART)


def nn(a, b, precision=None):
    return lax.dot_general(
        a, b, (((1,), (0,)), ((), ())), precision=precision, preferred_element_type=f32
    )


def nt(a, b):
    return lax.dot_general(a, b, (((1,), (1,)), ((), ())), preferred_element_type=f32)


def iota(shape, axis):
    return lax.broadcasted_iota(jnp.int32, shape, axis)


def split3(x):
    high = x.astype(bf16).astype(f32)
    rest = x - high
    mid = rest.astype(bf16).astype(f32)
    low = rest - mid
    part = iota(x.shape, 1) // HEADS
    picked = jnp.where(part == 0, high, jnp.where(part == 1, mid, jnp.where(part == 2, low, 0.0)))
    return picked.astype(bf16)


def head_sum(x, ones):
    high = x.astype(bf16)
    low = (x - high.astype(f32)).astype(bf16)
    return nt(high, ones) + nt(low, ones)


def tiled_heads(x, group):
    x = x.astype(f32)
    mine = jnp.where(group == 0, x[:, :HEADS], x[:, HEADS:])
    return jnp.concatenate([mine] * 4, axis=1)


def tiled_steps(x, group):
    x = x.astype(f32)
    mine = jnp.where(group == 0, x[:HEADS], x[HEADS:])
    return jnp.concatenate([mine] * 4, axis=0).T


def softplus(x):
    u = jnp.exp(-jnp.abs(x))
    small = u * (1.0 - u * (0.5 - u * (1.0 / 3.0 - u * 0.25)))
    return jnp.maximum(x, 0.0) + jnp.where(u < 0.01, small, jnp.log(1.0 + u))


def sigmoid(x):
    return 1.0 / (1.0 + jnp.exp(-x))


def sigmoid_by_tanh(x):
    return 0.5 + 0.5 * jnp.tanh(0.5 * x)


def run_copies(pairs, sems):
    copies = [pltpu.make_async_copy(a, b, sems.at[k]) for k, (a, b) in enumerate(pairs)]
    for copy in copies:
        copy.start()
    return copies


def pack_kernel(v, s, r, message, halo_a, halo_b, halos, r_here, sems):
    core, ring = place()
    there = 1 - core
    pairs = []
    rows = pl.ds(TOK - HALO, HALO)
    for group, halo in ((1, halo_a), (0, halo_b)):
        pairs.append((v.at[rows, pl.ds(group * WIDE, WIDE)], halo.at[:, pl.ds(0, WIDE)]))
        pairs.append(
            (s.at[rows, pl.ds(group * 2 * STATE, 2 * STATE)], halo.at[:, pl.ds(WIDE, 2 * STATE)])
        )
    v_there = pl.ds(pl.multiple_of(there * WIDE, 128), WIDE)
    s_there = pl.ds(pl.multiple_of(there * 2 * STATE, 128), 2 * STATE)
    for k, group in enumerate((1, 0)):
        at = pl.ds(k * HALO, HALO)
        pairs.append((v.at[rows, pl.ds(group * WIDE, WIDE)], halos.at[at, pl.ds(0, WIDE)]))
        pairs.append(
            (s.at[rows, pl.ds(group * 2 * STATE, 2 * STATE)], halos.at[at, pl.ds(WIDE, 2 * STATE)])
        )
    pairs.append((v.at[:, v_there], message.at[:, pl.ds(0, WIDE)]))
    pairs.append((s.at[:, s_there], message.at[:, pl.ds(WIDE, 2 * STATE)]))
    pairs.append((r, r_here))
    copies = run_copies(pairs, sems)
    copies.pop().wait()
    message[:, WIDE + 2 * STATE :] = tiled_steps(r_here[...], there).astype(bf16)
    for copy in copies:
        copy.wait()


def relay_kernel(halo_a, halo_b, relayed, out_a, out_b):
    index = lax.axis_index("ctx")
    handing = index == CORES * RING - 1
    out_a[...] = jnp.where(
        handing, relayed[:HALO].astype(f32), halo_a[...].astype(f32)
    ).astype(bf16)
    out_b[...] = jnp.where(
        handing, relayed[HALO:].astype(f32), halo_b[...].astype(f32)
    ).astype(bf16)


def pack_grad_kernel(g, own, across, sems):
    core, ring = place()
    copies = [
        pltpu.make_async_copy(
            g.at[:, pl.ds(pl.multiple_of(group * WIDE, 128), WIDE)], out, sems.at[k]
        )
        for k, (group, out) in enumerate(((core, own), (1 - core, across)))
    ]
    for copy in copies:
        copy.start()
    for copy in copies:
        copy.wait()


def ones_kernel(out):
    rows = iota((128, WIDE), 0) % HEADS
    cols = iota((128, WIDE), 1) // HEAD_DIM
    out[...] = jnp.where(rows == cols, 1.0, 0.0).astype(bf16)


def first_kernel(
    v, s, r, message, step_bias, decay_log, v_tap, v_off, s_tap, s_off, ones,
    x_out, xs_out, bc_out, pre_out, spre_out, wide, delta_out, within_out, sig_out, top_out,
    stop_out,
    buf, sbuf, raw,
):
    core, ring = place()
    mine, other = rows_of(core)
    raw[mine, :] = tiled_steps(r[...], core)
    raw[other, :] = message[:, WIDE + 2 * STATE :].astype(f32)
    pre = raw[...] + tiled_heads(step_bias[...], core)
    delta = softplus(pre)
    rate = -jnp.exp(tiled_heads(decay_log[...], core))
    lower = jnp.where(iota((ROWS, ROWS), 0) >= iota((ROWS, ROWS), 1), 1.0, 0.0).astype(f32)
    within = nn(lower, delta * rate, HIGH)
    delta_out[...] = delta
    within_out[...] = within
    sig_out[...] = sigmoid(pre)
    total = within[ROWS - 1 : ROWS, :]
    wide[...] = nn(split3(delta * jnp.exp(total - within)), ones[...])

    below = pl.ds(pl.multiple_of(8 + core * TOK, 8), TOK)
    above = pl.ds(pl.multiple_of(8 + (1 - core) * TOK, 8), TOK)
    v_mine = pl.ds(pl.multiple_of(core * WIDE, 128), WIDE)
    s_mine = pl.ds(pl.multiple_of(core * 2 * STATE, 128), 2 * STATE)
    buf[below, :] = v[:, v_mine].astype(f32)
    buf[above, :] = message[:, :WIDE].astype(f32)
    sbuf[below, :] = s[:, s_mine].astype(f32)
    sbuf[above, :] = message[:, WIDE : WIDE + 2 * STATE].astype(f32)
    buf[0:8, :] = jnp.zeros((8, WIDE), f32)
    sbuf[0:8, :] = jnp.zeros((8, 2 * STATE), f32)
    top_out[...] = buf[8 : 8 + TAIL, :]
    stop_out[...] = sbuf[8 : 8 + TAIL, :]

    def conv(source, tap, off, b, width):
        cols, par = block128(b), block128(b, core * width)
        acc = off[:, par] + tap[0:1, par] * source[5 : 5 + ROWS, cols]
        for j in range(1, CONV):
            acc = acc + tap[j : j + 1, par] * source[5 + j : 5 + j + ROWS, cols]
        return acc

    def state_block(b, carry):
        cols = block128(b)
        acc = conv(sbuf, s_tap, s_off, b, 2 * STATE)
        spre_out[:, cols] = acc
        bc_out[:, cols] = (acc * sigmoid_by_tanh(acc)).astype(bf16)
        return carry

    lax.fori_loop(0, 4, state_block, 0)

    def value_block(b, carry):
        cols = block128(b)
        acc = conv(buf, v_tap, v_off, b, WIDE)
        pre_out[:, cols] = acc
        post = (acc * sigmoid_by_tanh(acc)).astype(bf16)
        x_out[:, cols] = post
        xs_out[:, cols] = (post.astype(f32) * wide[:, cols]).astype(bf16)
        return carry

    lax.fori_loop(0, 16, value_block, 0)


def state_kernel_body(
    halo_a, halo_b, top, stop, wide, within, v_tap, v_off, s_tap, s_off, ones,
    x_in, xs_in, bc_in, pre_in, spre_in,
    m0, m1, m2, m3, x_out, xs_out, bc_out, pre_out, spre_out,
):
    core, ring = place()
    halo = halo_a[...].astype(f32) + halo_b[...].astype(f32)

    def first_rows(source, start, tap, off, c, width):
        par = pl.ds(pl.multiple_of(core * width + c, 128), PART)
        both = jnp.concatenate(
            [halo[:, start + c : start + c + PART], source[:, c : c + PART]], axis=0
        )
        acc = off[:, par] + tap[0:1, par] * both[5 : 5 + TAIL]
        for j in range(1, CONV):
            acc = acc + tap[j : j + 1, par] * both[5 + j : 5 + j + TAIL]
        return acc, (acc * sigmoid_by_tanh(acc)).astype(bf16)

    for c in range(0, WIDE, PART):
        cols = slice(c, c + PART)
        acc, post = first_rows(top, 0, v_tap, v_off, c, WIDE)
        pre_out[0:TAIL, cols] = acc
        x_out[0:TAIL, cols] = post
        xs_out[0:TAIL, cols] = (post.astype(f32) * wide[0:TAIL, cols]).astype(bf16)
    acc, post = first_rows(stop, WIDE, s_tap, s_off, 0, 2 * STATE)
    spre_out[0:TAIL, :] = acc
    bc_out[0:TAIL, :] = post
    total = within[ROWS - 1 : ROWS, :]
    write_t = bc_out[:, :STATE].astype(f32).T.astype(bf16)
    total_parts = split3(jnp.broadcast_to(total, (8, 128)))
    for slot, out in enumerate((m0, m1, m2, m3)):
        cols = head_columns(ring, slot)
        out[0:STATE, :] = nn(write_t, xs_out[:, cols]).astype(bf16)
        full = nn(total_parts, ones[:, cols])[0:1, :]
        high = full.astype(bf16).astype(f32)
        mid = (full - high).astype(bf16).astype(f32)
        low = full - high - mid
        row = iota((TAIL, PART), 0)
        out[STATE : STATE + TAIL, :] = jnp.where(
            row == 0, high, jnp.where(row == 1, mid, jnp.where(row == 2, low, 0.0))
        ).astype(bf16)


def slope_kernel(pre, spre, wide, sx_out, k_out, sbc_out):
    def slope(acc):
        sig = sigmoid_by_tanh(acc)
        return sig * (1.0 + acc * (1.0 - sig))

    def value_block(b, carry):
        cols = block128(b)
        out = slope(pre[:, cols])
        sx_out[:, cols] = out.astype(bf16)
        k_out[:, cols] = (out * wide[:, cols]).astype(bf16)
        return carry

    lax.fori_loop(0, 16, value_block, 0)

    def state_block(b, carry):
        cols = block128(b)
        sbc_out[:, cols] = slope(spre[:, cols]).astype(bf16)
        return carry

    lax.fori_loop(0, 4, state_block, 0)


def ring_totals(parts):
    out = []
    for part in parts:
        rows = part[STATE : STATE + TAIL, :].astype(f32)
        out.append(rows[0:1] + rows[1:2] + rows[2:3])
    return out


def between(totals, places, low, high):
    out = jnp.zeros_like(totals[0])
    for total, p in zip(totals, places):
        inside = jnp.logical_and(p > low, p < high)
        out = out + total * jnp.where(inside, 1.0, 0.0)
    return out


def edge_kernel(back, m0, m1, m2, m3, d0, d1, d2, d3, out):
    core, ring = place()
    places = [lax.rem(ring + RING - s, RING) for s in range(RING)]
    totals = ring_totals((m0, m1, m2, m3))
    weights = []
    for p in places:
        low, high = (-1, p) if back else (p, RING)
        weights.append(jnp.exp(between(totals, places, low, high)))
    for c in range(0, PART, 128):
        cols = slice(c, c + 128)
        acc = None
        for src, weight in zip((d0, d1, d2, d3), weights):
            term = weight[:, cols] * src[0:STATE, cols].astype(f32)
            acc = term if acc is None else acc + term
        out[:, cols] = acc.astype(bf16)


def scan_kernel(back, m0, m1, m2, m3, d0, d1, d2, d3, edge, o0, o1, o2, o3):
    core, ring = place()
    places = [lax.rem(ring + RING - s, RING) for s in range(RING)]
    totals = ring_totals((m0, m1, m2, m3))
    weights = []
    for here in places:
        low, high = (here, RING) if back else (-1, here)
        row = [jnp.exp(between(totals, places, low, high))]
        for p in places:
            low, high, live = (here, p, p > here) if back else (p, here, p < here)
            row.append(jnp.exp(between(totals, places, low, high)) * jnp.where(live, 1.0, 0.0))
        weights.append(row)
    for c in range(0, PART, 128):
        cols = slice(c, c + 128)
        for r in range(0, STATE, 64):
            rows = slice(r, r + 64)
            parts = [edge[rows, cols].astype(f32)]
            parts += [src[rows, cols].astype(f32) for src in (d0, d1, d2, d3)]
            for out, row in zip((o0, o1, o2, o3), weights):
                acc = row[0][:, cols] * parts[0]
                for weight, part in zip(row[1:], parts[1:]):
                    acc = acc + weight[:, cols] * part
                out[rows, cols] = acc.astype(bf16)


def second_kernel(g_own, g_in, bc, within, ones, d0, d1, d2, d3, dy_out, dye_out, wide):
    core, ring = place()
    mine, other = rows_of(core)
    dy_out[mine, :] = g_own[...]
    dy_out[other, :] = g_in[...]
    wide[...] = nn(split3(jnp.exp(within[...])), ones[...])
    read_t = bc[:, STATE:].astype(f32).T.astype(bf16)

    def block(b, carry):
        cols = block128(b)
        dye_out[:, cols] = (dy_out[:, cols].astype(f32) * wide[:, cols]).astype(bf16)
        return carry

    lax.fori_loop(0, 16, block, 0)
    for slot, out in enumerate((d0, d1, d2, d3)):
        out[...] = nn(read_t, dye_out[:, head_columns(ring, slot)]).astype(bf16)


def inner_kernel(part, x, dy, bc, delta, within, sx, skip_gain, ones, *refs):
    if part == 0:
        base_out, dbcs, diff_out, vsum_out = refs[:4]
        scratch = refs[4:]
    else:
        dbcs_in, diff_in, vsum_in, base_in = refs[:4]
        base_out, dbc_out, diff_out, vsum_out, top_out = refs[4:9]
        scratch = refs[9:]
        dbcs = scratch[-1]
    wide, skips, within_3, row_sum, bcs = scratch[:5]
    core, ring = place()
    half = ROWS // 2
    low_col, low_head = part * (WIDE // 2), part * (HEADS // 2)
    own = ones[:, low_col : low_col + WIDE // 2]
    wide[...] = nn(split3(delta[...]), own)
    skip = jnp.broadcast_to(tiled_heads(skip_gain[...], core), (8, 128))
    skips[...] = nn(split3(skip), own)
    scaled = within[...] * LOG2E
    lane_part = iota((ROWS, 128), 1) // HEADS
    left = jnp.where(lane_part == 3, 1.0, -split3(scaled).astype(f32)).astype(bf16)
    parts_t = split3(scaled).astype(f32).T
    for h in range(HEADS // 2):
        for piece in range(3):
            at = piece * HEADS + low_head + h
            within_3[h, piece : piece + 1, :] = parts_t[at : at + 1, :]
        within_3[h, 3:8, :] = jnp.zeros((5, ROWS), f32)
    write, read = bc[:, :STATE], bc[:, STATE:]
    bcs[...] = nt(write, read)
    if part == 0:
        dbcs[...] = jnp.zeros_like(dbcs)
        diff_out[...] = jnp.zeros_like(diff_out)
        vsum_out[...] = jnp.zeros_like(vsum_out)
    else:
        dbcs[...] = dbcs_in[...]
        diff_out[...] = diff_in[...]
        vsum_out[...] = vsum_in[...]
    row_sum[...] = jnp.zeros_like(row_sum)
    keep = iota((half, half), 1) >= iota((half, half), 0)
    lanes = iota((ROWS, 128), 1)
    first = lanes < HEAD_DIM
    row_head = iota((96, ROWS), 0) % HEADS
    pad = jnp.zeros((24, ROWS), f32)

    def pair(b, carry):
        cols, here = block128(b, low_col), block128(b)
        xb = x[:, cols].astype(f32)
        xd = (xb * wide[:, here]).astype(bf16)
        grad = dy[:, cols]
        zero = jnp.zeros_like(grad)
        top = jnp.zeros((half, 128), f32)
        bot = jnp.zeros((half, 128), f32)
        col_total = jnp.zeros((ROWS, 128), f32)
        grads_of = [0.0, 0.0, 0.0]
        for e in range(2):
            h = low_head + 2 * b + e
            g = jnp.where(first, grad, zero) if e == 0 else jnp.where(first, zero, grad)
            right = jnp.concatenate(
                [jnp.where(row_head == h, 1.0, 0.0), within_3[2 * b + e], pad], axis=0
            ).astype(bf16)
            gap0 = nn(left[:half], right)
            gap1 = nn(left[half:], right[:, half:])
            dm0 = nt(xd[:half], g)
            dm1 = nt(xd[half:], g[half:])
            blocks = (
                (jnp.where(keep, gap0[:, :half], -jnp.inf), dm0[:, :half], 0, 0),
                (gap0[:, half:], dm0[:, half:], 0, 1),
                (jnp.where(keep, gap1, -jnp.inf), dm1, 1, 1),
            )
            ps, ms = [], []
            for k, (gap, dm, r, c) in enumerate(blocks):
                decay = jnp.exp2(gap)
                m = decay * bcs[r * half : (r + 1) * half, c * half : (c + 1) * half]
                grads_of[k] = grads_of[k] + dm * decay
                ps.append(dm * m)
                ms.append(m.astype(bf16))
            sum_rows = jnp.concatenate(
                [
                    jnp.sum(ps[0], axis=0, keepdims=True),
                    jnp.sum(ps[1] + ps[2], axis=0, keepdims=True),
                ],
                axis=1,
            )
            row_sum[pl.ds(h, 1), :] = sum_rows
            top = top + nn(ms[0], g[:half]) + nn(ms[1], g[half:])
            bot = bot + nn(ms[2], g[half:])
            col = jnp.concatenate(
                [
                    jnp.sum(ps[0] + ps[1], axis=1, keepdims=True),
                    jnp.sum(ps[2], axis=1, keepdims=True),
                ],
                axis=0,
            )
            col_total = col_total + jnp.where(lanes % HEADS == h, col, 0.0)
        for k, (r, c) in enumerate(((0, 0), (0, 1), (1, 1))):
            rs, cs = slice(r * half, (r + 1) * half), slice(c * half, (c + 1) * half)
            dbcs[rs, cs] = dbcs[rs, cs] + grads_of[k]
        u = jnp.concatenate([top, bot], axis=0)
        diff_out[...] = diff_out[...] - col_total
        vsum_out[...] = vsum_out[...] + head_sum(xb * u, ones[:, cols])
        base_out[:, here] = (
            wide[:, here] * u + skips[0:1, here] * grad.astype(f32)
        ) * sx[:, cols].astype(f32)
        return carry

    lax.fori_loop(0, 8, pair, 0)
    for t in range(1, 4):
        row_sum[t * HEADS : (t + 1) * HEADS, :] = row_sum[0:HEADS, :]
    diff_out[...] = diff_out[...] + row_sum[...].T
    if part == 1:
        grad = dbcs[...]
        dbc_out[:, :STATE] = nn(grad.astype(bf16), read)
        dbc_out[:, STATE:] = nn(grad.T.astype(bf16), write)
        top_out[:, : WIDE // 2] = base_in[0:8, :]
        top_out[:, WIDE // 2 :] = base_out[0:8, :]


def carry_kernel(c0, c1, c2, c3, bc, dye, dbc, diff, ones, diff_out, dread_out, carried_out):
    core, ring = place()
    for slot, src in enumerate((c0, c1, c2, c3)):
        carried_out[:, head_columns(ring, slot)] = src[...]
    read = bc[:, STATE:]
    dread_out[...] = dbc[:, STATE:] + nt(dye[...], carried_out[...])
    outer = diff[...]
    for b in range(4):
        cols = slice(b * PART, (b + 1) * PART)
        part = nn(read, carried_out[:, cols]) * dye[:, cols].astype(f32)
        outer = outer + head_sum(part, ones[:, cols])
    later = jnp.where(iota((ROWS, ROWS), 1) >= iota((ROWS, ROWS), 0), 1.0, 0.0).astype(f32)
    diff_out[...] = nn(later, outer, HIGH)


def last_kernel(
    g0, g1, g2, g3, carried, bc, xs, k, base_0, base_1, sbc, delta, within, sig, diff, vsum,
    dread, dbc, decay_log, ones,
    e_out, es_out, steps_out,
    gbuf,
):
    core, ring = place()
    for slot, src in enumerate((g0, g1, g2, g3)):
        gbuf[:, head_columns(ring, slot)] = src[...]
    write = bc[:, :STATE]
    rsum = jnp.zeros((ROWS, 128), f32)
    tsum = jnp.zeros((8, 128), f32)
    for b in range(4):
        cols = slice(b * PART, (b + 1) * PART)
        grad = gbuf[:, cols]
        through = nn(write, grad)
        rsum = rsum + head_sum(xs[:, cols].astype(f32) * through, ones[:, cols])
        base = (base_0, base_1)[b // 2][:, (b % 2) * PART : (b % 2 + 1) * PART]
        e_out[:, cols] = base + k[:, cols].astype(f32) * through
        both = jnp.sum(
            grad.astype(f32) * carried[:, cols].astype(f32), axis=0, keepdims=True
        )
        tsum = tsum + head_sum(jnp.broadcast_to(both, (8, PART)), ones[:, cols])
    total = within[ROWS - 1 : ROWS, :]
    dtotal = tsum[0:1, :] * jnp.exp(total)
    ra, rb = iota((ROWS, ROWS), 0), iota((ROWS, ROWS), 1)
    earlier = jnp.where(rb < ra, 1.0, 0.0).astype(f32)
    da = diff[...] + nn(earlier, rsum, HIGH) + dtotal
    rate = -jnp.exp(tiled_heads(decay_log[...], core))
    steps_out[...] = (vsum[...] + rsum / delta[...] + rate * da) * sig[...]
    dwrite = dbc[:, :STATE] + nt(xs[...], gbuf[...])
    es_out[:, :STATE] = dwrite * sbc[:, :STATE].astype(f32)
    es_out[:, STATE:] = dread[...] * sbc[:, STATE:].astype(f32)


def back_kernel(
    e, es, steps, head, v_tap, s_tap, vg_own, sg_own, st_own, message, back, sback
):
    core, ring = place()
    mine, other = rows_of(core)
    body = ROWS - TAIL

    def conv(source, start, tap, b, width, out):
        cols, par = block128(b), block128(b, core * width)
        edge = jnp.concatenate(
            [source[body:, cols], head[:, block128(b, start)].astype(f32)], axis=0
        )
        acc = tap[CONV - 1 : CONV, par] * source[0:body, cols]
        end = tap[CONV - 1 : CONV, par] * edge[0:TAIL]
        for shift in range(1, CONV):
            weight = tap[CONV - 1 - shift : CONV - shift, par]
            acc = acc + weight * source[shift : shift + body, cols]
            end = end + weight * edge[shift : shift + TAIL]
        out[0:body, cols] = acc.astype(bf16)
        out[body:, cols] = end.astype(bf16)

    def value_block(b, carry):
        conv(e, 0, v_tap, b, WIDE, back)
        return carry

    lax.fori_loop(0, 16, value_block, 0)

    def state_block(b, carry):
        conv(es, WIDE, s_tap, b, 2 * STATE, sback)
        return carry

    lax.fori_loop(0, 4, state_block, 0)
    vg_own[...] = back[mine, :]
    message[:, :WIDE] = back[other, :]
    sg_own[...] = sback[mine, :]
    message[:, WIDE : WIDE + 2 * STATE] = sback[other, :]
    st_own[...] = steps[mine, :].astype(bf16)
    message[:, WIDE + 2 * STATE :] = steps[other, :].astype(bf16)


def head_kernel(g0, g1, g2, g3, bc, xs, k, base_top, sbc, dread, dbc, out):
    core, ring = place()
    write = bc[0:TAIL, :STATE]
    dwrite = dbc[0:8, :STATE]
    for slot, src in enumerate((g0, g1, g2, g3)):
        cols = head_columns(ring, slot)
        grad = src[...]
        through = nn(write, grad)[0:8]
        out[:, cols] = (
            base_top[:, cols] + k[0:TAIL, cols].astype(f32)[0:8] * through
        ).astype(bf16)
        dwrite = dwrite + nt(xs[0:TAIL, cols], grad)[0:8]
    slope = sbc[0:TAIL, :].astype(f32)[0:8]
    out[:, WIDE : WIDE + STATE] = (dwrite * slope[:, :STATE]).astype(bf16)
    out[:, WIDE + STATE :] = (dread[0:8, :] * slope[:, STATE:]).astype(bf16)


def join_kernel(v_own, s_own, t_own, message, v_out, s_out, t_out):
    core, ring = place()

    def place_in(out, own, arrived, width):
        out[:, pl.ds(pl.multiple_of(core * width, 128), width)] = own
        out[:, pl.ds(pl.multiple_of((1 - core) * width, 128), width)] = arrived

    place_in(v_out, v_own[...], message[:, :WIDE], WIDE)
    place_in(s_out, s_own[...], message[:, WIDE : WIDE + 2 * STATE], 2 * STATE)
    own = t_own[...].astype(f32).T[:HEADS]
    arrived = message[:, WIDE + 2 * STATE :].astype(f32).T[:HEADS]
    low = jnp.where(core == 0, own, arrived)
    high = jnp.where(core == 0, arrived, own)
    t_out[...] = jnp.concatenate([low, high], axis=0).astype(bf16)


def call(kernel, args, outs, scratch=(), name=None, anywhere=(), cost=None, aliases={}):
    vmem = pl.BlockSpec(memory_space=pltpu.VMEM)
    args = [pltpu.with_memory_space_constraint(a, pltpu.HBM) if k in anywhere else a for k, a in enumerate(args)]
    return pl.pallas_call(
        kernel,
        in_specs=[
            pl.BlockSpec(memory_space=pltpu.HBM) if k in anywhere else vmem for k in range(len(args))
        ],
        out_specs=[vmem for _ in outs],
        out_shape=[jax.ShapeDtypeStruct(*o) for o in outs],
        scratch_shapes=[s if not isinstance(s, tuple) else pltpu.VMEM(*s) for s in scratch],
        compiler_params=pltpu.CompilerParams(vmem_limit_bytes=24 * 1024 * 1024),
        cost_estimate=None
        if cost is None
        else pl.CostEstimate(flops=0, transcendentals=0, bytes_accessed=int(cost * 3.0e6)),
        input_output_aliases=aliases,
        name=name,
    )(*args)


def local(
    value_input, state_input, step_raw, upstream, step_bias, decay_log, skip_gain,
    value_kernel, value_offset, state_kernel, state_offset,
):
    count = lax.axis_size("ctx")
    chips = count // CORES
    per_half = count // HALVES

    def send(x, pairs):
        return lax.ppermute(x, "ctx", pairs)

    swap_pairs = [(i, i ^ 1) for i in range(count)]

    def around(i, shift):
        half, at, c = i // (RING * CORES), (i // CORES) % RING, i % CORES
        return (half * RING + (at + shift) % RING) * CORES + c

    def exchange(parts, sign):
        out = list(parts)
        for k in (2, 1, 3):
            out[k] = send(parts[k], [(i, around(i, sign * k)) for i in range(count)])
        return out

    row = lambda x: x.reshape(1, -1)
    v, s, r, g = value_input[0], state_input[0], step_raw[0].T, upstream[0]
    bias, rate_log, skip = row(step_bias), row(decay_log), row(skip_gain)
    joint = WIDE + 2 * STATE + 128
    tall = (ROWS, WIDE)
    narrow = (ROWS, 128)
    marked = ((STATE + TAIL, PART), bf16)
    state_part = ((STATE, PART), bf16)
    sems = pltpu.SemaphoreType.DMA

    message, halo_a, halo_b, halos = call(
        pack_kernel, [v, s, r],
        [((TOK, joint), bf16), ((HALO, WIDE + 2 * STATE), bf16), ((HALO, WIDE + 2 * STATE), bf16),
         ((2 * HALO, WIDE + 2 * STATE), bf16)],
        [((2 * HEADS, TOK), bf16), sems((11,))], "pack", (0, 1, 2),
    )
    middle = per_half - 1
    relayed = lax.ppermute(
        halos, ("pipe", "ctx"),
        [(p * count + middle, (1 - p) * count + middle) for p in range(2)],
    )
    message = send(message, swap_pairs)
    halo_a, halo_b = call(
        relay_kernel, [halo_a, halo_b, relayed], [((HALO, WIDE + 2 * STATE), bf16)] * 2, (), "relay"
    )

    def onward(x, step):
        pairs = []
        for p in range(2):
            for k in range(chips - 1):
                source = k * CORES + 1
                held = 1 - p if source == middle else p
                pairs.append((held * count + source, p * count + source + step))
        return lax.ppermute(x, ("pipe", "ctx"), pairs)

    g_own, g_in = call(
        pack_grad_kernel, [g], [((TOK, WIDE), bf16)] * 2, [sems((2,))], "pack_grad", (0,)
    )
    g_own, g_in, halo_a, halo_b = lax.optimization_barrier((g_own, g_in, halo_a, halo_b))
    halo_a = onward(halo_a, 2)
    halo_b = onward(halo_b, 1)
    g_own = lax.ppermute(g_own, "pipe", [(0, 1), (1, 0)])
    g_in = lax.ppermute(
        g_in,
        ("pipe", "ctx"),
        [(p * count + i, (1 - p) * count + (i ^ 1)) for p in range(2) for i in range(count)],
    )
    ones = call(ones_kernel, [], [((128, WIDE), bf16)], name="ones")[0]
    taps = [value_kernel, row(value_offset), state_kernel, row(state_offset)]
    half_done = [
        (tall, bf16), (tall, bf16), ((ROWS, 2 * STATE), bf16), (tall, f32),
        ((ROWS, 2 * STATE), f32),
    ]
    *begun, spread_scale, delta, within, sig, top, stop = call(
        first_kernel,
        [v, s, r, message, bias, rate_log] + taps + [ones],
        half_done + [(tall, f32)] + [(narrow, f32)] * 3
        + [((TAIL, WIDE), f32), ((TAIL, 2 * STATE), f32)],
        [((ROWS + 8, WIDE), f32), ((ROWS + 8, 2 * STATE), f32), (narrow, f32)],
        "first", cost=8,
    )
    m0, m1, m2, m3, x, xs, bc, pre, spre = call(
        state_kernel_body,
        [halo_a, halo_b, top, stop, spread_scale, within] + taps + [ones] + begun,
        [marked] * 4 + half_done, (), "states", cost=2,
        aliases={11 + j: 4 + j for j in range(5)},
    )
    marks = exchange((m0, m1, m2, m3), 1)
    sx, k, sbc = call(
        slope_kernel, [pre, spre, spread_scale],
        [(tall, bf16), (tall, bf16), ((ROWS, 2 * STATE), bf16)], (), "slopes", cost=2,
    )
    g_own, sx = lax.optimization_barrier((g_own, sx))
    d0, d1, d2, d3, dy, dye = call(
        second_kernel, [g_own, g_in, bc, within, ones],
        [state_part] * 4 + [(tall, bf16)] * 2, [(tall, f32)], "second", cost=4,
    )
    grads = exchange((d0, d1, d2, d3), 1)
    edge = call(
        functools.partial(edge_kernel, False), marks + marks, [state_part], (), "edge_forward",
        cost=2,
    )[0]
    edge_in = send(edge, [(i, i + per_half) for i in range(per_half)])
    half_wide = (ROWS, WIDE // 2)
    inner_scratch = [
        (half_wide, f32), ((8, WIDE // 2), f32), ((HEADS // 2, 8, ROWS), f32), ((128, ROWS), f32),
        ((ROWS, ROWS), f32),
    ]
    dy_now, _ = lax.optimization_barrier((dy, edge))
    base_0, dbcs, diff, vsum = call(
        functools.partial(inner_kernel, 0), [x, dy_now, bc, delta, within, sx, skip, ones],
        [(half_wide, f32), ((ROWS, ROWS), f32), (narrow, f32), (narrow, f32)],
        inner_scratch, "inner_0", cost=6,
    )
    edge_in, diff = lax.optimization_barrier((edge_in, diff))
    steps = call(
        functools.partial(scan_kernel, False), marks + marks + [edge_in],
        [state_part] * 4, (), "scan_forward", cost=3,
    )
    carried = exchange(steps, -1)
    *grads, _ = lax.optimization_barrier((*grads, base_0))
    edge_back = call(
        functools.partial(edge_kernel, True), marks + grads, [state_part], (), "edge_back", cost=2,
    )[0]
    edge_back = send(edge_back, [(i + per_half, i) for i in range(per_half)])
    steps_back = call(
        functools.partial(scan_kernel, True), marks + grads + [edge_back],
        [state_part] * 4, (), "scan_back", cost=3,
    )
    dy_now, _ = lax.optimization_barrier((dy, steps_back[0]))
    base_1, dbc, diff, vsum, base_top = call(
        functools.partial(inner_kernel, 1),
        [x, dy_now, bc, delta, within, sx, skip, ones, dbcs, diff, vsum, base_0],
        [(half_wide, f32), ((ROWS, 2 * STATE), f32), (narrow, f32), (narrow, f32),
         ((8, WIDE), f32)],
        inner_scratch + [((ROWS, ROWS), f32)], "inner_1", cost=6,
    )
    back = exchange(steps_back, -1)
    diff, dread, held = call(
        carry_kernel, list(carried) + [bc, dye, dbc, diff, ones],
        [(narrow, f32), ((ROWS, STATE), f32), ((STATE, WIDE), bf16)], (), "carry", cost=4,
    )
    head = call(
        head_kernel, list(back) + [bc, xs, k, base_top, sbc, dread, dbc],
        [((8, WIDE + 2 * STATE), bf16)], (), "head", cost=1,
    )[0]
    back[0], head = lax.optimization_barrier((back[0], head))
    head = send(head, [(i, i - CORES) for i in range(CORES, count)])
    e, es, steps = call(
        last_kernel,
        list(back)
        + [held, bc, xs, k, base_0, base_1, sbc, delta, within, sig, diff, vsum, dread, dbc,
           rate_log, ones],
        [(tall, f32), ((ROWS, 2 * STATE), f32), (narrow, f32)],
        [((STATE, WIDE), bf16)], "last", cost=5,
    )
    vg_own, sg_own, st_own, message = call(
        back_kernel, [e, es, steps, head, value_kernel, state_kernel],
        [((TOK, WIDE), bf16), ((TOK, 2 * STATE), bf16), ((TOK, 128), bf16),
         ((TOK, joint), bf16)],
        [(tall, bf16), ((ROWS, 2 * STATE), bf16)], "back", cost=3,
    )
    message = send(message, swap_pairs)
    value_out, state_out, step_out = call(
        join_kernel, [vg_own, sg_own, st_own, message],
        [((TOK, 2 * WIDE), bf16), ((TOK, 4 * STATE), bf16), ((2 * HEADS, TOK), bf16)],
        (), "join",
    )
    return value_out[None], state_out[None], step_out.T[None]


def solution(mesh):
    wide = P("pipe", "ctx", "tp")
    placed = (wide, wide, wide, wide, P("tp"), P("tp"), P("tp"), P(None, "tp"), P("tp"), P(None, "tp"), P("tp"))
    return jax.shard_map(
        local, mesh=mesh, in_specs=placed, out_specs=(wide, wide, wide), check_vma=False
    )
```

```python
import functools

import jax
import jax.numpy as jnp
from jax import lax
from jax.experimental import pallas as pl
from jax.experimental.pallas import tpu as pltpu
from jax.sharding import PartitionSpec as P

HEAD_DIM = 64
STATE = 256
CONV = 4
CORES = 2
RING = 4
HALVES = 2
f32 = jnp.float32
bf16 = jnp.bfloat16
HIGH = lax.Precision.HIGHEST

TOK = 128
ROWS = TOK * CORES
HEADS = 32
WIDE = HEADS * HEAD_DIM
PART = WIDE // RING
TAIL = 16
HALO = 8
LOG2E = 1.4426950408889634


def place():
    index = lax.axis_index("ctx")
    return lax.rem(index, CORES), lax.rem(lax.div(index, CORES), RING)


def rows_of(core):
    return (
        pl.ds(pl.multiple_of(core * TOK, TOK), TOK),
        pl.ds(pl.multiple_of((1 - core) * TOK, TOK), TOK),
    )


def block128(b, start=0):
    return pl.ds(pl.multiple_of(start + b * 128, 128), 128)


def head_columns(ring, slot):
    return pl.ds(pl.multiple_of(lax.rem(ring + slot, RING) * PART, PART), PART)


def nn(a, b, precision=None):
    return lax.dot_general(
        a, b, (((1,), (0,)), ((), ())), precision=precision, preferred_element_type=f32
    )


def nt(a, b):
    return lax.dot_general(a, b, (((1,), (1,)), ((), ())), preferred_element_type=f32)


def iota(shape, axis):
    return lax.broadcasted_iota(jnp.int32, shape, axis)


def split3(x):
    high = x.astype(bf16).astype(f32)
    rest = x - high
    mid = rest.astype(bf16).astype(f32)
    low = rest - mid
    part = iota(x.shape, 1) // HEADS
    picked = jnp.where(part == 0, high, jnp.where(part == 1, mid, jnp.where(part == 2, low, 0.0)))
    return picked.astype(bf16)


def head_sum(x, ones):
    high = x.astype(bf16)
    low = (x - high.astype(f32)).astype(bf16)
    return nt(high, ones) + nt(low, ones)


def tiled_heads(x, group):
    x = x.astype(f32)
    mine = jnp.where(group == 0, x[:, :HEADS], x[:, HEADS:])
    return jnp.concatenate([mine] * 4, axis=1)


def tiled_steps(x, group):
    x = x.astype(f32)
    mine = jnp.where(group == 0, x[:HEADS], x[HEADS:])
    return jnp.concatenate([mine] * 4, axis=0).T


def softplus(x):
    u = jnp.exp(-jnp.abs(x))
    small = u * (1.0 - u * (0.5 - u * (1.0 / 3.0 - u * 0.25)))
    return jnp.maximum(x, 0.0) + jnp.where(u < 0.01, small, jnp.log(1.0 + u))


def sigmoid(x):
    return 1.0 / (1.0 + jnp.exp(-x))


def sigmoid_by_tanh(x):
    return 0.5 + 0.5 * jnp.tanh(0.5 * x)


def run_copies(pairs, sems):
    copies = [pltpu.make_async_copy(a, b, sems.at[k]) for k, (a, b) in enumerate(pairs)]
    for copy in copies:
        copy.start()
    return copies


def pack_kernel(v, s, r, message, halo_a, halo_b, halos, r_here, sems):
    core, ring = place()
    there = 1 - core
    pairs = []
    rows = pl.ds(TOK - HALO, HALO)
    for group, halo in ((1, halo_a), (0, halo_b)):
        pairs.append((v.at[rows, pl.ds(group * WIDE, WIDE)], halo.at[:, pl.ds(0, WIDE)]))
        pairs.append(
            (s.at[rows, pl.ds(group * 2 * STATE, 2 * STATE)], halo.at[:, pl.ds(WIDE, 2 * STATE)])
        )
    v_there = pl.ds(pl.multiple_of(there * WIDE, 128), WIDE)
    s_there = pl.ds(pl.multiple_of(there * 2 * STATE, 128), 2 * STATE)
    for k, group in enumerate((1, 0)):
        at = pl.ds(k * HALO, HALO)
        pairs.append((v.at[rows, pl.ds(group * WIDE, WIDE)], halos.at[at, pl.ds(0, WIDE)]))
        pairs.append(
            (s.at[rows, pl.ds(group * 2 * STATE, 2 * STATE)], halos.at[at, pl.ds(WIDE, 2 * STATE)])
        )
    pairs.append((v.at[:, v_there], message.at[:, pl.ds(0, WIDE)]))
    pairs.append((s.at[:, s_there], message.at[:, pl.ds(WIDE, 2 * STATE)]))
    pairs.append((r, r_here))
    copies = run_copies(pairs, sems)
    copies.pop().wait()
    message[:, WIDE + 2 * STATE :] = tiled_steps(r_here[...], there).astype(bf16)
    for copy in copies:
        copy.wait()


def relay_kernel(halo_a, halo_b, relayed, out_a, out_b):
    index = lax.axis_index("ctx")
    handing = index == CORES * RING - 1
    out_a[...] = jnp.where(
        handing, relayed[:HALO].astype(f32), halo_a[...].astype(f32)
    ).astype(bf16)
    out_b[...] = jnp.where(
        handing, relayed[HALO:].astype(f32), halo_b[...].astype(f32)
    ).astype(bf16)


def pack_grad_kernel(g, own, across, sems):
    core, ring = place()
    copies = [
        pltpu.make_async_copy(
            g.at[:, pl.ds(pl.multiple_of(group * WIDE, 128), WIDE)], out, sems.at[k]
        )
        for k, (group, out) in enumerate(((core, own), (1 - core, across)))
    ]
    for copy in copies:
        copy.start()
    for copy in copies:
        copy.wait()


def ones_kernel(out):
    rows = iota((128, WIDE), 0) % HEADS
    cols = iota((128, WIDE), 1) // HEAD_DIM
    out[...] = jnp.where(rows == cols, 1.0, 0.0).astype(bf16)


def first_kernel(
    v, s, r, message, step_bias, decay_log, v_tap, v_off, s_tap, s_off, ones,
    x_out, xs_out, bc_out, pre_out, spre_out, wide, delta_out, within_out, sig_out, top_out,
    stop_out,
    buf, sbuf, raw,
):
    core, ring = place()
    mine, other = rows_of(core)
    raw[mine, :] = tiled_steps(r[...], core)
    raw[other, :] = message[:, WIDE + 2 * STATE :].astype(f32)
    pre = raw[...] + tiled_heads(step_bias[...], core)
    delta = softplus(pre)
    rate = -jnp.exp(tiled_heads(decay_log[...], core))
    lower = jnp.where(iota((ROWS, ROWS), 0) >= iota((ROWS, ROWS), 1), 1.0, 0.0).astype(f32)
    within = nn(lower, delta * rate, HIGH)
    delta_out[...] = delta
    within_out[...] = within
    sig_out[...] = sigmoid(pre)
    total = within[ROWS - 1 : ROWS, :]
    wide[...] = nn(split3(delta * jnp.exp(total - within)), ones[...])

    below = pl.ds(pl.multiple_of(8 + core * TOK, 8), TOK)
    above = pl.ds(pl.multiple_of(8 + (1 - core) * TOK, 8), TOK)
    v_mine = pl.ds(pl.multiple_of(core * WIDE, 128), WIDE)
    s_mine = pl.ds(pl.multiple_of(core * 2 * STATE, 128), 2 * STATE)
    buf[below, :] = v[:, v_mine].astype(f32)
    buf[above, :] = message[:, :WIDE].astype(f32)
    sbuf[below, :] = s[:, s_mine].astype(f32)
    sbuf[above, :] = message[:, WIDE : WIDE + 2 * STATE].astype(f32)
    buf[0:8, :] = jnp.zeros((8, WIDE), f32)
    sbuf[0:8, :] = jnp.zeros((8, 2 * STATE), f32)
    top_out[...] = buf[8 : 8 + TAIL, :]
    stop_out[...] = sbuf[8 : 8 + TAIL, :]

    def conv(source, tap, off, b, width):
        cols, par = block128(b), block128(b, core * width)
        acc = off[:, par] + tap[0:1, par] * source[5 : 5 + ROWS, cols]
        for j in range(1, CONV):
            acc = acc + tap[j : j + 1, par] * source[5 + j : 5 + j + ROWS, cols]
        return acc

    def state_block(b, carry):
        cols = block128(b)
        acc = conv(sbuf, s_tap, s_off, b, 2 * STATE)
        spre_out[:, cols] = acc
        bc_out[:, cols] = (acc * sigmoid_by_tanh(acc)).astype(bf16)
        return carry

    lax.fori_loop(0, 4, state_block, 0)

    def value_block(b, carry):
        cols = block128(b)
        acc = conv(buf, v_tap, v_off, b, WIDE)
        pre_out[:, cols] = acc
        post = (acc * sigmoid_by_tanh(acc)).astype(bf16)
        x_out[:, cols] = post
        xs_out[:, cols] = (post.astype(f32) * wide[:, cols]).astype(bf16)
        return carry

    lax.fori_loop(0, 16, value_block, 0)


def state_kernel_body(
    halo_a, halo_b, top, stop, wide, within, v_tap, v_off, s_tap, s_off, ones,
    x_in, xs_in, bc_in, pre_in, spre_in,
    m0, m1, m2, m3, x_out, xs_out, bc_out, pre_out, spre_out,
):
    core, ring = place()
    halo = halo_a[...].astype(f32) + halo_b[...].astype(f32)

    def first_rows(source, start, tap, off, c, width):
        par = pl.ds(pl.multiple_of(core * width + c, 128), PART)
        both = jnp.concatenate(
            [halo[:, start + c : start + c + PART], source[:, c : c + PART]], axis=0
        )
        acc = off[:, par] + tap[0:1, par] * both[5 : 5 + TAIL]
        for j in range(1, CONV):
            acc = acc + tap[j : j + 1, par] * both[5 + j : 5 + j + TAIL]
        return acc, (acc * sigmoid_by_tanh(acc)).astype(bf16)

    for c in range(0, WIDE, PART):
        cols = slice(c, c + PART)
        acc, post = first_rows(top, 0, v_tap, v_off, c, WIDE)
        pre_out[0:TAIL, cols] = acc
        x_out[0:TAIL, cols] = post
        xs_out[0:TAIL, cols] = (post.astype(f32) * wide[0:TAIL, cols]).astype(bf16)
    acc, post = first_rows(stop, WIDE, s_tap, s_off, 0, 2 * STATE)
    spre_out[0:TAIL, :] = acc
    bc_out[0:TAIL, :] = post
    total = within[ROWS - 1 : ROWS, :]
    write_t = bc_out[:, :STATE].astype(f32).T.astype(bf16)
    total_parts = split3(jnp.broadcast_to(total, (8, 128)))
    for slot, out in enumerate((m0, m1, m2, m3)):
        cols = head_columns(ring, slot)
        out[0:STATE, :] = nn(write_t, xs_out[:, cols]).astype(bf16)
        full = nn(total_parts, ones[:, cols])[0:1, :]
        high = full.astype(bf16).astype(f32)
        mid = (full - high).astype(bf16).astype(f32)
        low = full - high - mid
        row = iota((TAIL, PART), 0)
        out[STATE : STATE + TAIL, :] = jnp.where(
            row == 0, high, jnp.where(row == 1, mid, jnp.where(row == 2, low, 0.0))
        ).astype(bf16)


def slope_kernel(pre, spre, wide, sx_out, k_out, sbc_out):
    def slope(acc):
        sig = sigmoid_by_tanh(acc)
        return sig * (1.0 + acc * (1.0 - sig))

    def value_block(b, carry):
        cols = block128(b)
        out = slope(pre[:, cols])
        sx_out[:, cols] = out.astype(bf16)
        k_out[:, cols] = (out * wide[:, cols]).astype(bf16)
        return carry

    lax.fori_loop(0, 16, value_block, 0)

    def state_block(b, carry):
        cols = block128(b)
        sbc_out[:, cols] = slope(spre[:, cols]).astype(bf16)
        return carry

    lax.fori_loop(0, 4, state_block, 0)


def ring_totals(parts):
    out = []
    for part in parts:
        rows = part[STATE : STATE + TAIL, :].astype(f32)
        out.append(rows[0:1] + rows[1:2] + rows[2:3])
    return out


def between(totals, places, low, high):
    out = jnp.zeros_like(totals[0])
    for total, p in zip(totals, places):
        inside = jnp.logical_and(p > low, p < high)
        out = out + total * jnp.where(inside, 1.0, 0.0)
    return out


def edge_kernel(back, m0, m1, m2, m3, d0, d1, d2, d3, out):
    core, ring = place()
    places = [lax.rem(ring + RING - s, RING) for s in range(RING)]
    totals = ring_totals((m0, m1, m2, m3))
    weights = []
    for p in places:
        low, high = (-1, p) if back else (p, RING)
        weights.append(jnp.exp(between(totals, places, low, high)))
    for c in range(0, PART, 128):
        cols = slice(c, c + 128)
        acc = None
        for src, weight in zip((d0, d1, d2, d3), weights):
            term = weight[:, cols] * src[0:STATE, cols].astype(f32)
            acc = term if acc is None else acc + term
        out[:, cols] = acc.astype(bf16)


def scan_kernel(back, m0, m1, m2, m3, d0, d1, d2, d3, edge, o0, o1, o2, o3):
    core, ring = place()
    places = [lax.rem(ring + RING - s, RING) for s in range(RING)]
    totals = ring_totals((m0, m1, m2, m3))
    weights = []
    for here in places:
        low, high = (here, RING) if back else (-1, here)
        row = [jnp.exp(between(totals, places, low, high))]
        for p in places:
            low, high, live = (here, p, p > here) if back else (p, here, p < here)
            row.append(jnp.exp(between(totals, places, low, high)) * jnp.where(live, 1.0, 0.0))
        weights.append(row)
    for c in range(0, PART, 128):
        cols = slice(c, c + 128)
        for r in range(0, STATE, 64):
            rows = slice(r, r + 64)
            parts = [edge[rows, cols].astype(f32)]
            parts += [src[rows, cols].astype(f32) for src in (d0, d1, d2, d3)]
            for out, row in zip((o0, o1, o2, o3), weights):
                acc = row[0][:, cols] * parts[0]
                for weight, part in zip(row[1:], parts[1:]):
                    acc = acc + weight[:, cols] * part
                out[rows, cols] = acc.astype(bf16)


def second_kernel(g_own, g_in, bc, within, ones, d0, d1, d2, d3, dy_out, dye_out, wide):
    core, ring = place()
    mine, other = rows_of(core)
    dy_out[mine, :] = g_own[...]
    dy_out[other, :] = g_in[...]
    wide[...] = nn(split3(jnp.exp(within[...])), ones[...])
    read_t = bc[:, STATE:].astype(f32).T.astype(bf16)

    def block(b, carry):
        cols = block128(b)
        dye_out[:, cols] = (dy_out[:, cols].astype(f32) * wide[:, cols]).astype(bf16)
        return carry

    lax.fori_loop(0, 16, block, 0)
    for slot, out in enumerate((d0, d1, d2, d3)):
        out[...] = nn(read_t, dye_out[:, head_columns(ring, slot)]).astype(bf16)


def inner_kernel(part, x, dy, bc, delta, within, sx, skip_gain, ones, *refs):
    if part == 0:
        base_out, dbcs, diff_out, vsum_out = refs[:4]
        scratch = refs[4:]
    else:
        dbcs_in, diff_in, vsum_in, base_in = refs[:4]
        base_out, dbc_out, diff_out, vsum_out, top_out = refs[4:9]
        scratch = refs[9:]
        dbcs = scratch[-1]
    wide, skips, within_3, row_sum, bcs = scratch[:5]
    core, ring = place()
    half = ROWS // 2
    low_col, low_head = part * (WIDE // 2), part * (HEADS // 2)
    own = ones[:, low_col : low_col + WIDE // 2]
    wide[...] = nn(split3(delta[...]), own)
    skip = jnp.broadcast_to(tiled_heads(skip_gain[...], core), (8, 128))
    skips[...] = nn(split3(skip), own)
    scaled = within[...] * LOG2E
    lane_part = iota((ROWS, 128), 1) // HEADS
    left = jnp.where(lane_part == 3, 1.0, -split3(scaled).astype(f32)).astype(bf16)
    parts_t = split3(scaled).astype(f32).T
    for h in range(HEADS // 2):
        for piece in range(3):
            at = piece * HEADS + low_head + h
            within_3[h, piece : piece + 1, :] = parts_t[at : at + 1, :]
        within_3[h, 3:8, :] = jnp.zeros((5, ROWS), f32)
    write, read = bc[:, :STATE], bc[:, STATE:]
    bcs[...] = nt(write, read)
    if part == 0:
        dbcs[...] = jnp.zeros_like(dbcs)
        diff_out[...] = jnp.zeros_like(diff_out)
        vsum_out[...] = jnp.zeros_like(vsum_out)
    else:
        dbcs[...] = dbcs_in[...]
        diff_out[...] = diff_in[...]
        vsum_out[...] = vsum_in[...]
    row_sum[...] = jnp.zeros_like(row_sum)
    keep = iota((half, half), 1) >= iota((half, half), 0)
    lanes = iota((ROWS, 128), 1)
    first = lanes < HEAD_DIM
    row_head = iota((96, ROWS), 0) % HEADS
    pad = jnp.zeros((24, ROWS), f32)

    def pair(b, carry):
        cols, here = block128(b, low_col), block128(b)
        xb = x[:, cols].astype(f32)
        xd = (xb * wide[:, here]).astype(bf16)
        grad = dy[:, cols]
        zero = jnp.zeros_like(grad)
        top = jnp.zeros((half, 128), f32)
        bot = jnp.zeros((half, 128), f32)
        col_total = jnp.zeros((ROWS, 128), f32)
        grads_of = [0.0, 0.0, 0.0]
        for e in range(2):
            h = low_head + 2 * b + e
            g = jnp.where(first, grad, zero) if e == 0 else jnp.where(first, zero, grad)
            right = jnp.concatenate(
                [jnp.where(row_head == h, 1.0, 0.0), within_3[2 * b + e], pad], axis=0
            ).astype(bf16)
            gap0 = nn(left[:half], right)
            gap1 = nn(left[half:], right[:, half:])
            dm0 = nt(xd[:half], g)
            dm1 = nt(xd[half:], g[half:])
            blocks = (
                (jnp.where(keep, gap0[:, :half], -jnp.inf), dm0[:, :half], 0, 0),
                (gap0[:, half:], dm0[:, half:], 0, 1),
                (jnp.where(keep, gap1, -jnp.inf), dm1, 1, 1),
            )
            ps, ms = [], []
            for k, (gap, dm, r, c) in enumerate(blocks):
                decay = jnp.exp2(gap)
                m = decay * bcs[r * half : (r + 1) * half, c * half : (c + 1) * half]
                grads_of[k] = grads_of[k] + dm * decay
                ps.append(dm * m)
                ms.append(m.astype(bf16))
            sum_rows = jnp.concatenate(
                [
                    jnp.sum(ps[0], axis=0, keepdims=True),
                    jnp.sum(ps[1] + ps[2], axis=0, keepdims=True),
                ],
                axis=1,
            )
            row_sum[pl.ds(h, 1), :] = sum_rows
            top = top + nn(ms[0], g[:half]) + nn(ms[1], g[half:])
            bot = bot + nn(ms[2], g[half:])
            col = jnp.concatenate(
                [
                    jnp.sum(ps[0] + ps[1], axis=1, keepdims=True),
                    jnp.sum(ps[2], axis=1, keepdims=True),
                ],
                axis=0,
            )
            col_total = col_total + jnp.where(lanes % HEADS == h, col, 0.0)
        for k, (r, c) in enumerate(((0, 0), (0, 1), (1, 1))):
            rs, cs = slice(r * half, (r + 1) * half), slice(c * half, (c + 1) * half)
            dbcs[rs, cs] = dbcs[rs, cs] + grads_of[k]
        u = jnp.concatenate([top, bot], axis=0)
        diff_out[...] = diff_out[...] - col_total
        vsum_out[...] = vsum_out[...] + head_sum(xb * u, ones[:, cols])
        base_out[:, here] = (
            wide[:, here] * u + skips[0:1, here] * grad.astype(f32)
        ) * sx[:, cols].astype(f32)
        return carry

    lax.fori_loop(0, 8, pair, 0)
    for t in range(1, 4):
        row_sum[t * HEADS : (t + 1) * HEADS, :] = row_sum[0:HEADS, :]
    diff_out[...] = diff_out[...] + row_sum[...].T
    if part == 1:
        grad = dbcs[...]
        dbc_out[:, :STATE] = nn(grad.astype(bf16), read)
        dbc_out[:, STATE:] = nn(grad.T.astype(bf16), write)
        top_out[:, : WIDE // 2] = base_in[0:8, :]
        top_out[:, WIDE // 2 :] = base_out[0:8, :]


def carry_kernel(c0, c1, c2, c3, bc, dye, dbc, diff, ones, diff_out, dread_out, carried_out):
    core, ring = place()
    for slot, src in enumerate((c0, c1, c2, c3)):
        carried_out[:, head_columns(ring, slot)] = src[...]
    read = bc[:, STATE:]
    dread_out[...] = dbc[:, STATE:] + nt(dye[...], carried_out[...])
    outer = diff[...]
    for b in range(4):
        cols = slice(b * PART, (b + 1) * PART)
        part = nn(read, carried_out[:, cols]) * dye[:, cols].astype(f32)
        outer = outer + head_sum(part, ones[:, cols])
    later = jnp.where(iota((ROWS, ROWS), 1) >= iota((ROWS, ROWS), 0), 1.0, 0.0).astype(f32)
    diff_out[...] = nn(later, outer, HIGH)


def last_kernel(
    g0, g1, g2, g3, carried, bc, xs, k, base_0, base_1, sbc, delta, within, sig, diff, vsum,
    dread, dbc, decay_log, ones,
    e_out, es_out, steps_out,
    gbuf,
):
    core, ring = place()
    for slot, src in enumerate((g0, g1, g2, g3)):
        gbuf[:, head_columns(ring, slot)] = src[...]
    write = bc[:, :STATE]
    rsum = jnp.zeros((ROWS, 128), f32)
    tsum = jnp.zeros((8, 128), f32)
    for b in range(4):
        cols = slice(b * PART, (b + 1) * PART)
        grad = gbuf[:, cols]
        through = nn(write, grad)
        rsum = rsum + head_sum(xs[:, cols].astype(f32) * through, ones[:, cols])
        base = (base_0, base_1)[b // 2][:, (b % 2) * PART : (b % 2 + 1) * PART]
        e_out[:, cols] = base + k[:, cols].astype(f32) * through
        both = jnp.sum(
            grad.astype(f32) * carried[:, cols].astype(f32), axis=0, keepdims=True
        )
        tsum = tsum + head_sum(jnp.broadcast_to(both, (8, PART)), ones[:, cols])
    total = within[ROWS - 1 : ROWS, :]
    dtotal = tsum[0:1, :] * jnp.exp(total)
    ra, rb = iota((ROWS, ROWS), 0), iota((ROWS, ROWS), 1)
    earlier = jnp.where(rb < ra, 1.0, 0.0).astype(f32)
    da = diff[...] + nn(earlier, rsum, HIGH) + dtotal
    rate = -jnp.exp(tiled_heads(decay_log[...], core))
    steps_out[...] = (vsum[...] + rsum / delta[...] + rate * da) * sig[...]
    dwrite = dbc[:, :STATE] + nt(xs[...], gbuf[...])
    es_out[:, :STATE] = dwrite * sbc[:, :STATE].astype(f32)
    es_out[:, STATE:] = dread[...] * sbc[:, STATE:].astype(f32)


def back_kernel(
    e, es, steps, head, v_tap, s_tap, vg_own, sg_own, st_own, message, back, sback
):
    core, ring = place()
    mine, other = rows_of(core)
    body = ROWS - TAIL

    def conv(source, start, tap, b, width, out):
        cols, par = block128(b), block128(b, core * width)
        edge = jnp.concatenate(
            [source[body:, cols], head[:, block128(b, start)].astype(f32)], axis=0
        )
        acc = tap[CONV - 1 : CONV, par] * source[0:body, cols]
        end = tap[CONV - 1 : CONV, par] * edge[0:TAIL]
        for shift in range(1, CONV):
            weight = tap[CONV - 1 - shift : CONV - shift, par]
            acc = acc + weight * source[shift : shift + body, cols]
            end = end + weight * edge[shift : shift + TAIL]
        out[0:body, cols] = acc.astype(bf16)
        out[body:, cols] = end.astype(bf16)

    def value_block(b, carry):
        conv(e, 0, v_tap, b, WIDE, back)
        return carry

    lax.fori_loop(0, 16, value_block, 0)

    def state_block(b, carry):
        conv(es, WIDE, s_tap, b, 2 * STATE, sback)
        return carry

    lax.fori_loop(0, 4, state_block, 0)
    vg_own[...] = back[mine, :]
    message[:, :WIDE] = back[other, :]
    sg_own[...] = sback[mine, :]
    message[:, WIDE : WIDE + 2 * STATE] = sback[other, :]
    st_own[...] = steps[mine, :].astype(bf16)
    message[:, WIDE + 2 * STATE :] = steps[other, :].astype(bf16)


def head_kernel(g0, g1, g2, g3, bc, xs, k, base_top, sbc, dread, dbc, out):
    core, ring = place()
    write = bc[0:TAIL, :STATE]
    dwrite = dbc[0:8, :STATE]
    for slot, src in enumerate((g0, g1, g2, g3)):
        cols = head_columns(ring, slot)
        grad = src[...]
        through = nn(write, grad)[0:8]
        out[:, cols] = (
            base_top[:, cols] + k[0:TAIL, cols].astype(f32)[0:8] * through
        ).astype(bf16)
        dwrite = dwrite + nt(xs[0:TAIL, cols], grad)[0:8]
    slope = sbc[0:TAIL, :].astype(f32)[0:8]
    out[:, WIDE : WIDE + STATE] = (dwrite * slope[:, :STATE]).astype(bf16)
    out[:, WIDE + STATE :] = (dread[0:8, :] * slope[:, STATE:]).astype(bf16)


def join_kernel(v_own, s_own, t_own, message, v_out, s_out, t_out):
    core, ring = place()

    def place_in(out, own, arrived, width):
        out[:, pl.ds(pl.multiple_of(core * width, 128), width)] = own
        out[:, pl.ds(pl.multiple_of((1 - core) * width, 128), width)] = arrived

    place_in(v_out, v_own[...], message[:, :WIDE], WIDE)
    place_in(s_out, s_own[...], message[:, WIDE : WIDE + 2 * STATE], 2 * STATE)
    own = t_own[...].astype(f32).T[:HEADS]
    arrived = message[:, WIDE + 2 * STATE :].astype(f32).T[:HEADS]
    low = jnp.where(core == 0, own, arrived)
    high = jnp.where(core == 0, arrived, own)
    t_out[...] = jnp.concatenate([low, high], axis=0).astype(bf16)


def call(kernel, args, outs, scratch=(), name=None, anywhere=(), cost=None, aliases={}):
    vmem = pl.BlockSpec(memory_space=pltpu.VMEM)
    args = [pltpu.with_memory_space_constraint(a, pltpu.HBM) if k in anywhere else a for k, a in enumerate(args)]
    return pl.pallas_call(
        kernel,
        in_specs=[
            pl.BlockSpec(memory_space=pltpu.HBM) if k in anywhere else vmem for k in range(len(args))
        ],
        out_specs=[vmem for _ in outs],
        out_shape=[jax.ShapeDtypeStruct(*o) for o in outs],
        scratch_shapes=[s if not isinstance(s, tuple) else pltpu.VMEM(*s) for s in scratch],
        compiler_params=pltpu.CompilerParams(vmem_limit_bytes=24 * 1024 * 1024),
        cost_estimate=None
        if cost is None
        else pl.CostEstimate(flops=0, transcendentals=0, bytes_accessed=int(cost * 3.0e6)),
        input_output_aliases=aliases,
        name=name,
    )(*args)


def local(
    value_input, state_input, step_raw, upstream, step_bias, decay_log, skip_gain,
    value_kernel, value_offset, state_kernel, state_offset,
):
    count = lax.axis_size("ctx")
    chips = count // CORES
    per_half = count // HALVES

    def send(x, pairs):
        return lax.ppermute(x, "ctx", pairs)

    swap_pairs = [(i, i ^ 1) for i in range(count)]

    def around(i, shift):
        half, at, c = i // (RING * CORES), (i // CORES) % RING, i % CORES
        return (half * RING + (at + shift) % RING) * CORES + c

    def exchange(parts, sign):
        out = list(parts)
        for k in (1, 2, 3):
            out[k] = send(parts[k], [(i, around(i, sign * k)) for i in range(count)])
        return out

    row = lambda x: x.reshape(1, -1)
    v, s, r, g = value_input[0], state_input[0], step_raw[0].T, upstream[0]
    bias, rate_log, skip = row(step_bias), row(decay_log), row(skip_gain)
    joint = WIDE + 2 * STATE + 128
    tall = (ROWS, WIDE)
    narrow = (ROWS, 128)
    marked = ((STATE + TAIL, PART), bf16)
    state_part = ((STATE, PART), bf16)
    sems = pltpu.SemaphoreType.DMA

    message, halo_a, halo_b, halos = call(
        pack_kernel, [v, s, r],
        [((TOK, joint), bf16), ((HALO, WIDE + 2 * STATE), bf16), ((HALO, WIDE + 2 * STATE), bf16),
         ((2 * HALO, WIDE + 2 * STATE), bf16)],
        [((2 * HEADS, TOK), bf16), sems((11,))], "pack", (0, 1, 2),
    )
    middle = per_half - 1
    relayed = lax.ppermute(
        halos, ("pipe", "ctx"),
        [(p * count + middle, (1 - p) * count + middle) for p in range(2)],
    )
    message = send(message, swap_pairs)
    halo_a, halo_b = call(
        relay_kernel, [halo_a, halo_b, relayed], [((HALO, WIDE + 2 * STATE), bf16)] * 2, (), "relay"
    )

    def onward(x, step):
        pairs = []
        for p in range(2):
            for k in range(chips - 1):
                source = k * CORES + 1
                held = 1 - p if source == middle else p
                pairs.append((held * count + source, p * count + source + step))
        return lax.ppermute(x, ("pipe", "ctx"), pairs)

    g_own, g_in = call(
        pack_grad_kernel, [g], [((TOK, WIDE), bf16)] * 2, [sems((2,))], "pack_grad", (0,)
    )
    g_own, g_in, halo_a, halo_b = lax.optimization_barrier((g_own, g_in, halo_a, halo_b))
    halo_a = onward(halo_a, 2)
    halo_b = onward(halo_b, 1)
    g_own = lax.ppermute(g_own, "pipe", [(0, 1), (1, 0)])
    g_in = lax.ppermute(
        g_in,
        ("pipe", "ctx"),
        [(p * count + i, (1 - p) * count + (i ^ 1)) for p in range(2) for i in range(count)],
    )
    ones = call(ones_kernel, [], [((128, WIDE), bf16)], name="ones")[0]
    taps = [value_kernel, row(value_offset), state_kernel, row(state_offset)]
    half_done = [
        (tall, bf16), (tall, bf16), ((ROWS, 2 * STATE), bf16), (tall, f32),
        ((ROWS, 2 * STATE), f32),
    ]
    *begun, spread_scale, delta, within, sig, top, stop = call(
        first_kernel,
        [v, s, r, message, bias, rate_log] + taps + [ones],
        half_done + [(tall, f32)] + [(narrow, f32)] * 3
        + [((TAIL, WIDE), f32), ((TAIL, 2 * STATE), f32)],
        [((ROWS + 8, WIDE), f32), ((ROWS + 8, 2 * STATE), f32), (narrow, f32)],
        "first", cost=8,
    )
    m0, m1, m2, m3, x, xs, bc, pre, spre = call(
        state_kernel_body,
        [halo_a, halo_b, top, stop, spread_scale, within] + taps + [ones] + begun,
        [marked] * 4 + half_done, (), "states", cost=2,
        aliases={11 + j: 4 + j for j in range(5)},
    )
    marks = exchange((m0, m1, m2, m3), 1)
    sx, k, sbc = call(
        slope_kernel, [pre, spre, spread_scale],
        [(tall, bf16), (tall, bf16), ((ROWS, 2 * STATE), bf16)], (), "slopes", cost=2,
    )
    g_own, sx = lax.optimization_barrier((g_own, sx))
    d0, d1, d2, d3, dy, dye = call(
        second_kernel, [g_own, g_in, bc, within, ones],
        [state_part] * 4 + [(tall, bf16)] * 2, [(tall, f32)], "second", cost=4,
    )
    grads = exchange((d0, d1, d2, d3), 1)
    edge = call(
        functools.partial(edge_kernel, False), marks + marks, [state_part], (), "edge_forward",
        cost=2,
    )[0]
    edge_in = send(edge, [(i, i + per_half) for i in range(per_half)])
    half_wide = (ROWS, WIDE // 2)
    inner_scratch = [
        (half_wide, f32), ((8, WIDE // 2), f32), ((HEADS // 2, 8, ROWS), f32), ((128, ROWS), f32),
        ((ROWS, ROWS), f32),
    ]
    dy_now, _ = lax.optimization_barrier((dy, edge))
    base_0, dbcs, diff, vsum = call(
        functools.partial(inner_kernel, 0), [x, dy_now, bc, delta, within, sx, skip, ones],
        [(half_wide, f32), ((ROWS, ROWS), f32), (narrow, f32), (narrow, f32)],
        inner_scratch, "inner_0", cost=6,
    )
    edge_in, diff = lax.optimization_barrier((edge_in, diff))
    steps = call(
        functools.partial(scan_kernel, False), marks + marks + [edge_in],
        [state_part] * 4, (), "scan_forward", cost=3,
    )
    carried = exchange(steps, -1)
    *grads, _ = lax.optimization_barrier((*grads, base_0))
    edge_back = call(
        functools.partial(edge_kernel, True), marks + grads, [state_part], (), "edge_back", cost=2,
    )[0]
    edge_back = send(edge_back, [(i + per_half, i) for i in range(per_half)])
    steps_back = call(
        functools.partial(scan_kernel, True), marks + grads + [edge_back],
        [state_part] * 4, (), "scan_back", cost=3,
    )
    dy_now, _ = lax.optimization_barrier((dy, steps_back[0]))
    base_1, dbc, diff, vsum, base_top = call(
        functools.partial(inner_kernel, 1),
        [x, dy_now, bc, delta, within, sx, skip, ones, dbcs, diff, vsum, base_0],
        [(half_wide, f32), ((ROWS, 2 * STATE), f32), (narrow, f32), (narrow, f32),
         ((8, WIDE), f32)],
        inner_scratch + [((ROWS, ROWS), f32)], "inner_1", cost=6,
    )
    back = exchange(steps_back, -1)
    diff, dread, held = call(
        carry_kernel, list(carried) + [bc, dye, dbc, diff, ones],
        [(narrow, f32), ((ROWS, STATE), f32), ((STATE, WIDE), bf16)], (), "carry", cost=4,
    )
    head = call(
        head_kernel, list(back) + [bc, xs, k, base_top, sbc, dread, dbc],
        [((8, WIDE + 2 * STATE), bf16)], (), "head", cost=1,
    )[0]
    back[0], head = lax.optimization_barrier((back[0], head))
    head = send(head, [(i, i - CORES) for i in range(CORES, count)])
    e, es, steps = call(
        last_kernel,
        list(back)
        + [held, bc, xs, k, base_0, base_1, sbc, delta, within, sig, diff, vsum, dread, dbc,
           rate_log, ones],
        [(tall, f32), ((ROWS, 2 * STATE), f32), (narrow, f32)],
        [((STATE, WIDE), bf16)], "last", cost=5,
    )
    vg_own, sg_own, st_own, message = call(
        back_kernel, [e, es, steps, head, value_kernel, state_kernel],
        [((TOK, WIDE), bf16), ((TOK, 2 * STATE), bf16), ((TOK, 128), bf16),
         ((TOK, joint), bf16)],
        [(tall, bf16), ((ROWS, 2 * STATE), bf16)], "back", cost=3,
    )
    message = send(message, swap_pairs)
    value_out, state_out, step_out = call(
        join_kernel, [vg_own, sg_own, st_own, message],
        [((TOK, 2 * WIDE), bf16), ((TOK, 4 * STATE), bf16), ((2 * HEADS, TOK), bf16)],
        (), "join",
    )
    return value_out[None], state_out[None], step_out.T[None]


def solution(mesh):
    wide = P("pipe", "ctx", "tp")
    placed = (wide, wide, wide, wide, P("tp"), P("tp"), P("tp"), P(None, "tp"), P("tp"), P(None, "tp"), P("tp"))
    return jax.shard_map(
        local, mesh=mesh, in_specs=placed, out_specs=(wide, wide, wide), check_vma=False
    )
```
